128 devices in a mesh: section: 4 (over x), ctx: 32 (over y, z, core).
Axes of the slice: x: 4, y: 4, z: 4, core: 2. Of those that a mesh axis runs over, the one named last changes fastest.
Arguments:
- resid: bfloat16 [4, 4096, 6144], P('section', 'ctx'), may hold values from -6 to 6
- queries: bfloat16 [4, 4096, 6144], P('section', 'ctx'), may hold values from -6 to 6
- keys: bfloat16 [4, 4096, 6144], P('section', 'ctx'), may hold values from -6 to 6
- values: bfloat16 [4, 4096, 6144], P('section', 'ctx'), may hold values from -6 to 6
- log_decay: float32 [4, 4096, 48], P('section', 'ctx'), may hold values from -3 to 0
- attn_gain: float32 [4, 6144], P('section'), may hold values from 0.25 to 1.75
- moe_gain: float32 [4, 6144], P('section'), may hold values from 0.25 to 1.75
- experts: int32 [4, 4096, 2], P('section', 'ctx'), may hold values from 0 to 31, all different within a row; in each aligned block of 128 rows (0 to 127, 128 to 255, ..., all dimensions but the last counted through in order) at most 16 rows name the same one
- combine_weight: float32 [4, 4096, 2], P('section', 'ctx'), may hold values from 0.2 to 1
- w_up: bfloat16 [4, 6144, 20480], P('section', None, 'ctx'), may hold values from -0.078125 to 0.078125
- w_down: bfloat16 [4, 20480, 6144], P('section', 'ctx'), may hold values from -0.078125 to 0.078125
Outputs:
- received: bfloat16 [4, 4096, 6144], P('section', 'ctx')
The draws below stay inside these ranges and needn't reach their ends.
Inputs may be any that keep to these rules, and one draw needn't show every extreme that they name: In the rows of one device each expert is named at most 16 times, and the two experts of a token differ.
All inputs are finite; a program needn't handle non-finite values.
Results may differ from the reference program's by a relative error of at most 0.002.
Values may be sent and summed in bfloat16 or wider, within the bound.
A program may use at most 256 MiB of HBM per device.

```python
import math
import jax
import jax.numpy as jnp
import numpy as np
from jax import lax

D = 6144
LINEAR_HEADS = 48
HEAD = 128
EXPERTS = 32
FF = 5120
SHARDS = 8
CAP_SRC = 16
TOK_DEV = 128
SECTION_TOKENS = 4096
RELAY_SECTIONS = 4
EXP_FLY = 4
FF_DEV = 640


def draw_log_decay(key, part):
    random_parts_key = jax.random.split(key, 7)
    fraction = 0.5
    quick_heads = jax.random.uniform(random_parts_key[0], (RELAY_SECTIONS, 1, LINEAR_HEADS)) < fraction
    slow_rate = jax.random.uniform(random_parts_key[1], (RELAY_SECTIONS, 1, LINEAR_HEADS), minval=0.2, maxval=0.6) / SECTION_TOKENS
    fast_rate = jax.random.uniform(random_parts_key[2], (RELAY_SECTIONS, 1, LINEAR_HEADS), minval=2.5, maxval=4.2) / TOK_DEV
    baseline_rate = jnp.where(quick_heads, fast_rate, slow_rate)
    block_count = SECTION_TOKENS // TOK_DEV
    processor_rate = jax.random.uniform(random_parts_key[3], (RELAY_SECTIONS, block_count, 1, LINEAR_HEADS), minval=0.6, maxval=1.5)
    processor_rate = jnp.broadcast_to(processor_rate, (RELAY_SECTIONS, block_count, TOK_DEV, LINEAR_HEADS)).reshape(RELAY_SECTIONS, SECTION_TOKENS, LINEAR_HEADS)
    jaggedness = jax.random.uniform(random_parts_key[4], (RELAY_SECTIONS, SECTION_TOKENS, LINEAR_HEADS), minval=0.5, maxval=1.5)
    spike_positions = jax.random.randint(random_parts_key[5], (RELAY_SECTIONS, 1, 4), 0, SECTION_TOKENS)
    spike_struck = jnp.any(jnp.arange(SECTION_TOKENS)[None, :, None] == spike_positions, axis=2)[:, :, None]
    spike_penalty = jax.random.uniform(random_parts_key[6], (RELAY_SECTIONS, SECTION_TOKENS, LINEAR_HEADS), minval=0.2, maxval=0.4)
    final_result = -baseline_rate * processor_rate * jaggedness + jnp.where(spike_struck, jnp.log1p(-spike_penalty), 0.0)
    return final_result.astype(jnp.float32)


def block_levels(rng, dims, cuts, smallest, high):
    def one(axis_at, blocks):
        heights = jax.random.uniform(jax.random.fold_in(jax.random.fold_in(rng, 6), axis_at), (blocks,), jnp.float32, smallest / len(cuts), high / len(cuts))
        return jnp.repeat(jnp.exp(heights), dims[axis_at] // blocks).reshape((-1,) + (1,) * (len(dims) - axis_at - 1))

    loudness = one(*cuts[0])
    for cut in cuts[1:]:
        loudness = loudness * one(*cut)
    return loudness


def assign_block(rng, own, number, rows, count, top, reach, skew):
    order = jax.random.permutation(rng, count)
    crowded, usual = portions_of(count, rows * top, reach, skew, True), portions_of(count, rows * top, reach, skew, False)
    places = jnp.arange(count)

    def named(tallies, offset_by):
        used = int((tallies > 0).sum())
        fixed = max(1, used // 4)
        shifted = fixed + (places - fixed + offset_by * (used - fixed)) % max(1, count - fixed)
        return jnp.zeros((count,), jnp.int32).at[order[jnp.where(places < fixed, places, shifted)]].set(jnp.asarray(tallies, jnp.int32))

    tallies = jnp.where(number % 4 == 0, named(crowded, number // 4), named(usual, number - number // 4 - 1))
    mixed = jax.random.permutation(jax.random.fold_in(own, 3), count)
    source_of, taker = mixed[0:count // 2 * 2:2], mixed[1:count // 2 * 2:2]
    slack = jnp.minimum(tallies[source_of] - 1, reach - tallies[taker]) // 2
    slack = jnp.where((source_of == order[0]) | (taker == order[0]) | (tallies[taker] == 0), 0, jnp.maximum(slack, 0))
    shifted = jax.random.randint(jax.random.fold_in(own, 4), (count // 2,), 0, 1 << 20) % (slack + 1)
    tallies = tallies.at[source_of].add(-shifted).at[taker].add(shifted)
    items = jnp.searchsorted(jnp.cumsum(tallies), jnp.arange(rows * top), side="right").astype(jnp.int32)
    table = items.reshape(top, rows).T
    table = table[jax.random.permutation(jax.random.fold_in(own, 1), rows)]
    offset_by = jax.random.randint(jax.random.fold_in(own, 2), (rows, 1), 0, top)
    return jnp.take_along_axis(table, (jnp.arange(top)[None, :] + offset_by) % top, axis=1)


def portions_of(count, total, most, skew, full):
    loads = [(1 << 20) // math.isqrt(rank ** skew) + 1 for rank in range(1, count + 1)]
    largest = most if full else min(most, max(-(-total // count), total * loads[0] // sum(loads)))
    least = 1 if total - largest >= count - 1 else 0
    holding, rest = [largest] + [least] * (count - 1), total - largest - least * (count - 1)
    while rest > 0:
        movable = [i for i in range(1, count) if holding[i] < largest] or [i for i in range(1, count) if holding[i] < most]
        mass, remaining = sum([loads[i] for i in movable]), rest
        for i in movable:
            more = min(most - holding[i], max(1, remaining * loads[i] // mass), rest)
            holding[i] = holding[i] + more
            rest = rest - more
    return np.array(holding)


def bell_draw(stream_key, shape, scale, bound, shards=(), held_as=jnp.bfloat16):
    result = scale * jax.random.normal(stream_key, shape, jnp.float32)
    if shards:
        result = result * block_levels(stream_key, shape, shards, -0.22, 0.18)
    return jnp.clip(result, -bound, bound).astype(held_as)


def setup_inputs(seed: int = 0) -> dict:
    key_of = jax.random.split(jax.random.key(seed), 12)
    resid = bell_draw(key_of[0], (RELAY_SECTIONS, SECTION_TOKENS, D), 1.0, 6.0, ((0, 4), (1, 32)))
    queries = bell_draw(key_of[1], (RELAY_SECTIONS, SECTION_TOKENS, D), 1.0, 6.0, ((0, 4), (1, 32)))
    keys = bell_draw(key_of[2], (RELAY_SECTIONS, SECTION_TOKENS, D), 1.0, 6.0, ((0, 4), (1, 32)))
    values = bell_draw(key_of[3], (RELAY_SECTIONS, SECTION_TOKENS, D), 1.0, 6.0, ((0, 4), (1, 32)))
    log_decay = draw_log_decay(jax.random.fold_in(key_of[11], 71), 0)
    attn_gain = jnp.clip(1.0 + 0.15 * jax.random.normal(key_of[5], (RELAY_SECTIONS, D), jnp.float32), 0.25, 1.75)
    moe_gain = jnp.clip(1.0 + 0.15 * jax.random.normal(key_of[6], (RELAY_SECTIONS, D), jnp.float32), 0.25, 1.75)
    experts_keys = jax.random.split(jax.random.fold_in(key_of[7], 1), RELAY_SECTIONS * SECTION_TOKENS // TOK_DEV)
    experts_turns = jax.random.permutation(jax.random.fold_in(key_of[7], 3), RELAY_SECTIONS * SECTION_TOKENS // TOK_DEV)
    experts = jax.vmap(lambda own, number: assign_block(jax.random.fold_in(key_of[7], 2), own, number, TOK_DEV, EXPERTS, 2, CAP_SRC, 2))(experts_keys, experts_turns).reshape((RELAY_SECTIONS, SECTION_TOKENS, 2))
    combine_weight = jnp.clip(0.2 + 0.8 * jax.random.uniform(key_of[8], (RELAY_SECTIONS, SECTION_TOKENS, 2), jnp.float32) ** block_levels(key_of[8], (RELAY_SECTIONS, SECTION_TOKENS, 2), ((0, 4), (1, 32)), -0.2, 0.2), 0.2, 1.0)
    w_up = bell_draw(key_of[9], (RELAY_SECTIONS, D, EXP_FLY * FF), D ** -0.5, 0.078125, ((0, 4), (2, 32)))
    w_down = bell_draw(key_of[10], (RELAY_SECTIONS, EXP_FLY * FF, D), FF ** -0.5, 0.078125, ((0, 4), (1, 32)))
    return dict(resid=resid, queries=queries, keys=keys, values=values, log_decay=log_decay, attn_gain=attn_gain, moe_gain=moe_gain, experts=experts, combine_weight=combine_weight, w_up=w_up, w_down=w_down)


HIGH = lax.Precision.HIGHEST

def block_attention(query, keyrows, valrows, log_rate):
    cumul = jnp.cumsum(log_rate, axis=0)
    scores = jnp.einsum('thd,shd->hts', query, keyrows, precision=HIGH)
    spread = cumul.T[:, :, None] - cumul.T[:, None, :]
    length = log_rate.shape[0]
    lower = jnp.arange(length)[:, None] >= jnp.arange(length)[None, :]
    weights = jnp.exp(jnp.where(lower[None], spread, -1e+30))
    intra = jnp.einsum('hts,shd->thd', scores * weights, valrows, precision=HIGH)
    tail_decay = jnp.exp(cumul[-1][None, :] - cumul)
    state = jnp.einsum('thd,the->hde', keyrows * tail_decay[:, :, None], valrows, precision=HIGH)
    return (intra, cumul, jnp.exp(cumul[-1]), state)

def attention_section(queries, keys, values, log_decay):
    blocks = SECTION_TOKENS // TOK_DEV
    qrows = queries.astype(jnp.float32).reshape(blocks, TOK_DEV, LINEAR_HEADS, HEAD)
    krows = keys.astype(jnp.float32).reshape(blocks, TOK_DEV, LINEAR_HEADS, HEAD)
    vrows = values.astype(jnp.float32).reshape(blocks, TOK_DEV, LINEAR_HEADS, HEAD)
    lrows = log_decay.reshape(blocks, TOK_DEV, LINEAR_HEADS)

    def advance(carry, inputs):
        query, keyrows, valrows, log_rate = inputs
        intra, cumul, decay, state = block_attention(query, keyrows, valrows, log_rate)
        inter = jnp.exp(cumul)[:, :, None] * jnp.einsum('thd,hde->the', query, carry, precision=HIGH)
        carry = decay[:, None, None] * carry + state
        return (carry, (intra + inter).reshape(TOK_DEV, D))
    start_state = jnp.zeros((LINEAR_HEADS, HEAD, HEAD), jnp.float32)
    _, outputs = lax.scan(advance, start_state, (qrows, krows, vrows, lrows))
    return outputs.reshape(SECTION_TOKENS, D)

def rms_scale(values_in, gain):
    return values_in * lax.rsqrt(lax.optimization_barrier(jnp.mean(values_in * values_in, axis=-1, keepdims=True)) + 1e-06) * gain

def slots_of(chosen):
    onehot = (chosen[:, None] == jnp.arange(EXPERTS)[None, :]).astype(jnp.int32)
    before = jnp.cumsum(onehot, axis=0) - onehot
    return lax.optimization_barrier(jnp.sum(before * onehot, axis=1)).astype(jnp.int32)

def moe_section(normed, experts, combine_weight, w_up, w_down):
    blocks = SECTION_TOKENS // TOK_DEV
    chosen = experts.reshape(blocks, 2 * TOK_DEV)
    slot = jax.vmap(slots_of)(chosen)
    source = jnp.arange(blocks, dtype=jnp.int32)[:, None]
    token_of = (source * TOK_DEV + jnp.arange(2 * TOK_DEV, dtype=jnp.int32)[None, :] // 2).reshape(-1)
    total_rows = blocks * CAP_SRC
    gathered = jnp.zeros((2 * SECTION_TOKENS, D), jnp.float32)
    for expert_id in range(EXP_FLY):
        taken = (chosen == expert_id).reshape(-1)
        target = jnp.where(taken, (source * CAP_SRC + slot).reshape(-1), total_rows).astype(jnp.int32)
        rows = jnp.zeros((total_rows, D), jnp.bfloat16).at[target].set(normed[token_of], mode='drop')
        summed = jnp.zeros((total_rows, D), jnp.float32)
        for shard in range(SHARDS):
            first = expert_id * FF + shard * FF_DEV
            hidden = jax.nn.gelu(jnp.dot(rows, w_up[:, first:first + FF_DEV], preferred_element_type=jnp.float32), approximate=True).astype(jnp.bfloat16)
            part = jnp.dot(hidden, w_down[first:first + FF_DEV, :], preferred_element_type=jnp.float32).astype(jnp.bfloat16)
            summed = summed + part.astype(jnp.float32)
        picked = jnp.take(summed, jnp.clip(target, 0, total_rows - 1), axis=0)
        gathered = gathered + jnp.where(taken[:, None], picked, 0.0)
    weighted = gathered * combine_weight.reshape(-1)[:, None]
    return weighted.reshape(SECTION_TOKENS, 2, D).sum(axis=1)

def reference(resid, queries, keys, values, log_decay, attn_gain, moe_gain, experts, combine_weight, w_up, w_down):
    outputs = []
    for section_id in range(RELAY_SECTIONS):
        attn_raw = attention_section(queries[section_id], keys[section_id], values[section_id], log_decay[section_id])
        hres = resid[section_id].astype(jnp.float32) + rms_scale(attn_raw, attn_gain[section_id])
        normed = rms_scale(hres, moe_gain[section_id]).astype(jnp.bfloat16)
        mixed = moe_section(normed, experts[section_id], combine_weight[section_id], w_up[section_id], w_down[section_id])
        outputs.append((hres + mixed).astype(jnp.bfloat16))
    layer_out = jnp.stack(outputs)
    return jnp.roll(layer_out, 1, axis=0)
```

```python
import jax
import jax.numpy as jnp
from jax import lax
from jax.experimental import pallas as pl
from jax.experimental.pallas import tpu as pltpu
from jax.sharding import PartitionSpec as P

D = 6144
HEADS = 48
HEAD = 128
TOK = 128
EXPERTS = 32
SHARDS = 8
CAP = 16
FLY = 4
GROUP = 6
ROWS = GROUP * HEAD
MESSAGE = ROWS + 8
BF = jnp.bfloat16
F32 = jnp.float32
HIGH = lax.Precision.HIGHEST


def dot(a, b):
    return jnp.dot(a, b, preferred_element_type=F32)


def dot_t(a, b):
    return lax.dot_general(a, b, (((1,), (1,)), ((), ())), preferred_element_type=F32)


def parts(x):
    high = x.astype(BF)
    return high, (x - high.astype(F32)).astype(BF)


def place():
    me = lax.axis_index("ctx")
    return me // 8, lax.rem(me // 2, 4), lax.rem(me, 2)


def index_of(y, z, c):
    return (y * 4 + z) * 2 + c


def columns(h):
    return pl.ds(pl.multiple_of(h * HEAD, HEAD), HEAD)


def attention_kernel(
    q_hbm, k_hbm, v_hbm, resid_hbm, rate_ref, attn_gain_ref, moe_gain_ref, select_ref,
    hres_ref, outbox_ref,
    q_ref, k_ref, v_ref, resid_ref, cum_ref, total_ref, partner_total, own_state,
    partner_state, t_send, t_recv, within, r_send, r_recv, p_send, chip_prefix,
    f_send, prefix, attn_ref, square_ref,
    load_sems, small_sems, ps_send_sems, ps_recv_sems, t_send_sems, t_recv_sems,
    r_send_sems, r_recv_sems, p_send_sems, p_recv_sems, f_send_sems, f_recv_sems,
):
    y, z, c = place()
    loads = [
        pltpu.make_async_copy(a, b, load_sems.at[i])
        for i, (a, b) in enumerate(
            ((k_hbm, k_ref), (v_hbm, v_ref), (q_hbm, q_ref), (resid_hbm, resid_ref))
        )
    ]
    for load in loads:
        load.start()
    barrier = pltpu.get_barrier_semaphore()
    partner = index_of(y, z, 1 - c)
    z_peer = [index_of(y, lax.rem(z + d, 4), c) for d in range(4)]
    y_peer = [index_of(lax.rem(y + d, 4), z, c) for d in range(4)]
    for peer in [partner] + z_peer[1:] + y_peer[1:]:
        pl.semaphore_signal(barrier, inc=1, device_id={"ctx": peer})

    rate = rate_ref[...]
    earlier = lax.broadcasted_iota(jnp.int32, (TOK, TOK), 0)
    later = lax.broadcasted_iota(jnp.int32, (TOK, TOK), 1)
    cum_ref[...] = jnp.dot(
        rate, (earlier <= later).astype(F32), precision=HIGH, preferred_element_type=F32
    )
    total_ref[...] = jnp.dot(
        rate, jnp.ones((TOK, TOK), F32), precision=HIGH, preferred_element_type=F32
    )
    pl.semaphore_wait(barrier, 7)

    def remote(src, dst, send, recv, peer):
        copy = pltpu.make_async_remote_copy(
            src_ref=src, dst_ref=dst, send_sem=send, recv_sem=recv, device_id={"ctx": peer}
        )
        return copy

    started = []
    totals = remote(total_ref, partner_total, small_sems.at[0], small_sems.at[1], partner)
    totals.start()
    loads[0].wait()
    loads[1].wait()

    def state_of(h):
        row = jnp.exp(total_ref[pl.ds(h, 1), :] - cum_ref[pl.ds(h, 1), :])
        keys = k_ref[:, columns(h)].astype(F32).T * row
        high, low = parts(keys)
        values = v_ref[:, columns(h)]
        return dot(high, values) + dot(low, values)

    order = (2, 1, 3, 0)
    ps_copies = {}
    for d in order:
        j = lax.rem(z + d, 4)

        def one(i, carry, j=j):
            h = (1 - c) * 24 + j * GROUP + i
            own_state[1 - c, j, pl.ds(pl.multiple_of(i * HEAD, HEAD), HEAD), :] = state_of(h)
            return carry

        lax.fori_loop(0, GROUP, one, 0)
        copy = remote(
            own_state.at[1 - c, j], partner_state.at[j], ps_send_sems.at[d], ps_recv_sems.at[d], partner
        )
        copy.start()
        ps_copies[d] = copy
    totals.wait()

    zero_first = c == 0
    t_copies = {}
    for d in order:
        j = lax.rem(z + d, 4)

        def one(i, carry, j=j):
            h = c * 24 + j * GROUP + i
            own_state[c, j, pl.ds(pl.multiple_of(i * HEAD, HEAD), HEAD), :] = state_of(h)
            return carry

        lax.fori_loop(0, GROUP, one, 0)
        ps_copies[d].wait_recv()
        target = t_recv.at[0] if d == 0 else t_send.at[d - 1]

        def join(i, carry, j=j, target=target):
            h = c * 24 + j * GROUP + i
            mine = total_ref[pl.ds(h, 1), :]
            other = partner_total[pl.ds(h, 1), :]
            keep = jnp.exp(jnp.where(zero_first, other, 0.0))
            take = jnp.exp(jnp.where(zero_first, 0.0, mine))
            rows = pl.ds(pl.multiple_of(i * HEAD, HEAD), HEAD)
            target[rows, :] = keep * own_state[c, j, rows, :] + take * partner_state[j, rows, :]
            target[pl.ds(ROWS + i, 1), :] = mine + other
            return carry

        lax.fori_loop(0, GROUP, join, 0)
        target[ROWS + GROUP :, :] = jnp.zeros((8 - GROUP, HEAD), F32)
        if d:
            copy = remote(
                target, t_recv.at[d], t_send_sems.at[d - 1], t_recv_sems.at[d - 1], z_peer[d]
            )
            copy.start()
            t_copies[d] = copy

    loads[2].wait()
    lower = earlier >= later

    def intra(h, carry):
        cum = cum_ref[pl.ds(h, 1), :]
        across = jnp.broadcast_to(cum, (TOK, TOK))
        weights = jnp.exp(jnp.where(lower, across.T - across, -1e30))
        scores = dot_t(q_ref[:, columns(h)], k_ref[:, columns(h)]) * weights
        high, low = parts(scores)
        values = v_ref[:, columns(h)]
        attn_ref[:, columns(h)] = dot(high, values) + dot(low, values)
        return carry

    lax.fori_loop(0, 18, intra, 0)

    for d in (1, 3, 2):
        t_copies[d].wait_recv()

    def row_sum(i, carry):
        rows = pl.ds(pl.multiple_of(i * HEAD, HEAD), HEAD)
        label = pl.ds(ROWS + i, 1)
        state = t_recv[z, rows, :]
        within[1, rows, :] = state
        for other in range(1, 4):
            slot = lax.rem(z - other + 4, 4)
            state = state * jnp.exp(t_recv[slot, label, :]) + t_recv[slot, rows, :]
            if other < 3:
                within[other + 1, rows, :] = state
        r_send[rows, :] = state
        r_send[label, :] = (
            t_recv[0, label, :] + t_recv[1, label, :] + t_recv[2, label, :] + t_recv[3, label, :]
        )
        return carry

    lax.fori_loop(0, GROUP, row_sum, 0)
    r_send[ROWS + GROUP :, :] = jnp.zeros((8 - GROUP, HEAD), F32)
    r_copies = {}
    for d in (2, 1, 3):
        copy = remote(r_send, r_recv.at[d], r_send_sems.at[d - 1], r_recv_sems.at[d - 1], y_peer[d])
        copy.start()
        r_copies[d] = copy
    lax.fori_loop(18, 34, intra, 0)
    r_recv[0] = r_send[...]
    for d in (1, 3, 2):
        r_copies[d].wait_recv()

    def row_prefix(i, carry):
        rows = pl.ds(pl.multiple_of(i * HEAD, HEAD), HEAD)
        label = pl.ds(ROWS + i, 1)
        state = jnp.zeros((HEAD, HEAD), F32)
        for other in range(3):
            slot = lax.rem(y - other + 4, 4)
            joined = state * jnp.exp(r_recv[slot, label, :]) + r_recv[slot, rows, :]
            state = jnp.where(other < y, joined, state)
        within[0, rows, :] = state
        return carry

    lax.fori_loop(0, GROUP, row_prefix, 0)
    p_copies = {}
    for d in order:
        to = lax.rem(z + d, 4)
        target = chip_prefix.at[0] if d == 0 else p_send.at[d - 1]

        def chip(i, carry, to=to, target=target):
            rows = pl.ds(pl.multiple_of(i * HEAD, HEAD), HEAD)
            label = pl.ds(ROWS + i, 1)
            gone = jnp.zeros((1, HEAD), F32)
            for other in range(3):
                slot = lax.rem(z - other + 4, 4)
                gone = gone + jnp.where(other < to, t_recv[slot, label, :], 0.0)
            start = within[0, rows, :]
            target[rows, :] = start * jnp.exp(gone) + jnp.where(to > 0, within[jnp.maximum(to, 1), rows, :], 0.0)
            return carry

        lax.fori_loop(0, GROUP, chip, 0)
        if d:
            copy = remote(
                target, chip_prefix.at[d], p_send_sems.at[d - 1], p_recv_sems.at[d - 1], z_peer[d]
            )
            copy.start()
            p_copies[d] = copy
    lax.fori_loop(34, 48, intra, 0)

    f_copies = {}
    for d in (0, 1, 3, 2):
        if d:
            p_copies[d].wait_recv()
        j = lax.rem(z - d + 4, 4)

        def core(i, carry, d=d, j=j):
            h = c * 24 + j * GROUP + i
            rows = pl.ds(pl.multiple_of(i * HEAD, HEAD), HEAD)
            first_total = jnp.where(zero_first, total_ref[pl.ds(h, 1), :], partner_total[pl.ds(h, 1), :])
            first_state = jnp.where(zero_first, own_state[c, j, rows, :], partner_state[j, rows, :])
            base = chip_prefix[d, rows, :]
            full = base * jnp.exp(first_total) + first_state
            prefix[c, j, rows, :] = jnp.where(zero_first, base, full)
            f_send[j, rows, :] = jnp.where(zero_first, full, base)
            return carry

        lax.fori_loop(0, GROUP, core, 0)
        copy = remote(f_send.at[j], prefix.at[c, j], f_send_sems.at[d], f_recv_sems.at[d], partner)
        copy.start()
        f_copies[d] = copy

    square_ref[...] = jnp.zeros_like(square_ref)

    def inter(half, j):
        def one(i, carry):
            h = half * 24 + j * GROUP + i
            rows = pl.ds(pl.multiple_of(i * HEAD, HEAD), HEAD)
            across = jnp.broadcast_to(cum_ref[pl.ds(h, 1), :], (TOK, TOK)).T
            high, low = parts(prefix[half, j, rows, :])
            query = q_ref[:, columns(h)]
            out = attn_ref[:, columns(h)] + jnp.exp(across) * (dot(query, high) + dot(query, low))
            attn_ref[:, columns(h)] = out
            square_ref[...] += out * out
            return carry

        lax.fori_loop(0, GROUP, one, 0)

    for d in (0, 1, 3, 2):
        inter(c, lax.rem(z - d + 4, 4))
    for d in (0, 1, 3, 2):
        f_copies[d].wait_recv()
        inter(1 - c, lax.rem(z - d + 4, 4))
    loads[3].wait()
    scale = lax.rsqrt(jnp.sum(square_ref[...], axis=1, keepdims=True) * (1.0 / D) + 1e-6)
    scale = jnp.broadcast_to(scale, (TOK, HEAD))
    square_ref[...] = jnp.zeros_like(square_ref)

    def residual(h, carry):
        out = resid_ref[:, columns(h)].astype(F32) + attn_ref[:, columns(h)] * scale * attn_gain_ref[:, columns(h)]
        hres_ref[:, columns(h)] = out
        square_ref[...] += out * out
        return carry

    lax.fori_loop(0, HEADS, residual, 0)
    scale_2 = lax.rsqrt(jnp.sum(square_ref[...], axis=1, keepdims=True) * (1.0 / D) + 1e-6)
    scale_2 = jnp.broadcast_to(scale_2, (TOK, HEAD))
    select = select_ref[...]

    def norm(h, carry):
        normed = (hres_ref[:, columns(h)] * scale_2 * moe_gain_ref[:, columns(h)]).astype(BF)
        outbox_ref[:, columns(h)] = dot(select, normed).astype(BF)
        return carry

    lax.fori_loop(0, HEADS, norm, 0)
    for copies in (ps_copies, t_copies, r_copies, p_copies, f_copies):
        for copy in copies.values():
            copy.wait_send()


def attention(queries, keys, values, resid, rate, attn_gain, moe_gain, select):
    vmem = pl.BlockSpec(memory_space=pltpu.VMEM)
    hbm = pl.BlockSpec(memory_space=pl.ANY)
    dma = pltpu.SemaphoreType.DMA
    return pl.pallas_call(
        attention_kernel,
        out_shape=(
            jax.ShapeDtypeStruct((TOK, D), F32),
            jax.ShapeDtypeStruct((FLY * CAP, D), BF),
        ),
        in_specs=[hbm] * 4 + [vmem] * 4,
        out_specs=(vmem, vmem),
        scratch_shapes=[
            pltpu.VMEM((TOK, D), BF),
            pltpu.VMEM((TOK, D), BF),
            pltpu.VMEM((TOK, D), BF),
            pltpu.VMEM((TOK, D), BF),
            pltpu.VMEM((HEADS, TOK), F32),
            pltpu.VMEM((HEADS, TOK), F32),
            pltpu.VMEM((HEADS, TOK), F32),
            pltpu.VMEM((2, 4, ROWS, HEAD), F32),
            pltpu.VMEM((4, ROWS, HEAD), F32),
            pltpu.VMEM((3, MESSAGE, HEAD), F32),
            pltpu.VMEM((4, MESSAGE, HEAD), F32),
            pltpu.VMEM((4, ROWS, HEAD), F32),
            pltpu.VMEM((MESSAGE, HEAD), F32),
            pltpu.VMEM((4, MESSAGE, HEAD), F32),
            pltpu.VMEM((3, ROWS, HEAD), F32),
            pltpu.VMEM((4, ROWS, HEAD), F32),
            pltpu.VMEM((4, ROWS, HEAD), F32),
            pltpu.VMEM((2, 4, ROWS, HEAD), F32),
            pltpu.VMEM((TOK, D), F32),
            pltpu.VMEM((TOK, HEAD), F32),
            dma((4,)), dma((2,)), dma((4,)), dma((4,)), dma((3,)), dma((3,)),
            dma((3,)), dma((3,)), dma((3,)), dma((3,)), dma((4,)), dma((4,)),
        ],
        compiler_params=pltpu.CompilerParams(
            collective_id=0, has_side_effects=True, vmem_limit_bytes=56 * 2**20
        ),
        name="attention",
    )(queries, keys, values, resid, rate, attn_gain, moe_gain, select)


def slots_of(chosen):
    count = chosen.shape[0]
    onehot = (chosen[:, None] == jnp.arange(EXPERTS)[None, :]).astype(BF)
    before = (jnp.arange(count)[:, None] > jnp.arange(count)[None, :]).astype(BF)
    ahead = dot(before, onehot)
    return jnp.sum(ahead * onehot.astype(F32), axis=1).astype(jnp.int32)


def local(
    resid, queries, keys, values, log_decay, attn_gain, moe_gain, experts, combine_weight, w_up, w_down
):
    chosen = experts[0].reshape(-1)
    slot = slots_of(chosen)
    target = chosen * CAP + slot
    in_window = chosen < FLY
    select = ((target[None, :] == jnp.arange(FLY * CAP)[:, None]) & in_window[None, :]).astype(BF)
    select_tok = select.reshape(FLY * CAP, TOK, 2).sum(axis=2).astype(BF)
    hres, outbox = attention(
        queries[0], keys[0], values[0], resid[0], log_decay[0].T, attn_gain, moe_gain, select_tok
    )
    outbox = outbox.reshape(FLY, CAP, D)
    my_expert = lax.axis_index("ctx") // SHARDS
    mine = lax.dynamic_index_in_dim(
        lax.all_gather(outbox[None], "ctx", axis=0, tiled=True), my_expert, 1, False
    )
    count = mine.shape[0]
    hidden = jax.nn.gelu(dot(mine.reshape(count * CAP, D), w_up[0]), approximate=True).astype(BF)
    partial_value = dot(hidden, w_down[0]).astype(BF).reshape(count, CAP, D)
    returned = lax.all_to_all(partial_value, "ctx", split_axis=0, concat_axis=0, tiled=True)
    summed = returned.reshape(FLY, SHARDS, CAP, D).astype(F32).sum(axis=1)
    summed = summed.reshape(FLY * CAP, D)
    weighted = (select.astype(F32) * combine_weight[0].reshape(1, -1)).reshape(FLY * CAP, TOK, 2).sum(axis=2)
    mixed = lax.dot_general(weighted, summed, (((0,), (0,)), ((), ())), precision=HIGH, preferred_element_type=F32)
    layer_out = (hres + mixed).astype(BF)
    pairs = [(source, (source + 1) % 4) for source in range(4)]
    return lax.ppermute(layer_out[None], "section", pairs)


def solution(mesh):
    token = P("section", "ctx", None)
    return jax.shard_map(
        local,
        mesh=mesh,
        in_specs=(
            token, token, token, token, token,
            P("section", None), P("section", None),
            token, token,
            P("section", None, "ctx"), token,
        ),
        out_specs=token,
        check_vma=False,
    )
```

```python
import jax
import jax.numpy as jnp
from jax import lax
from jax.experimental import pallas as pl
from jax.experimental.pallas import tpu as pltpu
from jax.sharding import PartitionSpec as P

D = 6144
HEADS = 48
HEAD = 128
TOK = 128
EXPERTS = 32
SHARDS = 8
CAP = 16
FLY = 4
GROUP = 6
ROWS = GROUP * HEAD
MESSAGE = ROWS + 8
BF = jnp.bfloat16
F32 = jnp.float32
HIGH = lax.Precision.HIGHEST


def dot(a, b):
    return jnp.dot(a, b, preferred_element_type=F32)


def dot_t(a, b):
    return lax.dot_general(a, b, (((1,), (1,)), ((), ())), preferred_element_type=F32)


def parts(x):
    high = x.astype(BF)
    return high, (x - high.astype(F32)).astype(BF)


def place():
    me = lax.axis_index("ctx")
    return me // 8, lax.rem(me // 2, 4), lax.rem(me, 2)


def index_of(y, z, c):
    return (y * 4 + z) * 2 + c


def columns(h):
    return pl.ds(pl.multiple_of(h * HEAD, HEAD), HEAD)


def attention_kernel(
    q_hbm, k_hbm, v_hbm, resid_hbm, rate_ref, attn_gain_ref, moe_gain_ref, select_ref,
    high_ref, low_ref, outbox_ref,
    q_ref, k_ref, v_ref, resid_ref, cum_ref, total_ref, partner_total, own_state,
    partner_state, t_send, t_recv, within, r_send, r_recv, p_send, chip_prefix,
    f_send, prefix, attn_ref, square_ref,
    load_sems, small_sems, ps_send_sems, ps_recv_sems, t_send_sems, t_recv_sems,
    r_send_sems, r_recv_sems, p_send_sems, p_recv_sems, f_send_sems, f_recv_sems,
):
    y, z, c = place()
    loads = [
        pltpu.make_async_copy(a, b, load_sems.at[i])
        for i, (a, b) in enumerate(
            ((k_hbm, k_ref), (v_hbm, v_ref), (q_hbm, q_ref), (resid_hbm, resid_ref))
        )
    ]
    for load in loads:
        load.start()
    barrier = pltpu.get_barrier_semaphore()
    partner = index_of(y, z, 1 - c)
    z_peer = [index_of(y, lax.rem(z + d, 4), c) for d in range(4)]
    y_peer = [index_of(lax.rem(y + d, 4), z, c) for d in range(4)]
    for peer in [partner] + z_peer[1:] + y_peer[1:]:
        pl.semaphore_signal(barrier, inc=1, device_id={"ctx": peer})

    rate = rate_ref[...]
    earlier = lax.broadcasted_iota(jnp.int32, (TOK, TOK), 0)
    later = lax.broadcasted_iota(jnp.int32, (TOK, TOK), 1)
    cum_ref[...] = jnp.dot(
        rate, (earlier <= later).astype(F32), precision=HIGH, preferred_element_type=F32
    )
    total_ref[...] = jnp.dot(
        rate, jnp.ones((TOK, TOK), F32), precision=HIGH, preferred_element_type=F32
    )
    pl.semaphore_wait(barrier, 7)

    def remote(src, dst, send, recv, peer):
        copy = pltpu.make_async_remote_copy(
            src_ref=src, dst_ref=dst, send_sem=send, recv_sem=recv, device_id={"ctx": peer}
        )
        return copy

    started = []
    totals = remote(total_ref, partner_total, small_sems.at[0], small_sems.at[1], partner)
    totals.start()
    loads[0].wait()
    loads[1].wait()

    def state_of(h):
        row = jnp.exp(total_ref[pl.ds(h, 1), :] - cum_ref[pl.ds(h, 1), :])
        keys = k_ref[:, columns(h)].astype(F32).T * row
        high, low = parts(keys)
        values = v_ref[:, columns(h)]
        return dot(high, values) + dot(low, values)

    order = (2, 1, 3, 0)
    ps_copies = {}
    for d in order:
        j = lax.rem(z + d, 4)

        def one(i, carry, j=j):
            h = (1 - c) * 24 + j * GROUP + i
            own_state[1 - c, j, pl.ds(pl.multiple_of(i * HEAD, HEAD), HEAD), :] = state_of(h)
            return carry

        lax.fori_loop(0, GROUP, one, 0)
        copy = remote(
            own_state.at[1 - c, j], partner_state.at[j], ps_send_sems.at[d], ps_recv_sems.at[d], partner
        )
        copy.start()
        ps_copies[d] = copy
    totals.wait()

    zero_first = c == 0
    t_copies = {}
    for d in order:
        j = lax.rem(z + d, 4)

        def one(i, carry, j=j):
            h = c * 24 + j * GROUP + i
            own_state[c, j, pl.ds(pl.multiple_of(i * HEAD, HEAD), HEAD), :] = state_of(h)
            return carry

        lax.fori_loop(0, GROUP, one, 0)
        ps_copies[d].wait_recv()
        target = t_recv.at[0] if d == 0 else t_send.at[d - 1]

        def join(i, carry, j=j, target=target):
            h = c * 24 + j * GROUP + i
            mine = total_ref[pl.ds(h, 1), :]
            other = partner_total[pl.ds(h, 1), :]
            keep = jnp.exp(jnp.where(zero_first, other, 0.0))
            take = jnp.exp(jnp.where(zero_first, 0.0, mine))
            rows = pl.ds(pl.multiple_of(i * HEAD, HEAD), HEAD)
            target[rows, :] = keep * own_state[c, j, rows, :] + take * partner_state[j, rows, :]
            target[pl.ds(ROWS + i, 1), :] = mine + other
            return carry

        lax.fori_loop(0, GROUP, join, 0)
        target[ROWS + GROUP :, :] = jnp.zeros((8 - GROUP, HEAD), F32)
        if d:
            copy = remote(
                target, t_recv.at[d], t_send_sems.at[d - 1], t_recv_sems.at[d - 1], z_peer[d]
            )
            copy.start()
            t_copies[d] = copy

    loads[2].wait()
    lower = earlier >= later

    def intra(h, carry):
        cum = cum_ref[pl.ds(h, 1), :]
        across = jnp.broadcast_to(cum, (TOK, TOK))
        weights = jnp.exp(jnp.where(lower, across.T - across, -1e30))
        scores = dot_t(q_ref[:, columns(h)], k_ref[:, columns(h)]) * weights
        high, low = parts(scores)
        values = v_ref[:, columns(h)]
        attn_ref[:, columns(h)] = dot(high, values) + dot(low, values)
        return carry

    lax.fori_loop(0, 18, intra, 0)

    for d in (1, 3, 2):
        t_copies[d].wait_recv()

    def row_sum(i, carry):
        rows = pl.ds(pl.multiple_of(i * HEAD, HEAD), HEAD)
        label = pl.ds(ROWS + i, 1)
        state = t_recv[z, rows, :]
        within[1, rows, :] = state
        for other in range(1, 4):
            slot = lax.rem(z - other + 4, 4)
            state = state * jnp.exp(t_recv[slot, label, :]) + t_recv[slot, rows, :]
            if other < 3:
                within[other + 1, rows, :] = state
        r_send[rows, :] = state
        r_send[label, :] = (
            t_recv[0, label, :] + t_recv[1, label, :] + t_recv[2, label, :] + t_recv[3, label, :]
        )
        return carry

    lax.fori_loop(0, GROUP, row_sum, 0)
    r_send[ROWS + GROUP :, :] = jnp.zeros((8 - GROUP, HEAD), F32)
    r_copies = {}
    for d in (2, 1, 3):
        copy = remote(r_send, r_recv.at[d], r_send_sems.at[d - 1], r_recv_sems.at[d - 1], y_peer[d])
        copy.start()
        r_copies[d] = copy
    lax.fori_loop(18, 34, intra, 0)
    r_recv[0] = r_send[...]
    for d in (1, 3, 2):
        r_copies[d].wait_recv()

    def row_prefix(i, carry):
        rows = pl.ds(pl.multiple_of(i * HEAD, HEAD), HEAD)
        label = pl.ds(ROWS + i, 1)
        state = jnp.zeros((HEAD, HEAD), F32)
        for other in range(3):
            slot = lax.rem(y - other + 4, 4)
            joined = state * jnp.exp(r_recv[slot, label, :]) + r_recv[slot, rows, :]
            state = jnp.where(other < y, joined, state)
        within[0, rows, :] = state
        return carry

    lax.fori_loop(0, GROUP, row_prefix, 0)
    p_copies = {}
    for d in order:
        to = lax.rem(z + d, 4)
        target = chip_prefix.at[0] if d == 0 else p_send.at[d - 1]

        def chip(i, carry, to=to, target=target):
            rows = pl.ds(pl.multiple_of(i * HEAD, HEAD), HEAD)
            label = pl.ds(ROWS + i, 1)
            gone = jnp.zeros((1, HEAD), F32)
            for other in range(3):
                slot = lax.rem(z - other + 4, 4)
                gone = gone + jnp.where(other < to, t_recv[slot, label, :], 0.0)
            start = within[0, rows, :]
            target[rows, :] = start * jnp.exp(gone) + jnp.where(to > 0, within[jnp.maximum(to, 1), rows, :], 0.0)
            return carry

        lax.fori_loop(0, GROUP, chip, 0)
        if d:
            copy = remote(
                target, chip_prefix.at[d], p_send_sems.at[d - 1], p_recv_sems.at[d - 1], z_peer[d]
            )
            copy.start()
            p_copies[d] = copy
    lax.fori_loop(34, 48, intra, 0)

    f_copies = {}
    for d in (0, 1, 3, 2):
        if d:
            p_copies[d].wait_recv()
        j = lax.rem(z - d + 4, 4)

        def core(i, carry, d=d, j=j):
            h = c * 24 + j * GROUP + i
            rows = pl.ds(pl.multiple_of(i * HEAD, HEAD), HEAD)
            first_total = jnp.where(zero_first, total_ref[pl.ds(h, 1), :], partner_total[pl.ds(h, 1), :])
            first_state = jnp.where(zero_first, own_state[c, j, rows, :], partner_state[j, rows, :])
            base = chip_prefix[d, rows, :]
            full = base * jnp.exp(first_total) + first_state
            prefix[c, j, rows, :] = jnp.where(zero_first, base, full)
            f_send[j, rows, :] = jnp.where(zero_first, full, base)
            return carry

        lax.fori_loop(0, GROUP, core, 0)
        copy = remote(f_send.at[j], prefix.at[c, j], f_send_sems.at[d], f_recv_sems.at[d], partner)
        copy.start()
        f_copies[d] = copy

    square_ref[...] = jnp.zeros_like(square_ref)

    def inter(half, j):
        def one(i, carry):
            h = half * 24 + j * GROUP + i
            rows = pl.ds(pl.multiple_of(i * HEAD, HEAD), HEAD)
            across = jnp.broadcast_to(cum_ref[pl.ds(h, 1), :], (TOK, TOK)).T
            high, low = parts(prefix[half, j, rows, :])
            query = q_ref[:, columns(h)]
            out = attn_ref[:, columns(h)] + jnp.exp(across) * (dot(query, high) + dot(query, low))
            attn_ref[:, columns(h)] = out
            square_ref[...] += out * out
            return carry

        lax.fori_loop(0, GROUP, one, 0)

    for d in (0, 1, 3, 2):
        inter(c, lax.rem(z - d + 4, 4))
    for d in (0, 1, 3, 2):
        f_copies[d].wait_recv()
        inter(1 - c, lax.rem(z - d + 4, 4))
    loads[3].wait()
    scale = lax.rsqrt(jnp.sum(square_ref[...], axis=1, keepdims=True) * (1.0 / D) + 1e-6)
    scale = jnp.broadcast_to(scale, (TOK, HEAD))
    square_ref[...] = jnp.zeros_like(square_ref)

    def residual(h, carry):
        out = resid_ref[:, columns(h)].astype(F32) + attn_ref[:, columns(h)] * scale * attn_gain_ref[:, columns(h)]
        attn_ref[:, columns(h)] = out
        square_ref[...] += out * out
        return carry

    lax.fori_loop(0, HEADS, residual, 0)
    scale_2 = lax.rsqrt(jnp.sum(square_ref[...], axis=1, keepdims=True) * (1.0 / D) + 1e-6)
    scale_2 = jnp.broadcast_to(scale_2, (TOK, HEAD))
    select = select_ref[...]

    def norm(h, carry):
        out = attn_ref[:, columns(h)]
        high, low = parts(out)
        high_ref[:, columns(h)] = high
        low_ref[:, columns(h)] = dot(select, low).astype(BF)
        normed = (out * scale_2 * moe_gain_ref[:, columns(h)]).astype(BF)
        outbox_ref[:, columns(h)] = dot(select, normed).astype(BF)
        return carry

    lax.fori_loop(0, HEADS, norm, 0)
    for copies in (ps_copies, t_copies, r_copies, p_copies, f_copies):
        for copy in copies.values():
            copy.wait_send()


def attention(queries, keys, values, resid, rate, attn_gain, moe_gain, select):
    vmem = pl.BlockSpec(memory_space=pltpu.VMEM)
    hbm = pl.BlockSpec(memory_space=pl.ANY)
    dma = pltpu.SemaphoreType.DMA
    return pl.pallas_call(
        attention_kernel,
        out_shape=(
            jax.ShapeDtypeStruct((TOK, D), BF),
            jax.ShapeDtypeStruct((FLY * CAP, D), BF),
            jax.ShapeDtypeStruct((FLY * CAP, D), BF),
        ),
        in_specs=[hbm] * 4 + [vmem] * 4,
        out_specs=(vmem, vmem, vmem),
        scratch_shapes=[
            pltpu.VMEM((TOK, D), BF),
            pltpu.VMEM((TOK, D), BF),
            pltpu.VMEM((TOK, D), BF),
            pltpu.VMEM((TOK, D), BF),
            pltpu.VMEM((HEADS, TOK), F32),
            pltpu.VMEM((HEADS, TOK), F32),
            pltpu.VMEM((HEADS, TOK), F32),
            pltpu.VMEM((2, 4, ROWS, HEAD), F32),
            pltpu.VMEM((4, ROWS, HEAD), F32),
            pltpu.VMEM((3, MESSAGE, HEAD), F32),
            pltpu.VMEM((4, MESSAGE, HEAD), F32),
            pltpu.VMEM((4, ROWS, HEAD), F32),
            pltpu.VMEM((MESSAGE, HEAD), F32),
            pltpu.VMEM((4, MESSAGE, HEAD), F32),
            pltpu.VMEM((3, ROWS, HEAD), F32),
            pltpu.VMEM((4, ROWS, HEAD), F32),
            pltpu.VMEM((4, ROWS, HEAD), F32),
            pltpu.VMEM((2, 4, ROWS, HEAD), F32),
            pltpu.VMEM((TOK, D), F32),
            pltpu.VMEM((TOK, HEAD), F32),
            dma((4,)), dma((2,)), dma((4,)), dma((4,)), dma((3,)), dma((3,)),
            dma((3,)), dma((3,)), dma((3,)), dma((3,)), dma((4,)), dma((4,)),
        ],
        compiler_params=pltpu.CompilerParams(
            collective_id=0, has_side_effects=True, vmem_limit_bytes=56 * 2**20
        ),
        name="attention",
    )(queries, keys, values, resid, rate, attn_gain, moe_gain, select)


BLOCK = 4 * CAP
HALF = 2 * CAP
STEP = 512
UNITS = 640


def window_kernel(
    outbox_ref, high_ref, low_ref, mixing_ref, up_hbm, down_hbm,
    out_ref,
    up_ref, down_ref, rows_ref, part_ref, partner_part, total_ref, relay_in, relay_out,
    near_in, far_in, final_ref, sums_ref, high_in, low_in, mixing_in,
    load_sems, y_send, y_recv, core_send, core_recv, z_send, z_recv, hop_send, hop_recv,
    part_send, part_recv, ring_send, ring_recv, next_send, next_recv,
):
    y, z, c = place()
    section = lax.axis_index("section")
    after = lax.rem(section + 1, 4)
    before = lax.rem(section + 3, 4)
    loads = [
        pltpu.make_async_copy(up_hbm, up_ref, load_sems.at[0]),
        pltpu.make_async_copy(down_hbm, down_ref, load_sems.at[1]),
    ]
    for load in loads:
        load.start()
    z_plus, z_minus, z_far = lax.rem(z + 1, 4), lax.rem(z + 3, 4), lax.rem(z + 2, 4)
    partner = index_of(y, z, 1 - c)
    plus, minus = index_of(y, z_plus, c), index_of(y, z_minus, c)
    y_peer = [index_of(lax.rem(y + d, 4), z, c) for d in range(4)]
    barrier = pltpu.get_barrier_semaphore()
    for peer in [partner, plus, minus] + y_peer[1:]:
        pl.semaphore_signal(barrier, inc=1, device_id={"ctx": peer})
    for other in (after, before):
        for peer in y_peer:
            pl.semaphore_signal(barrier, inc=1, device_id={"section": other, "ctx": peer})
    pl.semaphore_wait(barrier, 14)

    sent = []

    def send(src, dst, send_sem, recv_sem, peer, section_to=None):
        target = {"ctx": peer} if section_to is None else {"section": section_to, "ctx": peer}
        copy = pltpu.make_async_remote_copy(
            src_ref=src, dst_ref=dst, send_sem=send_sem, recv_sem=recv_sem, device_id=target
        )
        copy.start()
        sent.append(copy)

    def arrived(dst, recv_sem, peer, section_to=None):
        target = {"ctx": peer} if section_to is None else {"section": section_to, "ctx": peer}
        pltpu.make_async_remote_copy(
            src_ref=dst, dst_ref=dst, send_sem=recv_sem, recv_sem=recv_sem, device_id=target
        ).wait_recv()

    spot = (0, 2, 1, 3)

    def piece(block, core, p):
        return rows_ref.at[block, pl.ds(pl.multiple_of(core * BLOCK + p * CAP, CAP), CAP), :]

    def box(e):
        return outbox_ref.at[pl.ds(pl.multiple_of(e * CAP, CAP), CAP), :]

    for d in (2, 1, 3):
        send(
            box(lax.rem(y + d, 4)), piece(z, c, spot[d]), y_send.at[d - 1], y_recv.at[d - 1], y_peer[d]
        )
    rows_ref[z, pl.ds(pl.multiple_of(c * BLOCK, CAP), CAP), :] = outbox_ref[
        pl.ds(pl.multiple_of(y * CAP, CAP), CAP), :
    ]

    def spread(p):
        src = piece(z, c, p)
        send(src, src, z_send.at[0, p], z_recv.at[0, p], plus)
        send(src, src, z_send.at[1, p], z_recv.at[1, p], minus)
        send(src, src, core_send.at[0, p], core_recv.at[0, p], partner)

    def from_minus(p):
        src = piece(z_minus, c, p)
        arrived(src, z_recv.at[0, p], minus)
        if p < 2:
            send(src, src, hop_send.at[p], hop_recv.at[p], plus)
        send(src, src, core_send.at[1, p], core_recv.at[1, p], partner)

    def from_plus(p):
        src = piece(z_plus, c, p)
        arrived(src, z_recv.at[1, p], plus)
        if p >= 2:
            send(src, src, hop_send.at[p], hop_recv.at[p], minus)
        send(src, src, core_send.at[2, p], core_recv.at[2, p], partner)

    def from_far(p):
        src = piece(z_far, c, p)
        arrived(src, hop_recv.at[p], minus if p < 2 else plus)
        send(src, src, core_send.at[3, p], core_recv.at[3, p], partner)

    spread(0)
    send(high_ref, high_in, next_send.at[0], next_recv.at[0], y_peer[0], after)
    send(low_ref, low_in, next_send.at[1], next_recv.at[1], y_peer[0], after)
    send(mixing_ref, mixing_in, next_send.at[2], next_recv.at[2], y_peer[0], after)
    for d in (1, 3, 2):
        arrived(piece(z, c, spot[d]), y_recv.at[d - 1], y_peer[4 - d])
        spread(spot[d])

    blocks = (z, z_minus, z_plus, z_far)
    for load in loads:
        load.wait()

    def compute(k):
        block = blocks[k]
        for p in range(4):
            arrived(piece(block, 1 - c, p), core_recv.at[k, p], partner)
        total_ref[...] = jnp.zeros_like(total_ref)

        def up(i, carry):
            at = pl.ds(pl.multiple_of(i * STEP, STEP), STEP)
            total_ref[...] += dot(rows_ref[block, :, at], up_ref[at, :])
            return carry

        lax.fori_loop(0, D // STEP, up, 0)
        hidden = jax.nn.gelu(total_ref[...], approximate=True).astype(BF)

        def down(i, carry):
            at = pl.ds(pl.multiple_of(i * STEP, STEP), STEP)
            part_ref[block, :, at] = dot(hidden, down_ref[:, at]).astype(BF)
            return carry

        lax.fori_loop(0, D // STEP, down, 0)
        other = part_ref.at[block, pl.ds(pl.multiple_of((1 - c) * BLOCK, BLOCK), BLOCK), :]
        send(other, partner_part.at[k], part_send.at[k], part_recv.at[k], partner)

    def own(k, half=None):
        if half is None:
            return part_ref.at[blocks[k], pl.ds(pl.multiple_of(c * BLOCK, BLOCK), BLOCK), :]
        return part_ref.at[blocks[k], pl.ds(pl.multiple_of(c * BLOCK + half * HALF, HALF), HALF), :]

    def over_columns(body):
        def one(i, carry):
            body(pl.ds(pl.multiple_of(i * STEP, STEP), STEP))
            return carry

        lax.fori_loop(0, D // STEP, one, 0)

    def core_sum(k):
        arrived(partner_part.at[k], part_recv.at[k], partner)
        mine = own(k)

        def add(at):
            mine[:, at] = (mine[:, at].astype(F32) + partner_part[k, :, at].astype(F32)).astype(BF)

        over_columns(add)

    compute(0)
    for p in (0, 1, 2, 3):
        from_minus(p)
        from_plus(p)
    compute(1)
    compute(2)
    for p in (0, 2, 1, 3):
        from_far(p)
    core_sum(1)
    send(own(1, 0), near_in.at[1], ring_send.at[1], ring_recv.at[1], minus)
    core_sum(2)
    send(own(2, 1), near_in.at[0], ring_send.at[0], ring_recv.at[0], plus)
    compute(3)
    core_sum(0)
    core_sum(3)
    send(own(3, 0), relay_in.at[0], ring_send.at[2], ring_recv.at[2], plus)
    send(own(3, 1), relay_in.at[1], ring_send.at[3], ring_recv.at[3], minus)

    def relay(side):
        peer = (minus, plus)[side]
        arrived(relay_in.at[side], ring_recv.at[2 + side], peer)
        mine = own(2 - side, side)

        def add(at):
            relay_out[side, :, at] = (
                mine[:, at].astype(F32) + relay_in[side, :, at].astype(F32)
            ).astype(BF)

        over_columns(add)
        send(
            relay_out.at[side], far_in.at[side], ring_send.at[4 + side], ring_recv.at[4 + side],
            (plus, minus)[side],
        )

    relay(0)
    relay(1)
    arrived(near_in.at[0], ring_recv.at[0], minus)
    arrived(near_in.at[1], ring_recv.at[1], plus)
    arrived(far_in.at[0], ring_recv.at[4], minus)
    arrived(far_in.at[1], ring_recv.at[5], plus)
    for half in range(2):
        mine = own(0, half)

        def add(at, half=half, mine=mine):
            final_ref[half * HALF : (half + 1) * HALF, at] = (
                mine[:, at].astype(F32)
                + near_in[1 - half, :, at].astype(F32)
                + far_in[half, :, at].astype(F32)
            ).astype(BF)

        over_columns(add)
        for d in ((0, 2), (1, 3))[half]:
            p = spot[d]
            send(
                final_ref.at[p * CAP : (p + 1) * CAP, :],
                sums_ref.at[pl.ds(pl.multiple_of(y * CAP, CAP), CAP), :],
                next_send.at[3 + d], next_recv.at[3 + d], y_peer[(4 - d) % 4], after,
            )
    arrived(high_in, next_recv.at[0], y_peer[0], before)
    arrived(low_in, next_recv.at[1], y_peer[0], before)
    arrived(mixing_in, next_recv.at[2], y_peer[0], before)
    for d in range(4):
        arrived(sums_ref.at[0:CAP, :], next_recv.at[3 + d], y_peer[d], before)
    first = mixing_in[:, :BLOCK].astype(BF)
    weight_high, weight_low = parts(mixing_in[:, BLOCK:])

    def mix(at):
        sums = sums_ref[:, at]
        mixed = dot(weight_high, sums) + dot(weight_low, sums)
        out_ref[:, at] = ((high_in[:, at].astype(F32) + dot(first, low_in[:, at])) + mixed).astype(BF)

    over_columns(mix)
    for copy in sent:
        copy.wait_send()


def window(outbox, high, low, mixing, w_up, w_down):
    vmem = pl.BlockSpec(memory_space=pltpu.VMEM)
    hbm = pl.BlockSpec(memory_space=pl.ANY)
    dma = pltpu.SemaphoreType.DMA
    return pl.pallas_call(
        window_kernel,
        out_shape=jax.ShapeDtypeStruct((TOK, D), BF),
        in_specs=[vmem] * 4 + [hbm] * 2,
        out_specs=vmem,
        scratch_shapes=[
            pltpu.VMEM((D, UNITS), BF),
            pltpu.VMEM((UNITS, D), BF),
            pltpu.VMEM((4, 2 * BLOCK, D), BF),
            pltpu.VMEM((4, 2 * BLOCK, D), BF),
            pltpu.VMEM((4, BLOCK, D), BF),
            pltpu.VMEM((2 * BLOCK, UNITS), F32),
            pltpu.VMEM((2, HALF, D), BF),
            pltpu.VMEM((2, HALF, D), BF),
            pltpu.VMEM((2, HALF, D), BF),
            pltpu.VMEM((2, HALF, D), BF),
            pltpu.VMEM((BLOCK, D), BF),
            pltpu.VMEM((BLOCK, D), BF),
            pltpu.VMEM((TOK, D), BF),
            pltpu.VMEM((BLOCK, D), BF),
            pltpu.VMEM((TOK, 2 * BLOCK), F32),
            dma((2,)), dma((3,)), dma((3,)), dma((4, 4)), dma((4, 4)), dma((2, 4)), dma((2, 4)),
            dma((4,)), dma((4,)), dma((4,)), dma((4,)), dma((6,)), dma((6,)), dma((7,)), dma((7,)),
        ],
        compiler_params=pltpu.CompilerParams(
            collective_id=1, has_side_effects=True, vmem_limit_bytes=60 * 2**20
        ),
        name="window",
    )(outbox, high, low, mixing, w_up, w_down)


def slots_of(chosen):
    count = chosen.shape[0]
    onehot = (chosen[:, None] == jnp.arange(EXPERTS)[None, :]).astype(BF)
    before = (jnp.arange(count)[:, None] > jnp.arange(count)[None, :]).astype(BF)
    ahead = dot(before, onehot)
    return jnp.sum(ahead * onehot.astype(F32), axis=1).astype(jnp.int32)


def local(
    resid, queries, keys, values, log_decay, attn_gain, moe_gain, experts, combine_weight, w_up, w_down
):
    chosen = experts[0].reshape(-1)
    slot = slots_of(chosen)
    target = chosen * CAP + slot
    in_window = chosen < FLY
    select = ((target[None, :] == jnp.arange(FLY * CAP)[:, None]) & in_window[None, :]).astype(BF)
    select_tok = select.reshape(FLY * CAP, TOK, 2).sum(axis=2).astype(BF)
    high, low, outbox = attention(
        queries[0], keys[0], values[0], resid[0], log_decay[0].T, attn_gain, moe_gain, select_tok
    )
    pairs = select.T.reshape(TOK, 2, FLY * CAP).astype(F32)
    inside = in_window.reshape(TOK, 2)
    first = jnp.where(inside[:, 0:1], pairs[:, 0], pairs[:, 1])
    weighted = (pairs * combine_weight[0][:, :, None]).sum(axis=1)
    mixing = jnp.concatenate([first, weighted], axis=1)
    return window(outbox, high, low, mixing, w_up[0], w_down[0])[None]


def solution(mesh):
    token = P("section", "ctx", None)
    return jax.shard_map(
        local,
        mesh=mesh,
        in_specs=(
            token, token, token, token, token,
            P("section", None), P("section", None),
            token, token,
            P("section", None, "ctx"), token,
        ),
        out_specs=token,
        check_vma=False,
    )
```

```python
import jax
import jax.numpy as jnp
from jax import lax
from jax.experimental import pallas as pl
from jax.experimental.pallas import tpu as pltpu
from jax.sharding import PartitionSpec as P

D = 6144
HEADS = 48
HEAD = 128
TOK = 128
EXPERTS = 32
SHARDS = 8
CAP = 16
FLY = 4
GROUP = 6
ROWS = GROUP * HEAD
MESSAGE = ROWS + 8
BF = jnp.bfloat16
F32 = jnp.float32
HIGH = lax.Precision.HIGHEST


def dot(a, b):
    return jnp.dot(a, b, preferred_element_type=F32)


def dot_t(a, b):
    return lax.dot_general(a, b, (((1,), (1,)), ((), ())), preferred_element_type=F32)


def parts(x):
    high = x.astype(BF)
    return high, (x - high.astype(F32)).astype(BF)


def place():
    me = lax.axis_index("ctx")
    return me // 8, lax.rem(me // 2, 4), lax.rem(me, 2)


def index_of(y, z, c):
    return (y * 4 + z) * 2 + c


def columns(h):
    return pl.ds(pl.multiple_of(h * HEAD, HEAD), HEAD)


def attention_kernel(
    q_hbm, k_hbm, v_hbm, resid_hbm, rate_ref, attn_gain_ref, moe_gain_ref, select_ref,
    high_ref, low_ref, outbox_ref,
    q_ref, k_ref, v_ref, resid_ref, cum_ref, total_ref, partner_total, own_state,
    partner_state, t_send, t_recv, within, r_send, r_recv, p_send, chip_prefix,
    f_send, prefix, attn_ref, square_ref,
    load_sems, small_sems, ps_send_sems, ps_recv_sems, t_send_sems, t_recv_sems,
    r_send_sems, r_recv_sems, p_send_sems, p_recv_sems, f_send_sems, f_recv_sems,
):
    y, z, c = place()
    loads = [
        pltpu.make_async_copy(a, b, load_sems.at[i])
        for i, (a, b) in enumerate(
            ((k_hbm, k_ref), (v_hbm, v_ref), (q_hbm, q_ref), (resid_hbm, resid_ref))
        )
    ]
    for load in loads:
        load.start()
    barrier = pltpu.get_barrier_semaphore()
    partner = index_of(y, z, 1 - c)
    z_peer = [index_of(y, lax.rem(z + d, 4), c) for d in range(4)]
    y_peer = [index_of(lax.rem(y + d, 4), z, c) for d in range(4)]
    for peer in [partner] + z_peer[1:] + y_peer[1:]:
        pl.semaphore_signal(barrier, inc=1, device_id={"ctx": peer})

    rate = rate_ref[...]
    earlier = lax.broadcasted_iota(jnp.int32, (TOK, TOK), 0)
    later = lax.broadcasted_iota(jnp.int32, (TOK, TOK), 1)
    cum_ref[...] = jnp.dot(
        rate, (earlier <= later).astype(F32), precision=HIGH, preferred_element_type=F32
    )
    total_ref[...] = jnp.dot(
        rate, jnp.ones((TOK, TOK), F32), precision=HIGH, preferred_element_type=F32
    )
    pl.semaphore_wait(barrier, 7)

    def remote(src, dst, send, recv, peer):
        copy = pltpu.make_async_remote_copy(
            src_ref=src, dst_ref=dst, send_sem=send, recv_sem=recv, device_id={"ctx": peer}
        )
        return copy

    started = []
    totals = remote(total_ref, partner_total, small_sems.at[0], small_sems.at[1], partner)
    totals.start()
    loads[0].wait()
    loads[1].wait()

    def state_of(h):
        row = jnp.exp(total_ref[pl.ds(h, 1), :] - cum_ref[pl.ds(h, 1), :])
        keys = k_ref[:, columns(h)].astype(F32).T * row
        high, low = parts(keys)
        values = v_ref[:, columns(h)]
        return dot(high, values) + dot(low, values)

    order = (2, 1, 3, 0)
    ps_copies = {}
    for d in order:
        j = lax.rem(z + d, 4)

        def one(i, carry, j=j):
            h = (1 - c) * 24 + j * GROUP + i
            own_state[1 - c, j, pl.ds(pl.multiple_of(i * HEAD, HEAD), HEAD), :] = state_of(h)
            return carry

        lax.fori_loop(0, GROUP, one, 0, unroll=6)
        copy = remote(
            own_state.at[1 - c, j], partner_state.at[j], ps_send_sems.at[d], ps_recv_sems.at[d], partner
        )
        copy.start()
        ps_copies[d] = copy
    totals.wait()

    zero_first = c == 0
    t_copies = {}
    for d in order:
        j = lax.rem(z + d, 4)

        def one(i, carry, j=j):
            h = c * 24 + j * GROUP + i
            own_state[c, j, pl.ds(pl.multiple_of(i * HEAD, HEAD), HEAD), :] = state_of(h)
            return carry

        lax.fori_loop(0, GROUP, one, 0, unroll=6)
        ps_copies[d].wait_recv()
        target = t_recv.at[0] if d == 0 else t_send.at[d - 1]

        def join(i, carry, j=j, target=target):
            h = c * 24 + j * GROUP + i
            mine = total_ref[pl.ds(h, 1), :]
            other = partner_total[pl.ds(h, 1), :]
            keep = jnp.exp(jnp.where(zero_first, other, 0.0))
            take = jnp.exp(jnp.where(zero_first, 0.0, mine))
            rows = pl.ds(pl.multiple_of(i * HEAD, HEAD), HEAD)
            target[rows, :] = keep * own_state[c, j, rows, :] + take * partner_state[j, rows, :]
            target[pl.ds(ROWS + i, 1), :] = mine + other
            return carry

        lax.fori_loop(0, GROUP, join, 0, unroll=2)
        target[ROWS + GROUP :, :] = jnp.zeros((8 - GROUP, HEAD), F32)
        if d:
            copy = remote(
                target, t_recv.at[d], t_send_sems.at[d - 1], t_recv_sems.at[d - 1], z_peer[d]
            )
            copy.start()
            t_copies[d] = copy

    loads[2].wait()
    lower = earlier >= later

    def intra(h, carry):
        cum = cum_ref[pl.ds(h, 1), :]
        across = jnp.broadcast_to(cum, (TOK, TOK))
        weights = jnp.exp(jnp.where(lower, across.T - across, -1e30))
        scores = dot_t(q_ref[:, columns(h)], k_ref[:, columns(h)]) * weights
        high, low = parts(scores)
        values = v_ref[:, columns(h)]
        attn_ref[:, columns(h)] = dot(high, values) + dot(low, values)
        return carry

    lax.fori_loop(0, 18, intra, 0, unroll=6)

    for d in (1, 3, 2):
        t_copies[d].wait_recv()

    def row_sum(i, carry):
        rows = pl.ds(pl.multiple_of(i * HEAD, HEAD), HEAD)
        label = pl.ds(ROWS + i, 1)
        state = t_recv[z, rows, :]
        within[1, rows, :] = state
        for other in range(1, 4):
            slot = lax.rem(z - other + 4, 4)
            state = state * jnp.exp(t_recv[slot, label, :]) + t_recv[slot, rows, :]
            if other < 3:
                within[other + 1, rows, :] = state
        r_send[rows, :] = state
        r_send[label, :] = (
            t_recv[0, label, :] + t_recv[1, label, :] + t_recv[2, label, :] + t_recv[3, label, :]
        )
        return carry

    lax.fori_loop(0, GROUP, row_sum, 0, unroll=2)
    r_send[ROWS + GROUP :, :] = jnp.zeros((8 - GROUP, HEAD), F32)
    r_copies = {}
    for d in (2, 1, 3):
        copy = remote(r_send, r_recv.at[d], r_send_sems.at[d - 1], r_recv_sems.at[d - 1], y_peer[d])
        copy.start()
        r_copies[d] = copy
    lax.fori_loop(18, 36, intra, 0, unroll=6)
    r_recv[0] = r_send[...]
    for d in (1, 3, 2):
        r_copies[d].wait_recv()

    def row_prefix(i, carry):
        rows = pl.ds(pl.multiple_of(i * HEAD, HEAD), HEAD)
        label = pl.ds(ROWS + i, 1)
        state = jnp.zeros((HEAD, HEAD), F32)
        for other in range(3):
            slot = lax.rem(y - other + 4, 4)
            joined = state * jnp.exp(r_recv[slot, label, :]) + r_recv[slot, rows, :]
            state = jnp.where(other < y, joined, state)
        within[0, rows, :] = state
        return carry

    lax.fori_loop(0, GROUP, row_prefix, 0, unroll=2)
    p_copies = {}
    for d in order:
        to = lax.rem(z + d, 4)
        target = chip_prefix.at[0] if d == 0 else p_send.at[d - 1]

        def chip(i, carry, to=to, target=target):
            rows = pl.ds(pl.multiple_of(i * HEAD, HEAD), HEAD)
            label = pl.ds(ROWS + i, 1)
            gone = jnp.zeros((1, HEAD), F32)
            for other in range(3):
                slot = lax.rem(z - other + 4, 4)
                gone = gone + jnp.where(other < to, t_recv[slot, label, :], 0.0)
            start = within[0, rows, :]
            target[rows, :] = start * jnp.exp(gone) + jnp.where(to > 0, within[jnp.maximum(to, 1), rows, :], 0.0)
            return carry

        lax.fori_loop(0, GROUP, chip, 0, unroll=2)
        if d:
            copy = remote(
                target, chip_prefix.at[d], p_send_sems.at[d - 1], p_recv_sems.at[d - 1], z_peer[d]
            )
            copy.start()
            p_copies[d] = copy
    lax.fori_loop(36, 48, intra, 0, unroll=6)

    f_copies = {}
    for d in (0, 1, 3, 2):
        if d:
            p_copies[d].wait_recv()
        j = lax.rem(z - d + 4, 4)

        def core(i, carry, d=d, j=j):
            h = c * 24 + j * GROUP + i
            rows = pl.ds(pl.multiple_of(i * HEAD, HEAD), HEAD)
            first_total = jnp.where(zero_first, total_ref[pl.ds(h, 1), :], partner_total[pl.ds(h, 1), :])
            first_state = jnp.where(zero_first, own_state[c, j, rows, :], partner_state[j, rows, :])
            base = chip_prefix[d, rows, :]
            full = base * jnp.exp(first_total) + first_state
            prefix[c, j, rows, :] = jnp.where(zero_first, base, full)
            f_send[j, rows, :] = jnp.where(zero_first, full, base)
            return carry

        lax.fori_loop(0, GROUP, core, 0, unroll=2)
        copy = remote(f_send.at[j], prefix.at[c, j], f_send_sems.at[d], f_recv_sems.at[d], partner)
        copy.start()
        f_copies[d] = copy

    square_ref[...] = jnp.zeros_like(square_ref)

    def inter(half, j):
        def one(i, carry):
            h = half * 24 + j * GROUP + i
            rows = pl.ds(pl.multiple_of(i * HEAD, HEAD), HEAD)
            across = jnp.broadcast_to(cum_ref[pl.ds(h, 1), :], (TOK, TOK)).T
            high, low = parts(prefix[half, j, rows, :])
            query = q_ref[:, columns(h)]
            out = attn_ref[:, columns(h)] + jnp.exp(across) * (dot(query, high) + dot(query, low))
            attn_ref[:, columns(h)] = out
            square_ref[...] += out * out
            return carry

        lax.fori_loop(0, GROUP, one, 0, unroll=6)

    for d in (0, 1, 3, 2):
        inter(c, lax.rem(z - d + 4, 4))
    for d in (0, 1, 3, 2):
        f_copies[d].wait_recv()
        inter(1 - c, lax.rem(z - d + 4, 4))
    loads[3].wait()
    scale = lax.rsqrt(jnp.sum(square_ref[...], axis=1, keepdims=True) * (1.0 / D) + 1e-6)
    scale = jnp.broadcast_to(scale, (TOK, HEAD))
    square_ref[...] = jnp.zeros_like(square_ref)

    def residual(h, carry):
        out = resid_ref[:, columns(h)].astype(F32) + attn_ref[:, columns(h)] * scale * attn_gain_ref[:, columns(h)]
        attn_ref[:, columns(h)] = out
        square_ref[...] += out * out
        return carry

    lax.fori_loop(0, HEADS, residual, 0, unroll=6)
    scale_2 = lax.rsqrt(jnp.sum(square_ref[...], axis=1, keepdims=True) * (1.0 / D) + 1e-6)
    scale_2 = jnp.broadcast_to(scale_2, (TOK, HEAD))
    select = select_ref[...]

    def norm(h, carry):
        out = attn_ref[:, columns(h)]
        high, low = parts(out)
        high_ref[:, columns(h)] = high
        low_ref[:, columns(h)] = dot(select, low).astype(BF)
        normed = (out * scale_2 * moe_gain_ref[:, columns(h)]).astype(BF)
        outbox_ref[:, columns(h)] = dot(select, normed).astype(BF)
        return carry

    lax.fori_loop(0, HEADS, norm, 0, unroll=6)
    for copies in (ps_copies, t_copies, r_copies, p_copies, f_copies):
        for copy in copies.values():
            copy.wait_send()


def attention(queries, keys, values, resid, rate, attn_gain, moe_gain, select):
    vmem = pl.BlockSpec(memory_space=pltpu.VMEM)
    hbm = pl.BlockSpec(memory_space=pl.ANY)
    dma = pltpu.SemaphoreType.DMA
    return pl.pallas_call(
        attention_kernel,
        out_shape=(
            jax.ShapeDtypeStruct((TOK, D), BF),
            jax.ShapeDtypeStruct((FLY * CAP, D), BF),
            jax.ShapeDtypeStruct((FLY * CAP, D), BF),
        ),
        in_specs=[hbm] * 4 + [vmem] * 4,
        out_specs=(vmem, vmem, vmem),
        scratch_shapes=[
            pltpu.VMEM((TOK, D), BF),
            pltpu.VMEM((TOK, D), BF),
            pltpu.VMEM((TOK, D), BF),
            pltpu.VMEM((TOK, D), BF),
            pltpu.VMEM((HEADS, TOK), F32),
            pltpu.VMEM((HEADS, TOK), F32),
            pltpu.VMEM((HEADS, TOK), F32),
            pltpu.VMEM((2, 4, ROWS, HEAD), F32),
            pltpu.VMEM((4, ROWS, HEAD), F32),
            pltpu.VMEM((3, MESSAGE, HEAD), F32),
            pltpu.VMEM((4, MESSAGE, HEAD), F32),
            pltpu.VMEM((4, ROWS, HEAD), F32),
            pltpu.VMEM((MESSAGE, HEAD), F32),
            pltpu.VMEM((4, MESSAGE, HEAD), F32),
            pltpu.VMEM((3, ROWS, HEAD), F32),
            pltpu.VMEM((4, ROWS, HEAD), F32),
            pltpu.VMEM((4, ROWS, HEAD), F32),
            pltpu.VMEM((2, 4, ROWS, HEAD), F32),
            pltpu.VMEM((TOK, D), F32),
            pltpu.VMEM((TOK, HEAD), F32),
            dma((4,)), dma((2,)), dma((4,)), dma((4,)), dma((3,)), dma((3,)),
            dma((3,)), dma((3,)), dma((3,)), dma((3,)), dma((4,)), dma((4,)),
        ],
        compiler_params=pltpu.CompilerParams(
            collective_id=0, has_side_effects=True, vmem_limit_bytes=56 * 2**20
        ),
        name="attention",
    )(queries, keys, values, resid, rate, attn_gain, moe_gain, select)


BLOCK = 4 * CAP
HALF = 2 * CAP
STEP = 1024
UNITS = 640
CHUNKS = 4
WIDE = D // CHUNKS
NARROW = 512


def window_kernel(
    outbox_ref, high_ref, low_ref, mixing_ref, up_hbm, down_hbm,
    out_ref,
    up_ref, down_ref, rows_ref, total_ref, hidden_ref, part_ref, partner_part, sum_ref,
    relay_in, relay_out, near_in, far_in, final_ref, sums_ref, high_in, low_in, mixing_in,
    load_sems, y_send, y_recv, core_send, core_recv, z_send, z_recv, hop_send, hop_recv,
    part_send, part_recv, ring_send, ring_recv, next_send, next_recv, sums_send, sums_recv,
):
    y, z, c = place()
    section = lax.axis_index("section")
    after = lax.rem(section + 1, 4)
    before = lax.rem(section + 3, 4)
    loads = [
        pltpu.make_async_copy(up_hbm, up_ref, load_sems.at[0]),
        pltpu.make_async_copy(down_hbm, down_ref, load_sems.at[1]),
    ]
    for load in loads:
        load.start()
    partner = index_of(y, z, 1 - c)
    plus, minus = index_of(y, lax.rem(z + 1, 4), c), index_of(y, lax.rem(z + 3, 4), c)
    y_peer = [index_of(lax.rem(y + d, 4), z, c) for d in range(4)]
    barrier = pltpu.get_barrier_semaphore()
    for peer in [partner, plus, minus] + y_peer[1:]:
        pl.semaphore_signal(barrier, inc=1, device_id={"ctx": peer})
    for other in (after, before):
        for peer in y_peer:
            pl.semaphore_signal(barrier, inc=1, device_id={"section": other, "ctx": peer})
    pl.semaphore_wait(barrier, 14)

    sent = []

    def send(src, dst, send_sem, recv_sem, peer, section_to=None):
        target = {"ctx": peer} if section_to is None else {"section": section_to, "ctx": peer}
        copy = pltpu.make_async_remote_copy(
            src_ref=src, dst_ref=dst, send_sem=send_sem, recv_sem=recv_sem, device_id=target
        )
        copy.start()
        sent.append(copy)

    def arrived(dst, recv_sem, peer, section_to=None):
        target = {"ctx": peer} if section_to is None else {"section": section_to, "ctx": peer}
        pltpu.make_async_remote_copy(
            src_ref=dst, dst_ref=dst, send_sem=recv_sem, recv_sem=recv_sem, device_id=target
        ).wait_recv()

    spot = (0, 2, 1, 3)

    def piece(block, core, p):
        return rows_ref.at[pl.ds(pl.multiple_of((2 * block + core) * BLOCK + p * CAP, CAP), CAP), :]

    def box(e):
        return pl.ds(pl.multiple_of(e * CAP, CAP), CAP)

    for d in (2, 1, 3):
        send(
            outbox_ref.at[box(lax.rem(y + d, 4)), :], piece(0, c, spot[d]),
            y_send.at[d - 1], y_recv.at[d - 1], y_peer[d],
        )
    rows_ref[pl.ds(pl.multiple_of(c * BLOCK, CAP), CAP), :] = outbox_ref[box(y), :]

    def spread(p):
        src = piece(0, c, p)
        send(src, piece(1, c, p), z_send.at[0, p], z_recv.at[0, p], plus)
        send(src, piece(2, c, p), z_send.at[1, p], z_recv.at[1, p], minus)
        send(src, src, core_send.at[0, p], core_recv.at[0, p], partner)

    def from_minus(p):
        src = piece(1, c, p)
        arrived(src, z_recv.at[0, p], minus)
        if p < 2:
            send(src, piece(3, c, p), hop_send.at[p], hop_recv.at[p], plus)
        send(src, src, core_send.at[1, p], core_recv.at[1, p], partner)

    def from_plus(p):
        src = piece(2, c, p)
        arrived(src, z_recv.at[1, p], plus)
        if p >= 2:
            send(src, piece(3, c, p), hop_send.at[p], hop_recv.at[p], minus)
        send(src, src, core_send.at[2, p], core_recv.at[2, p], partner)

    def from_far(p):
        src = piece(3, c, p)
        arrived(src, hop_recv.at[p], minus if p < 2 else plus)
        send(src, src, core_send.at[3, p], core_recv.at[3, p], partner)

    spread(0)
    send(high_ref, high_in, next_send.at[0], next_recv.at[0], y_peer[0], after)
    send(low_ref, low_in, next_send.at[1], next_recv.at[1], y_peer[0], after)
    send(mixing_ref, mixing_in, next_send.at[2], next_recv.at[2], y_peer[0], after)
    for d in (1, 3, 2):
        arrived(piece(0, c, spot[d]), y_recv.at[d - 1], y_peer[4 - d])
        spread(spot[d])
    for p in (0, 2, 3, 1):
        from_minus(p)
        from_plus(p)

    def up(blocks):
        first, count = blocks[0] * 2 * BLOCK, len(blocks) * 2 * BLOCK
        for block in blocks:
            for p in range(4):
                arrived(piece(block, 1 - c, p), core_recv.at[block, p], partner)
        total_ref[:count, :] = jnp.zeros((count, UNITS), F32)

        def one(i, carry):
            at = pl.ds(pl.multiple_of(i * STEP, STEP), STEP)
            total_ref[:count, :] += dot(rows_ref[first : first + count, at], up_ref[at, :])
            return carry

        lax.fori_loop(0, D // STEP, one, 0)
        hidden_ref[first : first + count, :] = jax.nn.gelu(
            total_ref[:count, :], approximate=True
        ).astype(BF)

    loads[0].wait()
    up((0, 1, 2))
    for p in (0, 2, 3, 1):
        from_far(p)
    up((3,))
    loads[1].wait()

    def down(q):
        for i in range(WIDE // NARROW):
            at = slice(i * NARROW, (i + 1) * NARROW)
            out = dot(hidden_ref[...], down_ref[:, q * WIDE + i * NARROW : q * WIDE + (i + 1) * NARROW])
            out = out.astype(BF)
            for block in range(4):
                for core in range(2):
                    row = (2 * block + core) * BLOCK
                    part_ref[q, core, block * BLOCK : (block + 1) * BLOCK, at] = out[row : row + BLOCK, :]
        send(part_ref.at[q, 1 - c], partner_part.at[q], part_send.at[q], part_recv.at[q], partner)

    def over_columns(body):
        def one(i, carry):
            body(pl.ds(pl.multiple_of(i * NARROW, NARROW), NARROW))
            return carry

        lax.fori_loop(0, WIDE // NARROW, one, 0)

    def share(q, block, half):
        first = block * BLOCK + half * HALF
        return sum_ref.at[q, first : first + HALF, :]

    def core_sum(q):
        arrived(partner_part.at[q], part_recv.at[q], partner)

        def add(at):
            sum_ref[q, :, at] = (
                part_ref[q, c, :, at].astype(F32) + partner_part[q, :, at].astype(F32)
            ).astype(BF)

        over_columns(add)
        send(share(q, 3, 0), relay_in.at[q, 0], ring_send.at[q, 2], ring_recv.at[q, 2], plus)
        send(share(q, 3, 1), relay_in.at[q, 1], ring_send.at[q, 3], ring_recv.at[q, 3], minus)
        send(share(q, 2, 1), near_in.at[q, 0], ring_send.at[q, 0], ring_recv.at[q, 0], plus)
        send(share(q, 1, 0), near_in.at[q, 1], ring_send.at[q, 1], ring_recv.at[q, 1], minus)

    def relay(q):
        for side in range(2):
            arrived(relay_in.at[q, side], ring_recv.at[q, 2 + side], (minus, plus)[side])
            mine = share(q, 2 - side, side)

            def add(at, side=side, mine=mine):
                relay_out[q, side, :, at] = (
                    mine[:, at].astype(F32) + relay_in[q, side, :, at].astype(F32)
                ).astype(BF)

            over_columns(add)
            send(
                relay_out.at[q, side], far_in.at[q, side],
                ring_send.at[q, 4 + side], ring_recv.at[q, 4 + side], (plus, minus)[side],
            )

    def final(q):
        arrived(near_in.at[q, 0], ring_recv.at[q, 0], minus)
        arrived(near_in.at[q, 1], ring_recv.at[q, 1], plus)
        arrived(far_in.at[q, 0], ring_recv.at[q, 4], minus)
        arrived(far_in.at[q, 1], ring_recv.at[q, 5], plus)
        for half in range(2):
            mine = share(q, 0, half)

            def add(at, half=half, mine=mine):
                final_ref[q, half * HALF : (half + 1) * HALF, at] = (
                    mine[:, at].astype(F32)
                    + near_in[q, 1 - half, :, at].astype(F32)
                    + far_in[q, half, :, at].astype(F32)
                ).astype(BF)

            over_columns(add)
            for d in ((0, 2), (1, 3))[half]:
                p = spot[d]
                send(
                    final_ref.at[q, p * CAP : (p + 1) * CAP, :], sums_ref.at[q, box(y), :],
                    sums_send.at[q, d], sums_recv.at[q, d], y_peer[(4 - d) % 4], after,
                )

    down(0)
    down(1)
    core_sum(0)
    down(2)
    core_sum(1)
    relay(0)
    down(3)
    core_sum(2)
    relay(1)
    final(0)
    core_sum(3)
    relay(2)
    final(1)
    relay(3)
    final(2)
    final(3)
    arrived(high_in, next_recv.at[0], y_peer[0], before)
    arrived(low_in, next_recv.at[1], y_peer[0], before)
    arrived(mixing_in, next_recv.at[2], y_peer[0], before)
    first = mixing_in[:, :BLOCK].astype(BF)
    weight_high, weight_low = parts(mixing_in[:, BLOCK:])
    for q in range(CHUNKS):
        for d in range(4):
            arrived(sums_ref.at[q, 0:CAP, :], sums_recv.at[q, d], y_peer[d], before)
        for i in range(WIDE // NARROW):
            sums = sums_ref[q, :, i * NARROW : (i + 1) * NARROW]
            at = slice(q * WIDE + i * NARROW, q * WIDE + (i + 1) * NARROW)
            mixed = dot(weight_high, sums) + dot(weight_low, sums)
            out_ref[:, at] = ((high_in[:, at].astype(F32) + dot(first, low_in[:, at])) + mixed).astype(BF)
    for copy in sent:
        copy.wait_send()


def window(outbox, high, low, mixing, w_up, w_down):
    vmem = pl.BlockSpec(memory_space=pltpu.VMEM)
    hbm = pl.BlockSpec(memory_space=pl.ANY)
    dma = pltpu.SemaphoreType.DMA
    return pl.pallas_call(
        window_kernel,
        out_shape=jax.ShapeDtypeStruct((TOK, D), BF),
        in_specs=[vmem] * 4 + [hbm] * 2,
        out_specs=vmem,
        scratch_shapes=[
            pltpu.VMEM((D, UNITS), BF),
            pltpu.VMEM((UNITS, D), BF),
            pltpu.VMEM((8 * BLOCK, D), BF),
            pltpu.VMEM((6 * BLOCK, UNITS), F32),
            pltpu.VMEM((8 * BLOCK, UNITS), BF),
            pltpu.VMEM((CHUNKS, 2, 4 * BLOCK, WIDE), BF),
            pltpu.VMEM((CHUNKS, 4 * BLOCK, WIDE), BF),
            pltpu.VMEM((CHUNKS, 4 * BLOCK, WIDE), BF),
            pltpu.VMEM((CHUNKS, 2, HALF, WIDE), BF),
            pltpu.VMEM((CHUNKS, 2, HALF, WIDE), BF),
            pltpu.VMEM((CHUNKS, 2, HALF, WIDE), BF),
            pltpu.VMEM((CHUNKS, 2, HALF, WIDE), BF),
            pltpu.VMEM((CHUNKS, BLOCK, WIDE), BF),
            pltpu.VMEM((CHUNKS, BLOCK, WIDE), BF),
            pltpu.VMEM((TOK, D), BF),
            pltpu.VMEM((BLOCK, D), BF),
            pltpu.VMEM((TOK, 2 * BLOCK), F32),
            dma((2,)), dma((3,)), dma((3,)), dma((4, 4)), dma((4, 4)), dma((2, 4)), dma((2, 4)),
            dma((4,)), dma((4,)), dma((CHUNKS,)), dma((CHUNKS,)), dma((CHUNKS, 6)), dma((CHUNKS, 6)),
            dma((3,)), dma((3,)), dma((CHUNKS, 4)), dma((CHUNKS, 4)),
        ],
        compiler_params=pltpu.CompilerParams(
            collective_id=1, has_side_effects=True, vmem_limit_bytes=60 * 2**20
        ),
        name="window",
    )(outbox, high, low, mixing, w_up, w_down)


def slots_of(chosen):
    count = chosen.shape[0]
    onehot = (chosen[:, None] == jnp.arange(EXPERTS)[None, :]).astype(BF)
    before = (jnp.arange(count)[:, None] > jnp.arange(count)[None, :]).astype(BF)
    ahead = dot(before, onehot)
    return jnp.sum(ahead * onehot.astype(F32), axis=1).astype(jnp.int32)


def local(
    resid, queries, keys, values, log_decay, attn_gain, moe_gain, experts, combine_weight, w_up, w_down
):
    chosen = experts[0].reshape(-1)
    slot = slots_of(chosen)
    target = chosen * CAP + slot
    in_window = chosen < FLY
    select = ((target[None, :] == jnp.arange(FLY * CAP)[:, None]) & in_window[None, :]).astype(BF)
    select_tok = select.reshape(FLY * CAP, TOK, 2).sum(axis=2).astype(BF)
    high, low, outbox = attention(
        queries[0], keys[0], values[0], resid[0], log_decay[0].T, attn_gain, moe_gain, select_tok
    )
    pairs = select.T.reshape(TOK, 2, FLY * CAP).astype(F32)
    inside = in_window.reshape(TOK, 2)
    first = jnp.where(inside[:, 0:1], pairs[:, 0], pairs[:, 1])
    weighted = (pairs * combine_weight[0][:, :, None]).sum(axis=1)
    mixing = jnp.concatenate([first, weighted], axis=1)
    return window(outbox, high, low, mixing, w_up[0], w_down[0])[None]


def solution(mesh):
    token = P("section", "ctx", None)
    return jax.shard_map(
        local,
        mesh=mesh,
        in_specs=(
            token, token, token, token, token,
            P("section", None), P("section", None),
            token, token,
            P("section", None, "ctx"), token,
        ),
        out_specs=token,
        check_vma=False,
    )
```

```python
import jax
import jax.numpy as jnp
from jax import lax
from jax.experimental import pallas as pl
from jax.experimental.pallas import tpu as pltpu
from jax.sharding import PartitionSpec as P

D = 6144
HEADS = 48
HEAD = 128
TOK = 128
EXPERTS = 32
SHARDS = 8
CAP = 16
FLY = 4
SUB = 2
ROWS = SUB * HEAD
MESSAGE = ROWS + 8
BF = jnp.bfloat16
F32 = jnp.float32
HIGH = lax.Precision.HIGHEST


def dot(a, b):
    return jnp.dot(a, b, preferred_element_type=F32)


def dot_t(a, b):
    return lax.dot_general(a, b, (((1,), (1,)), ((), ())), preferred_element_type=F32)


def parts(x):
    high = x.astype(BF)
    return high, (x - high.astype(F32)).astype(BF)


def place():
    me = lax.axis_index("ctx")
    return me // 8, lax.rem(me // 2, 4), lax.rem(me, 2)


def index_of(y, z, c):
    return (y * 4 + z) * 2 + c


def columns(h):
    return pl.ds(pl.multiple_of(h * HEAD, HEAD), HEAD)


def attention_kernel(
    q_hbm, k_hbm, v_hbm, resid_hbm, rate_ref, attn_gain_ref, moe_gain_ref, select_ref,
    high_ref, low_ref, outbox_ref,
    q_ref, k_ref, v_ref, resid_ref, cum_ref, total_ref, partner_total, own_state,
    partner_state, t_send, t_recv, within, r_send, r_recv, p_send, chip_prefix,
    f_send, prefix, attn_ref, square_ref,
    load_sems, small_sems, ps_send_sems, ps_recv_sems, t_send_sems, t_recv_sems,
    r_send_sems, r_recv_sems, p_send_sems, p_recv_sems, f_send_sems, f_recv_sems,
):
    y, z, c = place()
    loads = [
        pltpu.make_async_copy(a, b, load_sems.at[i])
        for i, (a, b) in enumerate(
            ((k_hbm, k_ref), (v_hbm, v_ref), (q_hbm, q_ref), (resid_hbm, resid_ref))
        )
    ]
    for load in loads:
        load.start()
    barrier = pltpu.get_barrier_semaphore()
    partner = index_of(y, z, 1 - c)
    z_peer = [index_of(y, lax.rem(z + d, 4), c) for d in range(4)]
    y_peer = [index_of(lax.rem(y + d, 4), z, c) for d in range(4)]
    for peer in [partner] + z_peer[1:] + y_peer[1:]:
        pl.semaphore_signal(barrier, inc=1, device_id={"ctx": peer})

    rate = rate_ref[...]
    earlier = lax.broadcasted_iota(jnp.int32, (TOK, TOK), 0)
    later = lax.broadcasted_iota(jnp.int32, (TOK, TOK), 1)
    cum_ref[...] = jnp.dot(
        rate, (earlier <= later).astype(F32), precision=HIGH, preferred_element_type=F32
    )
    total_ref[...] = jnp.dot(
        rate, jnp.ones((TOK, TOK), F32), precision=HIGH, preferred_element_type=F32
    )
    copies = []

    def remote(src, dst, send_sem, recv_sem, peer):
        copy = pltpu.make_async_remote_copy(
            src_ref=src, dst_ref=dst, send_sem=send_sem, recv_sem=recv_sem, device_id={"ctx": peer}
        )
        copy.start()
        copies.append(copy)
        return copy

    def tile(i):
        return pl.ds(pl.multiple_of(i * HEAD, HEAD), HEAD)

    def state_of(h):
        row = jnp.exp(total_ref[pl.ds(h, 1), :] - cum_ref[pl.ds(h, 1), :])
        keys = k_ref[:, columns(h)].astype(F32).T * row
        high, low = parts(keys)
        values = v_ref[:, columns(h)]
        return dot(high, values) + dot(low, values)

    def states(half, s):
        def one(n, carry):
            own_state[half, s, tile(n), :] = state_of(half * 24 + s * 8 + n)
            return carry

        lax.fori_loop(0, 8, one, 0, unroll=8)

    loads[0].wait()
    loads[1].wait()
    states(1 - c, 0)
    pl.semaphore_wait(barrier, 7)
    totals = remote(total_ref, partner_total, small_sems.at[0], small_sems.at[1], partner)
    zero_first = c == 0

    def swap(s):
        return remote(
            own_state.at[1 - c, s], partner_state.at[s], ps_send_sems.at[s], ps_recv_sems.at[s], partner
        )

    order = (2, 1, 3, 0)
    t_copies = {}

    def join(s):
        for d in order:
            j = lax.rem(z + d, 4)
            target = t_recv.at[s, 0] if d == 0 else t_send.at[s, d - 1]
            for i in range(SUB):
                h = c * 24 + s * 8 + j * SUB + i
                rows = tile(j * SUB + i)
                mine = total_ref[pl.ds(h, 1), :]
                other = partner_total[pl.ds(h, 1), :]
                keep = jnp.exp(jnp.where(zero_first, other, 0.0))
                take = jnp.exp(jnp.where(zero_first, 0.0, mine))
                target[i * HEAD : (i + 1) * HEAD, :] = (
                    keep * own_state[c, s, rows, :] + take * partner_state[s, rows, :]
                )
                target[ROWS + i : ROWS + i + 1, :] = mine + other
            target[ROWS + SUB :, :] = jnp.zeros((8 - SUB, HEAD), F32)
            if d:
                t_copies[s, d] = remote(
                    target, t_recv.at[s, d], t_send_sems.at[s, d - 1], t_recv_sems.at[s, d - 1], z_peer[d]
                )

    lower = earlier >= later

    def intra(first, last):
        def one(h, carry):
            across = jnp.broadcast_to(cum_ref[pl.ds(h, 1), :], (TOK, TOK))
            weights = jnp.exp(jnp.where(lower, across.T - across, -1e30))
            scores = dot_t(q_ref[:, columns(h)], k_ref[:, columns(h)]) * weights
            high, low = parts(scores)
            values = v_ref[:, columns(h)]
            attn_ref[:, columns(h)] = dot(high, values) + dot(low, values)
            return carry

        lax.fori_loop(first, last, one, 0, unroll=6)

    r_copies = {}

    def row_sum(s):
        for d in (1, 3, 2):
            t_copies[s, d].wait_recv()
        for i in range(SUB):
            rows = slice(i * HEAD, (i + 1) * HEAD)
            label = slice(ROWS + i, ROWS + i + 1)
            state = t_recv[s, z, rows, :]
            within[s, 1, rows, :] = state
            for other in range(1, 4):
                slot = lax.rem(z - other + 4, 4)
                state = state * jnp.exp(t_recv[s, slot, label, :]) + t_recv[s, slot, rows, :]
                if other < 3:
                    within[s, other + 1, rows, :] = state
            r_send[s, rows, :] = state
            r_send[s, label, :] = (
                t_recv[s, 0, label, :] + t_recv[s, 1, label, :]
                + t_recv[s, 2, label, :] + t_recv[s, 3, label, :]
            )
        r_send[s, ROWS + SUB :, :] = jnp.zeros((8 - SUB, HEAD), F32)
        for d in (2, 1, 3):
            r_copies[s, d] = remote(
                r_send.at[s], r_recv.at[s, d], r_send_sems.at[s, d - 1], r_recv_sems.at[s, d - 1], y_peer[d]
            )
        r_recv[s, 0] = r_send[s]

    p_copies = {}

    def chip_prefixes(s):
        for d in (1, 3, 2):
            r_copies[s, d].wait_recv()
        for i in range(SUB):
            rows = slice(i * HEAD, (i + 1) * HEAD)
            label = slice(ROWS + i, ROWS + i + 1)
            state = jnp.zeros((HEAD, HEAD), F32)
            for other in range(3):
                slot = lax.rem(y - other + 4, 4)
                joined = state * jnp.exp(r_recv[s, slot, label, :]) + r_recv[s, slot, rows, :]
                state = jnp.where(other < y, joined, state)
            within[s, 0, rows, :] = state
        for d in order:
            to = lax.rem(z + d, 4)
            target = chip_prefix.at[s, 0] if d == 0 else p_send.at[s, d - 1]
            for i in range(SUB):
                rows = slice(i * HEAD, (i + 1) * HEAD)
                label = slice(ROWS + i, ROWS + i + 1)
                gone = jnp.zeros((1, HEAD), F32)
                for other in range(3):
                    slot = lax.rem(z - other + 4, 4)
                    gone = gone + jnp.where(other < to, t_recv[s, slot, label, :], 0.0)
                inside = within[s, jnp.maximum(to, 1), rows, :]
                target[rows, :] = within[s, 0, rows, :] * jnp.exp(gone) + jnp.where(to > 0, inside, 0.0)
            if d:
                p_copies[s, d] = remote(
                    target, chip_prefix.at[s, d], p_send_sems.at[s, d - 1], p_recv_sems.at[s, d - 1], z_peer[d]
                )

    f_copies = {}

    def finish(s):
        for d in (0, 1, 3, 2):
            if d:
                p_copies[s, d].wait_recv()
            j = lax.rem(z - d + 4, 4)
            for i in range(SUB):
                h = c * 24 + s * 8 + j * SUB + i
                rows = tile(j * SUB + i)
                first_total = jnp.where(
                    zero_first, total_ref[pl.ds(h, 1), :], partner_total[pl.ds(h, 1), :]
                )
                first_state = jnp.where(zero_first, own_state[c, s, rows, :], partner_state[s, rows, :])
                base = chip_prefix[s, d, i * HEAD : (i + 1) * HEAD, :]
                full = base * jnp.exp(first_total) + first_state
                prefix[c, s, rows, :] = jnp.where(zero_first, base, full)
                f_send[s, rows, :] = jnp.where(zero_first, full, base)
        f_copies[s] = remote(f_send.at[s], prefix.at[c, s], f_send_sems.at[s], f_recv_sems.at[s], partner)

    square_ref[...] = jnp.zeros_like(square_ref)

    def inter(half, s):
        def one(n, carry):
            h = half * 24 + s * 8 + n
            across = jnp.broadcast_to(cum_ref[pl.ds(h, 1), :], (TOK, TOK)).T
            high, low = parts(prefix[half, s, tile(n), :])
            query = q_ref[:, columns(h)]
            out = attn_ref[:, columns(h)] + jnp.exp(across) * (dot(query, high) + dot(query, low))
            attn_ref[:, columns(h)] = out
            square_ref[...] += out * out
            return carry

        lax.fori_loop(0, 8, one, 0, unroll=8)

    swaps = [swap(0)]
    states(c, 0)
    totals.wait_recv()
    swaps[0].wait_recv()
    join(0)
    for s in (1, 2):
        states(1 - c, s)
        swaps.append(swap(s))
        states(c, s)
        swaps[s].wait_recv()
        join(s)
    loads[2].wait()
    intra(0, 12)
    row_sum(0)
    intra(12, 24)
    row_sum(1)
    chip_prefixes(0)
    intra(24, 36)
    row_sum(2)
    chip_prefixes(1)
    intra(36, 48)
    chip_prefixes(2)
    for s in range(3):
        finish(s)
        inter(c, s)
        f_copies[s].wait_recv()
        inter(1 - c, s)
    loads[3].wait()
    scale = lax.rsqrt(jnp.sum(square_ref[...], axis=1, keepdims=True) * (1.0 / D) + 1e-6)
    scale = jnp.broadcast_to(scale, (TOK, HEAD))
    square_ref[...] = jnp.zeros_like(square_ref)

    def residual(h, carry):
        out = resid_ref[:, columns(h)].astype(F32) + attn_ref[:, columns(h)] * scale * attn_gain_ref[:, columns(h)]
        attn_ref[:, columns(h)] = out
        square_ref[...] += out * out
        return carry

    lax.fori_loop(0, HEADS, residual, 0, unroll=6)
    scale_2 = lax.rsqrt(jnp.sum(square_ref[...], axis=1, keepdims=True) * (1.0 / D) + 1e-6)
    scale_2 = jnp.broadcast_to(scale_2, (TOK, HEAD))
    select = select_ref[...]

    def norm(h, carry):
        out = attn_ref[:, columns(h)]
        high, low = parts(out)
        high_ref[:, columns(h)] = high
        low_ref[:, columns(h)] = dot(select, low).astype(BF)
        normed = (out * scale_2 * moe_gain_ref[:, columns(h)]).astype(BF)
        outbox_ref[:, columns(h)] = dot(select, normed).astype(BF)
        return carry

    lax.fori_loop(0, HEADS, norm, 0, unroll=6)
    for copy in copies:
        copy.wait_send()


def attention(queries, keys, values, resid, rate, attn_gain, moe_gain, select):
    vmem = pl.BlockSpec(memory_space=pltpu.VMEM)
    hbm = pl.BlockSpec(memory_space=pl.ANY)
    dma = pltpu.SemaphoreType.DMA
    return pl.pallas_call(
        attention_kernel,
        out_shape=(
            jax.ShapeDtypeStruct((TOK, D), BF),
            jax.ShapeDtypeStruct((FLY * CAP, D), BF),
            jax.ShapeDtypeStruct((FLY * CAP, D), BF),
        ),
        in_specs=[hbm] * 4 + [vmem] * 4,
        out_specs=(vmem, vmem, vmem),
        scratch_shapes=[
            pltpu.VMEM((TOK, D), BF),
            pltpu.VMEM((TOK, D), BF),
            pltpu.VMEM((TOK, D), BF),
            pltpu.VMEM((TOK, D), BF),
            pltpu.VMEM((HEADS, TOK), F32),
            pltpu.VMEM((HEADS, TOK), F32),
            pltpu.VMEM((HEADS, TOK), F32),
            pltpu.VMEM((2, 3, 4 * ROWS, HEAD), F32),
            pltpu.VMEM((3, 4 * ROWS, HEAD), F32),
            pltpu.VMEM((3, 3, MESSAGE, HEAD), F32),
            pltpu.VMEM((3, 4, MESSAGE, HEAD), F32),
            pltpu.VMEM((3, 4, ROWS, HEAD), F32),
            pltpu.VMEM((3, MESSAGE, HEAD), F32),
            pltpu.VMEM((3, 4, MESSAGE, HEAD), F32),
            pltpu.VMEM((3, 3, ROWS, HEAD), F32),
            pltpu.VMEM((3, 4, ROWS, HEAD), F32),
            pltpu.VMEM((3, 4 * ROWS, HEAD), F32),
            pltpu.VMEM((2, 3, 4 * ROWS, HEAD), F32),
            pltpu.VMEM((TOK, D), F32),
            pltpu.VMEM((TOK, HEAD), F32),
            dma((4,)), dma((2,)), dma((3,)), dma((3,)), dma((3, 3)), dma((3, 3)),
            dma((3, 3)), dma((3, 3)), dma((3, 3)), dma((3, 3)), dma((3,)), dma((3,)),
        ],
        compiler_params=pltpu.CompilerParams(
            collective_id=0, has_side_effects=True, vmem_limit_bytes=56 * 2**20
        ),
        name="attention",
    )(queries, keys, values, resid, rate, attn_gain, moe_gain, select)


BLOCK = 4 * CAP
HALF = 2 * CAP
STEP = 1024
UNITS = 640
CHUNKS = 4
WIDE = D // CHUNKS
NARROW = 512


def window_kernel(
    outbox_ref, high_ref, low_ref, mixing_ref, up_hbm, down_hbm,
    out_ref,
    up_ref, down_ref, rows_ref, total_ref, hidden_ref, part_ref, partner_part, sum_ref,
    relay_in, relay_out, near_in, far_in, final_ref, sums_ref, high_in, low_in, mixing_in,
    load_sems, y_send, y_recv, core_send, core_recv, z_send, z_recv, hop_send, hop_recv,
    part_send, part_recv, ring_send, ring_recv, next_send, next_recv, sums_send, sums_recv,
):
    y, z, c = place()
    section = lax.axis_index("section")
    after = lax.rem(section + 1, 4)
    before = lax.rem(section + 3, 4)
    loads = [
        pltpu.make_async_copy(up_hbm, up_ref, load_sems.at[0]),
        pltpu.make_async_copy(down_hbm, down_ref, load_sems.at[1]),
    ]
    for load in loads:
        load.start()
    partner = index_of(y, z, 1 - c)
    plus, minus = index_of(y, lax.rem(z + 1, 4), c), index_of(y, lax.rem(z + 3, 4), c)
    y_peer = [index_of(lax.rem(y + d, 4), z, c) for d in range(4)]
    barrier = pltpu.get_barrier_semaphore()
    for peer in [partner, plus, minus] + y_peer[1:]:
        pl.semaphore_signal(barrier, inc=1, device_id={"ctx": peer})
    for other in (after, before):
        for peer in y_peer:
            pl.semaphore_signal(barrier, inc=1, device_id={"section": other, "ctx": peer})
    pl.semaphore_wait(barrier, 14)

    sent = []

    def send(src, dst, send_sem, recv_sem, peer, section_to=None):
        target = {"ctx": peer} if section_to is None else {"section": section_to, "ctx": peer}
        copy = pltpu.make_async_remote_copy(
            src_ref=src, dst_ref=dst, send_sem=send_sem, recv_sem=recv_sem, device_id=target
        )
        copy.start()
        sent.append(copy)

    def arrived(dst, recv_sem, peer, section_to=None):
        target = {"ctx": peer} if section_to is None else {"section": section_to, "ctx": peer}
        pltpu.make_async_remote_copy(
            src_ref=dst, dst_ref=dst, send_sem=recv_sem, recv_sem=recv_sem, device_id=target
        ).wait_recv()

    spot = (0, 2, 1, 3)

    def piece(block, core, p):
        return rows_ref.at[pl.ds(pl.multiple_of((2 * block + core) * BLOCK + p * CAP, CAP), CAP), :]

    def box(e):
        return pl.ds(pl.multiple_of(e * CAP, CAP), CAP)

    for d in (2, 1, 3):
        send(
            outbox_ref.at[box(lax.rem(y + d, 4)), :], piece(0, c, spot[d]),
            y_send.at[d - 1], y_recv.at[d - 1], y_peer[d],
        )
    rows_ref[pl.ds(pl.multiple_of(c * BLOCK, CAP), CAP), :] = outbox_ref[box(y), :]

    def spread(p):
        src = piece(0, c, p)
        send(src, piece(1, c, p), z_send.at[0, p], z_recv.at[0, p], plus)
        send(src, piece(2, c, p), z_send.at[1, p], z_recv.at[1, p], minus)
        send(src, src, core_send.at[0, p], core_recv.at[0, p], partner)

    def from_minus(p):
        src = piece(1, c, p)
        arrived(src, z_recv.at[0, p], minus)
        if p < 2:
            send(src, piece(3, c, p), hop_send.at[p], hop_recv.at[p], plus)
        send(src, src, core_send.at[1, p], core_recv.at[1, p], partner)

    def from_plus(p):
        src = piece(2, c, p)
        arrived(src, z_recv.at[1, p], plus)
        if p >= 2:
            send(src, piece(3, c, p), hop_send.at[p], hop_recv.at[p], minus)
        send(src, src, core_send.at[2, p], core_recv.at[2, p], partner)

    def from_far(p):
        src = piece(3, c, p)
        arrived(src, hop_recv.at[p], minus if p < 2 else plus)
        send(src, src, core_send.at[3, p], core_recv.at[3, p], partner)

    spread(0)
    send(high_ref, high_in, next_send.at[0], next_recv.at[0], y_peer[0], after)
    send(low_ref, low_in, next_send.at[1], next_recv.at[1], y_peer[0], after)
    send(mixing_ref, mixing_in, next_send.at[2], next_recv.at[2], y_peer[0], after)
    for d in (1, 3, 2):
        arrived(piece(0, c, spot[d]), y_recv.at[d - 1], y_peer[4 - d])
        spread(spot[d])
    for p in (0, 2, 3, 1):
        from_minus(p)
        from_plus(p)

    def up(blocks):
        first, count = blocks[0] * 2 * BLOCK, len(blocks) * 2 * BLOCK
        for block in blocks:
            for p in range(4):
                arrived(piece(block, 1 - c, p), core_recv.at[block, p], partner)
        total_ref[:count, :] = jnp.zeros((count, UNITS), F32)

        def one(i, carry):
            at = pl.ds(pl.multiple_of(i * STEP, STEP), STEP)
            total_ref[:count, :] += dot(rows_ref[first : first + count, at], up_ref[at, :])
            return carry

        lax.fori_loop(0, D // STEP, one, 0)
        hidden_ref[first : first + count, :] = jax.nn.gelu(
            total_ref[:count, :], approximate=True
        ).astype(BF)

    loads[0].wait()
    up((0, 1, 2))
    for p in (0, 2, 3, 1):
        from_far(p)
    up((3,))
    loads[1].wait()

    def down(q):
        for i in range(WIDE // NARROW):
            at = slice(i * NARROW, (i + 1) * NARROW)
            out = dot(hidden_ref[...], down_ref[:, q * WIDE + i * NARROW : q * WIDE + (i + 1) * NARROW])
            out = out.astype(BF)
            for block in range(4):
                for core in range(2):
                    row = (2 * block + core) * BLOCK
                    part_ref[q, core, block * BLOCK : (block + 1) * BLOCK, at] = out[row : row + BLOCK, :]
        send(part_ref.at[q, 1 - c], partner_part.at[q], part_send.at[q], part_recv.at[q], partner)

    def over_columns(body):
        def one(i, carry):
            body(pl.ds(pl.multiple_of(i * NARROW, NARROW), NARROW))
            return carry

        lax.fori_loop(0, WIDE // NARROW, one, 0)

    def share(q, block, half):
        first = block * BLOCK + half * HALF
        return sum_ref.at[q, first : first + HALF, :]

    def core_sum(q):
        arrived(partner_part.at[q], part_recv.at[q], partner)

        def add(at):
            sum_ref[q, :, at] = (
                part_ref[q, c, :, at].astype(F32) + partner_part[q, :, at].astype(F32)
            ).astype(BF)

        over_columns(add)
        send(share(q, 3, 0), relay_in.at[q, 0], ring_send.at[q, 2], ring_recv.at[q, 2], plus)
        send(share(q, 3, 1), relay_in.at[q, 1], ring_send.at[q, 3], ring_recv.at[q, 3], minus)
        send(share(q, 2, 1), near_in.at[q, 0], ring_send.at[q, 0], ring_recv.at[q, 0], plus)
        send(share(q, 1, 0), near_in.at[q, 1], ring_send.at[q, 1], ring_recv.at[q, 1], minus)

    def relay(q):
        for side in range(2):
            arrived(relay_in.at[q, side], ring_recv.at[q, 2 + side], (minus, plus)[side])
            mine = share(q, 2 - side, side)

            def add(at, side=side, mine=mine):
                relay_out[q, side, :, at] = (
                    mine[:, at].astype(F32) + relay_in[q, side, :, at].astype(F32)
                ).astype(BF)

            over_columns(add)
            send(
                relay_out.at[q, side], far_in.at[q, side],
                ring_send.at[q, 4 + side], ring_recv.at[q, 4 + side], (plus, minus)[side],
            )

    def final(q):
        arrived(near_in.at[q, 0], ring_recv.at[q, 0], minus)
        arrived(near_in.at[q, 1], ring_recv.at[q, 1], plus)
        arrived(far_in.at[q, 0], ring_recv.at[q, 4], minus)
        arrived(far_in.at[q, 1], ring_recv.at[q, 5], plus)
        for half in range(2):
            mine = share(q, 0, half)

            def add(at, half=half, mine=mine):
                final_ref[q, half * HALF : (half + 1) * HALF, at] = (
                    mine[:, at].astype(F32)
                    + near_in[q, 1 - half, :, at].astype(F32)
                    + far_in[q, half, :, at].astype(F32)
                ).astype(BF)

            over_columns(add)
            for d in ((0, 2), (1, 3))[half]:
                p = spot[d]
                send(
                    final_ref.at[q, p * CAP : (p + 1) * CAP, :], sums_ref.at[q, box(y), :],
                    sums_send.at[q, d], sums_recv.at[q, d], y_peer[(4 - d) % 4], after,
                )

    down(0)
    down(1)
    core_sum(0)
    down(2)
    core_sum(1)
    relay(0)
    down(3)
    core_sum(2)
    relay(1)
    final(0)
    core_sum(3)
    relay(2)
    final(1)
    relay(3)
    final(2)
    final(3)
    arrived(high_in, next_recv.at[0], y_peer[0], before)
    arrived(low_in, next_recv.at[1], y_peer[0], before)
    arrived(mixing_in, next_recv.at[2], y_peer[0], before)
    first = mixing_in[:, :BLOCK].astype(BF)
    weight_high, weight_low = parts(mixing_in[:, BLOCK:])
    for q in range(CHUNKS):
        for d in range(4):
            arrived(sums_ref.at[q, 0:CAP, :], sums_recv.at[q, d], y_peer[d], before)
        for i in range(WIDE // NARROW):
            sums = sums_ref[q, :, i * NARROW : (i + 1) * NARROW]
            at = slice(q * WIDE + i * NARROW, q * WIDE + (i + 1) * NARROW)
            mixed = dot(weight_high, sums) + dot(weight_low, sums)
            out_ref[:, at] = ((high_in[:, at].astype(F32) + dot(first, low_in[:, at])) + mixed).astype(BF)
    for copy in sent:
        copy.wait_send()


def window(outbox, high, low, mixing, w_up, w_down):
    vmem = pl.BlockSpec(memory_space=pltpu.VMEM)
    hbm = pl.BlockSpec(memory_space=pl.ANY)
    dma = pltpu.SemaphoreType.DMA
    return pl.pallas_call(
        window_kernel,
        out_shape=jax.ShapeDtypeStruct((TOK, D), BF),
        in_specs=[vmem] * 4 + [hbm] * 2,
        out_specs=vmem,
        scratch_shapes=[
            pltpu.VMEM((D, UNITS), BF),
            pltpu.VMEM((UNITS, D), BF),
            pltpu.VMEM((8 * BLOCK, D), BF),
            pltpu.VMEM((6 * BLOCK, UNITS), F32),
            pltpu.VMEM((8 * BLOCK, UNITS), BF),
            pltpu.VMEM((CHUNKS, 2, 4 * BLOCK, WIDE), BF),
            pltpu.VMEM((CHUNKS, 4 * BLOCK, WIDE), BF),
            pltpu.VMEM((CHUNKS, 4 * BLOCK, WIDE), BF),
            pltpu.VMEM((CHUNKS, 2, HALF, WIDE), BF),
            pltpu.VMEM((CHUNKS, 2, HALF, WIDE), BF),
            pltpu.VMEM((CHUNKS, 2, HALF, WIDE), BF),
            pltpu.VMEM((CHUNKS, 2, HALF, WIDE), BF),
            pltpu.VMEM((CHUNKS, BLOCK, WIDE), BF),
            pltpu.VMEM((CHUNKS, BLOCK, WIDE), BF),
            pltpu.VMEM((TOK, D), BF),
            pltpu.VMEM((BLOCK, D), BF),
            pltpu.VMEM((TOK, 2 * BLOCK), F32),
            dma((2,)), dma((3,)), dma((3,)), dma((4, 4)), dma((4, 4)), dma((2, 4)), dma((2, 4)),
            dma((4,)), dma((4,)), dma((CHUNKS,)), dma((CHUNKS,)), dma((CHUNKS, 6)), dma((CHUNKS, 6)),
            dma((3,)), dma((3,)), dma((CHUNKS, 4)), dma((CHUNKS, 4)),
        ],
        compiler_params=pltpu.CompilerParams(
            collective_id=1, has_side_effects=True, vmem_limit_bytes=60 * 2**20
        ),
        name="window",
    )(outbox, high, low, mixing, w_up, w_down)


def slots_of(chosen):
    count = chosen.shape[0]
    onehot = (chosen[:, None] == jnp.arange(EXPERTS)[None, :]).astype(BF)
    before = (jnp.arange(count)[:, None] > jnp.arange(count)[None, :]).astype(BF)
    ahead = dot(before, onehot)
    return jnp.sum(ahead * onehot.astype(F32), axis=1).astype(jnp.int32)


def local(
    resid, queries, keys, values, log_decay, attn_gain, moe_gain, experts, combine_weight, w_up, w_down
):
    chosen = experts[0].reshape(-1)
    slot = slots_of(chosen)
    target = chosen * CAP + slot
    in_window = chosen < FLY
    select = ((target[None, :] == jnp.arange(FLY * CAP)[:, None]) & in_window[None, :]).astype(BF)
    select_tok = select.reshape(FLY * CAP, TOK, 2).sum(axis=2).astype(BF)
    high, low, outbox = attention(
        queries[0], keys[0], values[0], resid[0], log_decay[0].T, attn_gain, moe_gain, select_tok
    )
    pairs = select.T.reshape(TOK, 2, FLY * CAP).astype(F32)
    inside = in_window.reshape(TOK, 2)
    first = jnp.where(inside[:, 0:1], pairs[:, 0], pairs[:, 1])
    weighted = (pairs * combine_weight[0][:, :, None]).sum(axis=1)
    mixing = jnp.concatenate([first, weighted], axis=1)
    return window(outbox, high, low, mixing, w_up[0], w_down[0])[None]


def solution(mesh):
    token = P("section", "ctx", None)
    return jax.shard_map(
        local,
        mesh=mesh,
        in_specs=(
            token, token, token, token, token,
            P("section", None), P("section", None),
            token, token,
            P("section", None, "ctx"), token,
        ),
        out_specs=token,
        check_vma=False,
    )
```

```python
import jax
import jax.numpy as jnp
from jax import lax
from jax.experimental import pallas as pl
from jax.experimental.pallas import tpu as pltpu
from jax.sharding import PartitionSpec as P

D = 6144
HEADS = 48
HEAD = 128
TOK = 128
CAP = 16
FLY = 4
SUB = 2
ROWS = SUB * HEAD
MESSAGE = ROWS + 8
BF = jnp.bfloat16
F32 = jnp.float32
HIGH = lax.Precision.HIGHEST


def dot(a, b):
    return jnp.dot(a, b, preferred_element_type=F32)


def dot_t(a, b):
    return lax.dot_general(a, b, (((1,), (1,)), ((), ())), preferred_element_type=F32)


def parts(x):
    high = x.astype(BF)
    return high, (x - high.astype(F32)).astype(BF)


def place():
    me = lax.axis_index("ctx")
    return me // 8, lax.rem(me // 2, 4), lax.rem(me, 2)


def index_of(y, z, c):
    return (y * 4 + z) * 2 + c


def columns(h):
    return pl.ds(pl.multiple_of(h * HEAD, HEAD), HEAD)


BLOCK = 4 * CAP
STEP = 1024
UNITS = 640
CHUNKS = 3
PAIR = 2 * CAP
WIDE = D // CHUNKS
NARROW = 512


def scan_attention(
    where, barrier,
    q_hbm, k_hbm, v_hbm, resid_hbm, rate_ref, attn_gain_ref, moe_gain_ref, experts_ref, combine_ref,
    high_ref, low_ref, outbox_ref, mixing_ref,
    partner_total, partner_state, t_recv, r_recv, chip_prefix, prefix,
    load_sems, small_sems, ps_send_sems, ps_recv_sems, t_send_sems, t_recv_sems,
    r_send_sems, r_recv_sems, p_send_sems, p_recv_sems, f_send_sems, f_recv_sems,
    q_ref, k_ref, v_ref, resid_ref, cum_ref, total_ref, own_state,
    t_send, within, r_send, p_send, f_send, attn_ref, square_ref, select_ref,
):
    y, z, c = where
    loads = [
        pltpu.make_async_copy(a, b, load_sems.at[i])
        for i, (a, b) in enumerate(
            ((k_hbm, k_ref), (v_hbm, v_ref), (q_hbm, q_ref), (resid_hbm, resid_ref))
        )
    ]
    for load in loads:
        load.start()
    partner = index_of(y, z, 1 - c)
    z_peer = [index_of(y, lax.rem(z + d, 4), c) for d in range(4)]
    y_peer = [index_of(lax.rem(y + d, 4), z, c) for d in range(4)]
    rate = rate_ref[...]
    earlier = lax.broadcasted_iota(jnp.int32, (TOK, TOK), 0)
    later = lax.broadcasted_iota(jnp.int32, (TOK, TOK), 1)
    cum_ref[...] = jnp.dot(
        rate, (earlier <= later).astype(F32), precision=HIGH, preferred_element_type=F32
    )
    total_ref[...] = jnp.dot(
        rate, jnp.ones((TOK, TOK), F32), precision=HIGH, preferred_element_type=F32
    )
    copies = []

    def remote(src, dst, send_sem, recv_sem, peer):
        copy = pltpu.make_async_remote_copy(
            src_ref=src, dst_ref=dst, send_sem=send_sem, recv_sem=recv_sem, device_id={"ctx": peer}
        )
        copy.start()
        copies.append(copy)
        return copy

    def tile(i):
        return pl.ds(pl.multiple_of(i * HEAD, HEAD), HEAD)

    def state_of(h):
        row = jnp.exp(total_ref[pl.ds(h, 1), :] - cum_ref[pl.ds(h, 1), :])
        keys = k_ref[:, columns(h)].astype(F32).T * row
        high, low = parts(keys)
        values = v_ref[:, columns(h)]
        return dot(high, values) + dot(low, values)

    def states(half, s):
        def one(n, carry):
            own_state[half, s, tile(n), :] = state_of(half * 24 + s * 8 + n)
            return carry

        lax.fori_loop(0, 8, one, 0, unroll=8)

    loads[0].wait()
    loads[1].wait()
    states(1 - c, 0)
    pl.semaphore_wait(barrier, 15)
    totals = remote(total_ref, partner_total, small_sems.at[0], small_sems.at[1], partner)
    zero_first = c == 0

    def swap(s):
        return remote(
            own_state.at[1 - c, s], partner_state.at[s], ps_send_sems.at[s], ps_recv_sems.at[s], partner
        )

    order = (2, 1, 3, 0)
    t_copies = {}

    def join(s):
        for d in order:
            j = lax.rem(z + d, 4)
            target = t_recv.at[s, 0] if d == 0 else t_send.at[s, d - 1]
            for i in range(SUB):
                h = c * 24 + s * 8 + j * SUB + i
                rows = tile(j * SUB + i)
                mine = total_ref[pl.ds(h, 1), :]
                other = partner_total[pl.ds(h, 1), :]
                keep = jnp.exp(jnp.where(zero_first, other, 0.0))
                take = jnp.exp(jnp.where(zero_first, 0.0, mine))
                target[i * HEAD : (i + 1) * HEAD, :] = (
                    keep * own_state[c, s, rows, :] + take * partner_state[s, rows, :]
                )
                target[ROWS + i : ROWS + i + 1, :] = mine + other
            target[ROWS + SUB :, :] = jnp.zeros((8 - SUB, HEAD), F32)
            if d:
                t_copies[s, d] = remote(
                    target, t_recv.at[s, d], t_send_sems.at[s, d - 1], t_recv_sems.at[s, d - 1], z_peer[d]
                )

    lower = earlier >= later

    def intra(first, last):
        def one(h, carry):
            across = jnp.broadcast_to(cum_ref[pl.ds(h, 1), :], (TOK, TOK))
            weights = jnp.exp(jnp.where(lower, across.T - across, -1e30))
            scores = dot_t(q_ref[:, columns(h)], k_ref[:, columns(h)]) * weights
            high, low = parts(scores)
            values = v_ref[:, columns(h)]
            attn_ref[:, columns(h)] = dot(high, values) + dot(low, values)
            return carry

        lax.fori_loop(first, last, one, 0, unroll=6)

    r_copies = {}

    def row_sum(s):
        for d in (1, 3, 2):
            t_copies[s, d].wait_recv()
        for i in range(SUB):
            rows = slice(i * HEAD, (i + 1) * HEAD)
            label = slice(ROWS + i, ROWS + i + 1)
            state = t_recv[s, z, rows, :]
            within[s, 1, rows, :] = state
            for other in range(1, 4):
                slot = lax.rem(z - other + 4, 4)
                state = state * jnp.exp(t_recv[s, slot, label, :]) + t_recv[s, slot, rows, :]
                if other < 3:
                    within[s, other + 1, rows, :] = state
            r_send[s, rows, :] = state
            r_send[s, label, :] = (
                t_recv[s, 0, label, :] + t_recv[s, 1, label, :]
                + t_recv[s, 2, label, :] + t_recv[s, 3, label, :]
            )
        r_send[s, ROWS + SUB :, :] = jnp.zeros((8 - SUB, HEAD), F32)
        for d in (2, 1, 3):
            r_copies[s, d] = remote(
                r_send.at[s], r_recv.at[s, d], r_send_sems.at[s, d - 1], r_recv_sems.at[s, d - 1], y_peer[d]
            )
        r_recv[s, 0] = r_send[s]

    p_copies = {}

    def chip_prefixes(s):
        for d in (1, 3, 2):
            r_copies[s, d].wait_recv()
        for i in range(SUB):
            rows = slice(i * HEAD, (i + 1) * HEAD)
            label = slice(ROWS + i, ROWS + i + 1)
            state = jnp.zeros((HEAD, HEAD), F32)
            for other in range(3):
                slot = lax.rem(y - other + 4, 4)
                joined = state * jnp.exp(r_recv[s, slot, label, :]) + r_recv[s, slot, rows, :]
                state = jnp.where(other < y, joined, state)
            within[s, 0, rows, :] = state
        for d in order:
            to = lax.rem(z + d, 4)
            target = chip_prefix.at[s, 0] if d == 0 else p_send.at[s, d - 1]
            for i in range(SUB):
                rows = slice(i * HEAD, (i + 1) * HEAD)
                label = slice(ROWS + i, ROWS + i + 1)
                gone = jnp.zeros((1, HEAD), F32)
                for other in range(3):
                    slot = lax.rem(z - other + 4, 4)
                    gone = gone + jnp.where(other < to, t_recv[s, slot, label, :], 0.0)
                inside = within[s, jnp.maximum(to, 1), rows, :]
                target[rows, :] = within[s, 0, rows, :] * jnp.exp(gone) + jnp.where(to > 0, inside, 0.0)
            if d:
                p_copies[s, d] = remote(
                    target, chip_prefix.at[s, d], p_send_sems.at[s, d - 1], p_recv_sems.at[s, d - 1], z_peer[d]
                )

    f_copies = {}

    def finish(s):
        for d in (0, 1, 3, 2):
            if d:
                p_copies[s, d].wait_recv()
            j = lax.rem(z - d + 4, 4)
            for i in range(SUB):
                h = c * 24 + s * 8 + j * SUB + i
                rows = tile(j * SUB + i)
                first_total = jnp.where(
                    zero_first, total_ref[pl.ds(h, 1), :], partner_total[pl.ds(h, 1), :]
                )
                first_state = jnp.where(zero_first, own_state[c, s, rows, :], partner_state[s, rows, :])
                base = chip_prefix[s, d, i * HEAD : (i + 1) * HEAD, :]
                full = base * jnp.exp(first_total) + first_state
                prefix[c, s, rows, :] = jnp.where(zero_first, base, full)
                f_send[s, rows, :] = jnp.where(zero_first, full, base)
        f_copies[s] = remote(f_send.at[s], prefix.at[c, s], f_send_sems.at[s], f_recv_sems.at[s], partner)

    square_ref[...] = jnp.zeros_like(square_ref)

    def tables():
        expert, slot = later // CAP, lax.rem(later, CAP)
        chosen = [
            jnp.broadcast_to(experts_ref[j : j + 1, :].astype(F32), (TOK, TOK)).T for j in range(2)
        ]
        weight = [jnp.broadcast_to(combine_ref[j : j + 1, :], (TOK, TOK)).T for j in range(2)]
        window = later < FLY * CAP
        named = [(one == expert.astype(F32)) & window for one in chosen]
        either = named[0] | named[1]
        ahead = dot((earlier > later).astype(F32).astype(BF), either.astype(F32).astype(BF))
        match = either & (ahead == slot.astype(F32))
        found = match.astype(F32)
        select_ref[...] = found.T[: FLY * CAP, :].astype(BF)
        first = jnp.where(chosen[0] < FLY, named[0].astype(F32), named[1].astype(F32))
        mixing_ref[:TOK, :] = first * found
        mixing_ref[TOK:, :] = jnp.where(named[0], weight[0], weight[1]) * found

    def inter(half, s):
        def one(n, carry):
            h = half * 24 + s * 8 + n
            across = jnp.broadcast_to(cum_ref[pl.ds(h, 1), :], (TOK, TOK)).T
            high, low = parts(prefix[half, s, tile(n), :])
            query = q_ref[:, columns(h)]
            out = attn_ref[:, columns(h)] + jnp.exp(across) * (dot(query, high) + dot(query, low))
            attn_ref[:, columns(h)] = out
            square_ref[...] += out * out
            return carry

        lax.fori_loop(0, 8, one, 0, unroll=8)

    swaps = [swap(0)]
    states(c, 0)
    totals.wait_recv()
    swaps[0].wait_recv()
    join(0)
    for s in (1, 2):
        states(1 - c, s)
        swaps.append(swap(s))
        states(c, s)
        swaps[s].wait_recv()
        join(s)
    loads[2].wait()
    tables()
    intra(0, 12)
    row_sum(0)
    intra(12, 24)
    row_sum(1)
    chip_prefixes(0)
    intra(24, 36)
    row_sum(2)
    chip_prefixes(1)
    intra(36, 48)
    chip_prefixes(2)
    for s in range(3):
        finish(s)
        inter(c, s)
        f_copies[s].wait_recv()
        inter(1 - c, s)
    loads[3].wait()
    scale = lax.rsqrt(jnp.sum(square_ref[...], axis=1, keepdims=True) * (1.0 / D) + 1e-6)
    scale = jnp.broadcast_to(scale, (TOK, HEAD))
    square_ref[...] = jnp.zeros_like(square_ref)

    def residual(h, carry):
        out = resid_ref[:, columns(h)].astype(F32) + attn_ref[:, columns(h)] * scale * attn_gain_ref[:, columns(h)]
        attn_ref[:, columns(h)] = out
        square_ref[...] += out * out
        return carry

    lax.fori_loop(0, HEADS, residual, 0, unroll=6)
    scale_2 = lax.rsqrt(jnp.sum(square_ref[...], axis=1, keepdims=True) * (1.0 / D) + 1e-6)
    scale_2 = jnp.broadcast_to(scale_2, (TOK, HEAD))
    select = select_ref[...]

    def norm(h, carry):
        out = attn_ref[:, columns(h)]
        high, low = parts(out)
        high_ref[:, columns(h)] = high
        low_ref[:, columns(h)] = dot(select, low).astype(BF)
        normed = (out * scale_2 * moe_gain_ref[:, columns(h)]).astype(BF)
        outbox_ref[:, columns(h)] = dot(select, normed).astype(BF)
        return carry

    lax.fori_loop(0, HEADS, norm, 0, unroll=6)
    for copy in copies:
        copy.wait_send()


def expert_window(
    where,
    outbox_ref, high_ref, low_ref, mixing_ref, up_hbm, down_hbm,
    high_in, low_in, mixing_in, sums_ref,
    rows_ref, partner_part, relay_in, near_in, far_in,
    load_sems, y_send, y_recv, core_send, core_recv, z_send, z_recv, hop_send, hop_recv,
    part_send, part_recv, ring_send, ring_recv, next_send, next_recv, sums_send, sums_recv,
    up_ref, down_ref, total_ref, hidden_ref, part_ref, sum_ref, relay_out, final_ref,
):
    y, z, c = where
    section = lax.axis_index("section")
    after = lax.rem(section + 1, 4)
    before = lax.rem(section + 3, 4)
    loads = [
        pltpu.make_async_copy(up_hbm, up_ref, load_sems.at[0]),
        pltpu.make_async_copy(down_hbm, down_ref, load_sems.at[1]),
    ]
    for load in loads:
        load.start()
    partner = index_of(y, z, 1 - c)
    plus, minus = index_of(y, lax.rem(z + 1, 4), c), index_of(y, lax.rem(z + 3, 4), c)
    y_peer = [index_of(lax.rem(y + d, 4), z, c) for d in range(4)]
    sent = []

    def send(src, dst, send_sem, recv_sem, peer, section_to=None):
        target = {"ctx": peer} if section_to is None else {"section": section_to, "ctx": peer}
        copy = pltpu.make_async_remote_copy(
            src_ref=src, dst_ref=dst, send_sem=send_sem, recv_sem=recv_sem, device_id=target
        )
        copy.start()
        sent.append(copy)

    def arrived(dst, recv_sem, peer, section_to=None):
        target = {"ctx": peer} if section_to is None else {"section": section_to, "ctx": peer}
        pltpu.make_async_remote_copy(
            src_ref=dst, dst_ref=dst, send_sem=recv_sem, recv_sem=recv_sem, device_id=target
        ).wait_recv()

    spot = (0, 1, 3, 2)

    def piece(block, core, p):
        row = p // 2 * 4 * BLOCK + block * BLOCK + core * PAIR + p % 2 * CAP
        return rows_ref.at[pl.ds(pl.multiple_of(row, CAP), CAP), :]

    def box(e):
        return pl.ds(pl.multiple_of(e * CAP, CAP), CAP)

    def to_column(d):
        send(
            outbox_ref.at[box(lax.rem(y + d, 4)), :], piece(0, c, spot[d]),
            y_send.at[d - 1], y_recv.at[d - 1], y_peer[d],
        )

    to_column(1)
    to_column(3)
    rows_ref[pl.ds(pl.multiple_of(c * PAIR, CAP), CAP), :] = outbox_ref[box(y), :]

    def spread(p):
        src = piece(0, c, p)
        send(src, piece(1, c, p), z_send.at[0, p], z_recv.at[0, p], plus)
        send(src, piece(2, c, p), z_send.at[1, p], z_recv.at[1, p], minus)
        send(src, src, core_send.at[0, p], core_recv.at[0, p], partner)

    def from_minus(p):
        src = piece(1, c, p)
        arrived(src, z_recv.at[0, p], minus)
        if p % 2 == 0:
            send(src, piece(3, c, p), hop_send.at[p], hop_recv.at[p], plus)
        send(src, src, core_send.at[1, p], core_recv.at[1, p], partner)

    def from_plus(p):
        src = piece(2, c, p)
        arrived(src, z_recv.at[1, p], plus)
        if p % 2 == 1:
            send(src, piece(3, c, p), hop_send.at[p], hop_recv.at[p], minus)
        send(src, src, core_send.at[2, p], core_recv.at[2, p], partner)

    def from_far(p):
        src = piece(3, c, p)
        arrived(src, hop_recv.at[p], plus if p % 2 else minus)
        send(src, src, core_send.at[3, p], core_recv.at[3, p], partner)

    def from_column(d):
        arrived(piece(0, c, spot[d]), y_recv.at[d - 1], y_peer[4 - d])
        spread(spot[d])

    def up(g):
        first, count = g * 4 * BLOCK, 4 * BLOCK
        for block in range(4):
            for p in (2 * g, 2 * g + 1):
                arrived(piece(block, 1 - c, p), core_recv.at[block, p], partner)
        total_ref[...] = jnp.zeros_like(total_ref)

        def one(i, carry):
            at = pl.ds(pl.multiple_of(i * STEP, STEP), STEP)
            total_ref[...] += dot(rows_ref[first : first + count, at], up_ref[at, :])
            return carry

        lax.fori_loop(0, D // STEP, one, 0)
        hidden_ref[first : first + count, :] = jax.nn.gelu(total_ref[...], approximate=True).astype(BF)

    def down(g, q):
        first = g * 4 * BLOCK

        def one(i, carry):
            at = pl.ds(pl.multiple_of(i * NARROW, NARROW), NARROW)
            from_at = pl.ds(pl.multiple_of(q * WIDE + i * NARROW, NARROW), NARROW)
            out = dot(hidden_ref[first : first + 4 * BLOCK, :], down_ref[:, from_at]).astype(BF)
            for block in range(4):
                for core in range(2):
                    row = block * BLOCK + core * PAIR
                    part_ref[g, q, core, block * PAIR : (block + 1) * PAIR, at] = out[row : row + PAIR, :]
            return carry

        lax.fori_loop(0, WIDE // NARROW, one, 0)
        send(
            part_ref.at[g, q, 1 - c], partner_part.at[g, q], part_send.at[g, q], part_recv.at[g, q], partner
        )

    def over_columns(body):
        def one(i, carry):
            body(pl.ds(pl.multiple_of(i * NARROW, NARROW), NARROW))
            return carry

        lax.fori_loop(0, WIDE // NARROW, one, 0)

    def share(g, q, block, i):
        first = block * PAIR + i * CAP
        return sum_ref.at[g, q, first : first + CAP, :]

    def core_sum(g, q):
        arrived(partner_part.at[g, q], part_recv.at[g, q], partner)

        def add(at):
            sum_ref[g, q, :, at] = (
                part_ref[g, q, c, :, at].astype(F32) + partner_part[g, q, :, at].astype(F32)
            ).astype(BF)

        over_columns(add)
        out, back = ring_send.at[g, q], ring_recv.at[g, q]
        send(share(g, q, 3, 0), relay_in.at[g, q, 0], out.at[2], back.at[2], plus)
        send(share(g, q, 3, 1), relay_in.at[g, q, 1], out.at[3], back.at[3], minus)
        send(share(g, q, 2, 1), near_in.at[g, q, 0], out.at[0], back.at[0], plus)
        send(share(g, q, 1, 0), near_in.at[g, q, 1], out.at[1], back.at[1], minus)

    def relay(g, q):
        for side in range(2):
            arrived(relay_in.at[g, q, side], ring_recv.at[g, q, 2 + side], (minus, plus)[side])
            mine = share(g, q, 2 - side, side)

            def add(at, side=side, mine=mine):
                relay_out[g, q, side, :, at] = (
                    mine[:, at].astype(F32) + relay_in[g, q, side, :, at].astype(F32)
                ).astype(BF)

            over_columns(add)
            send(
                relay_out.at[g, q, side], far_in.at[g, q, side],
                ring_send.at[g, q, 4 + side], ring_recv.at[g, q, 4 + side], (plus, minus)[side],
            )

    def final(g, q):
        arrived(near_in.at[g, q, 0], ring_recv.at[g, q, 0], minus)
        arrived(near_in.at[g, q, 1], ring_recv.at[g, q, 1], plus)
        arrived(far_in.at[g, q, 0], ring_recv.at[g, q, 4], minus)
        arrived(far_in.at[g, q, 1], ring_recv.at[g, q, 5], plus)
        for i in range(2):
            mine = share(g, q, 0, i)
            p = 2 * g + i

            def add(at, i=i, p=p, mine=mine):
                final_ref[q, p * CAP : (p + 1) * CAP, at] = (
                    mine[:, at].astype(F32)
                    + near_in[g, q, 1 - i, :, at].astype(F32)
                    + far_in[g, q, i, :, at].astype(F32)
                ).astype(BF)

            over_columns(add)
            d = spot[p]
            send(
                final_ref.at[q, p * CAP : (p + 1) * CAP, :], sums_ref.at[box(y), q * WIDE : (q + 1) * WIDE],
                sums_send.at[q, d], sums_recv.at[q, d], y_peer[(4 - d) % 4], after,
            )

    spread(0)
    send(high_ref, high_in, next_send.at[0], next_recv.at[0], y_peer[0], after)
    send(low_ref, low_in, next_send.at[1], next_recv.at[1], y_peer[0], after)
    send(mixing_ref, mixing_in, next_send.at[2], next_recv.at[2], y_peer[0], after)
    from_column(1)
    to_column(2)
    from_column(3)
    from_minus(0)
    from_plus(0)
    from_column(2)
    from_minus(1)
    from_plus(1)
    from_far(0)
    from_far(1)
    loads[0].wait()
    up(0)
    for p in (2, 3):
        from_minus(p)
        from_plus(p)
    loads[1].wait()
    down(0, 0)
    down(0, 1)
    core_sum(0, 0)
    down(0, 2)
    core_sum(0, 1)
    core_sum(0, 2)
    from_far(2)
    from_far(3)
    up(1)
    for q in range(CHUNKS):
        relay(0, q)
    down(1, 0)
    down(1, 1)
    core_sum(1, 0)
    down(1, 2)
    core_sum(1, 1)
    final(0, 0)
    core_sum(1, 2)
    final(0, 1)
    relay(1, 0)
    final(0, 2)
    relay(1, 1)
    final(1, 0)
    relay(1, 2)
    arrived(high_in, next_recv.at[0], y_peer[0], before)
    arrived(low_in, next_recv.at[1], y_peer[0], before)
    arrived(mixing_in, next_recv.at[2], y_peer[0], before)
    final(1, 1)
    final(1, 2)
    for q in range(CHUNKS):
        for d in range(4):
            arrived(sums_ref.at[0:CAP, q * WIDE : (q + 1) * WIDE], sums_recv.at[q, d], y_peer[d], before)
    for copy in sent:
        copy.wait_send()


def layer_kernel(
    q_hbm, k_hbm, v_hbm, resid_hbm, rate_ref, attn_gain_ref, moe_gain_ref, experts_ref, combine_ref,
    up_hbm, down_hbm,
    high_in, low_in, mixing_in, sums_ref,
    high_ref, low_ref, outbox_ref, mixing_ref,
    partner_total, partner_state, t_recv, r_recv, chip_prefix, prefix,
    rows_ref, partner_part, relay_in, near_in, far_in,
    *sems,
):
    y, z, c = place()
    section = lax.axis_index("section")
    barrier = pltpu.get_barrier_semaphore()
    ring = [index_of(y, lax.rem(z + d, 4), c) for d in (1, 2, 3)]
    column = [index_of(lax.rem(y + d, 4), z, c) for d in range(4)]
    for peer in [index_of(y, z, 1 - c)] + ring + column[1:]:
        pl.semaphore_signal(barrier, inc=1, device_id={"ctx": peer})
    for step in (1, 3):
        for peer in column:
            pl.semaphore_signal(
                barrier, inc=1, device_id={"section": lax.rem(section + step, 4), "ctx": peer}
            )

    def first(*local_refs):
        scan_attention(
            (y, z, c), barrier,
            q_hbm, k_hbm, v_hbm, resid_hbm, rate_ref, attn_gain_ref, moe_gain_ref, experts_ref, combine_ref,
            high_ref, low_ref, outbox_ref, mixing_ref,
            partner_total, partner_state, t_recv, r_recv, chip_prefix, prefix,
            *sems[:12], *local_refs,
        )

    pl.run_scoped(
        first,
        pltpu.VMEM((TOK, D), BF),
        pltpu.VMEM((TOK, D), BF),
        pltpu.VMEM((TOK, D), BF),
        pltpu.VMEM((TOK, D), BF),
        pltpu.VMEM((HEADS, TOK), F32),
        pltpu.VMEM((HEADS, TOK), F32),
        pltpu.VMEM((2, 3, 4 * ROWS, HEAD), F32),
        pltpu.VMEM((3, 3, MESSAGE, HEAD), F32),
        pltpu.VMEM((3, 4, ROWS, HEAD), F32),
        pltpu.VMEM((3, MESSAGE, HEAD), F32),
        pltpu.VMEM((3, 3, ROWS, HEAD), F32),
        pltpu.VMEM((3, 4 * ROWS, HEAD), F32),
        pltpu.VMEM((TOK, D), F32),
        pltpu.VMEM((TOK, HEAD), F32),
        pltpu.VMEM((FLY * CAP, TOK), BF),
    )

    def second(*local_refs):
        expert_window(
            (y, z, c), outbox_ref, high_ref, low_ref, mixing_ref, up_hbm, down_hbm,
            high_in, low_in, mixing_in, sums_ref,
            rows_ref, partner_part, relay_in, near_in, far_in,
            *sems[12:], *local_refs,
        )

    pl.run_scoped(
        second,
        pltpu.VMEM((D, UNITS), BF),
        pltpu.VMEM((UNITS, D), BF),
        pltpu.VMEM((4 * BLOCK, UNITS), F32),
        pltpu.VMEM((8 * BLOCK, UNITS), BF),
        pltpu.VMEM((2, CHUNKS, 2, 4 * PAIR, WIDE), BF),
        pltpu.VMEM((2, CHUNKS, 4 * PAIR, WIDE), BF),
        pltpu.VMEM((2, CHUNKS, 2, CAP, WIDE), BF),
        pltpu.VMEM((CHUNKS, BLOCK, WIDE), BF),
    )


def layer(queries, keys, values, resid, rate, attn_gain, moe_gain, experts, combine, w_up, w_down):
    vmem = pl.BlockSpec(memory_space=pltpu.VMEM)
    hbm = pl.BlockSpec(memory_space=pl.ANY)
    dma = pltpu.SemaphoreType.DMA
    return pl.pallas_call(
        layer_kernel,
        out_shape=(
            jax.ShapeDtypeStruct((TOK, D), BF),
            jax.ShapeDtypeStruct((BLOCK, D), BF),
            jax.ShapeDtypeStruct((2 * TOK, TOK), F32),
            jax.ShapeDtypeStruct((BLOCK, D), BF),
        ),
        in_specs=[hbm] * 4 + [vmem] * 5 + [hbm] * 2,
        out_specs=(hbm, hbm, hbm, hbm),
        scratch_shapes=[
            pltpu.VMEM((TOK, D), BF),
            pltpu.VMEM((BLOCK, D), BF),
            pltpu.VMEM((BLOCK, D), BF),
            pltpu.VMEM((2 * TOK, TOK), F32),
            pltpu.VMEM((HEADS, TOK), F32),
            pltpu.VMEM((3, 4 * ROWS, HEAD), F32),
            pltpu.VMEM((3, 4, MESSAGE, HEAD), F32),
            pltpu.VMEM((3, 4, MESSAGE, HEAD), F32),
            pltpu.VMEM((3, 4, ROWS, HEAD), F32),
            pltpu.VMEM((2, 3, 4 * ROWS, HEAD), F32),
            pltpu.VMEM((8 * BLOCK, D), BF),
            pltpu.VMEM((2, CHUNKS, 4 * PAIR, WIDE), BF),
            pltpu.VMEM((2, CHUNKS, 2, CAP, WIDE), BF),
            pltpu.VMEM((2, CHUNKS, 2, CAP, WIDE), BF),
            pltpu.VMEM((2, CHUNKS, 2, CAP, WIDE), BF),
            dma((4,)), dma((2,)), dma((3,)), dma((3,)), dma((3, 3)), dma((3, 3)),
            dma((3, 3)), dma((3, 3)), dma((3, 3)), dma((3, 3)), dma((3,)), dma((3,)),
            dma((2,)), dma((3,)), dma((3,)), dma((4, 4)), dma((4, 4)), dma((2, 4)), dma((2, 4)),
            dma((4,)), dma((4,)), dma((2, CHUNKS)), dma((2, CHUNKS)),
            dma((2, CHUNKS, 6)), dma((2, CHUNKS, 6)),
            dma((3,)), dma((3,)), dma((CHUNKS, 4)), dma((CHUNKS, 4)),
        ],
        compiler_params=pltpu.CompilerParams(
            collective_id=0, has_side_effects=True, vmem_limit_bytes=60 * 2**20
        ),
        name="layer",
    )(queries, keys, values, resid, rate, attn_gain, moe_gain, experts, combine, w_up, w_down)


def mix_kernel(high_ref, low_ref, mixing_ref, sums_ref, out_ref):
    first = mixing_ref[:TOK, :BLOCK].astype(BF)
    weight_high, weight_low = parts(mixing_ref[TOK:, :BLOCK])
    for i in range(D // 2 // NARROW):
        at = slice(i * NARROW, (i + 1) * NARROW)
        sums = sums_ref[:, at]
        mixed = dot(weight_high, sums) + dot(weight_low, sums)
        out_ref[:, at] = ((high_ref[:, at].astype(F32) + dot(first, low_ref[:, at])) + mixed).astype(BF)


def mix(high, low, mixing, sums):
    wide = D // 2
    return pl.pallas_call(
        mix_kernel,
        out_shape=jax.ShapeDtypeStruct((TOK, D), BF),
        grid=(D // wide,),
        in_specs=[
            pl.BlockSpec((TOK, wide), lambda i: (0, i)),
            pl.BlockSpec((BLOCK, wide), lambda i: (0, i)),
            pl.BlockSpec((2 * TOK, TOK), lambda i: (0, 0)),
            pl.BlockSpec((BLOCK, wide), lambda i: (0, i)),
        ],
        out_specs=pl.BlockSpec((TOK, wide), lambda i: (0, i)),
        compiler_params=pltpu.CompilerParams(vmem_limit_bytes=32 * 2**20),
        name="mix",
    )(high, low, mixing, sums)


def local(
    resid, queries, keys, values, log_decay, attn_gain, moe_gain, experts, combine_weight, w_up, w_down
):
    high, low, mixing, sums = layer(
        queries[0], keys[0], values[0], resid[0], log_decay[0].T, attn_gain, moe_gain,
        experts[0].T, combine_weight[0].T, w_up[0], w_down[0],
    )
    return mix(high, low, mixing, sums)[None]


def solution(mesh):
    token = P("section", "ctx", None)
    return jax.shard_map(
        local,
        mesh=mesh,
        in_specs=(
            token, token, token, token, token,
            P("section", None), P("section", None),
            token, token,
            P("section", None, "ctx"), token,
        ),
        out_specs=token,
        check_vma=False,
    )
```

```python
import jax
import jax.numpy as jnp
from jax import lax
from jax.experimental import pallas as pl
from jax.experimental.pallas import tpu as pltpu
from jax.sharding import PartitionSpec as P

D = 6144
HEADS = 48
HEAD = 128
TOK = 128
CAP = 16
FLY = 4
GROUPS = 3
SUB = 2
BATCH = 4 * SUB
ROWS = SUB * HEAD
MESSAGE = ROWS + 8
BF = jnp.bfloat16
F32 = jnp.float32
HIGH = lax.Precision.HIGHEST


def dot(a, b):
    return jnp.dot(a, b, preferred_element_type=F32)


def dot_t(a, b):
    return lax.dot_general(a, b, (((1,), (1,)), ((), ())), preferred_element_type=F32)


def parts(x):
    high = x.astype(BF)
    return high, (x - high.astype(F32)).astype(BF)


def place():
    me = lax.axis_index("ctx")
    return me // 8, lax.rem(me // 2, 4), lax.rem(me, 2)


def index_of(y, z, c):
    return (y * 4 + z) * 2 + c


def columns(h):
    return pl.ds(pl.multiple_of(h * HEAD, HEAD), HEAD)


BLOCK = 4 * CAP
STEP = 1024
UNITS = 640
CHUNKS = 3
PAIR = 2 * CAP
WIDE = D // CHUNKS
NARROW = 512


def scan_attention(
    where, barrier,
    q_hbm, k_hbm, v_hbm, resid_hbm, rate_ref, attn_gain_ref, moe_gain_ref, experts_ref, combine_ref,
    attn_ref, first_ref, weight_ref, outbox_ref, mixing_ref,
    partner_total, partner_state, t_recv, r_recv, chip_prefix, prefix,
    load_sems, small_sems, ps_send_sems, ps_recv_sems, t_send_sems, t_recv_sems,
    r_send_sems, r_recv_sems, p_send_sems, p_recv_sems, f_send_sems, f_recv_sems,
    q_ref, k_ref, v_ref, resid_ref, cum_ref, total_ref, own_state,
    t_send, within, r_send, p_send, f_send, square_ref, select_ref,
):
    y, z, c = where
    loads = [
        pltpu.make_async_copy(a, b, load_sems.at[i])
        for i, (a, b) in enumerate(
            ((k_hbm, k_ref), (v_hbm, v_ref), (q_hbm, q_ref), (resid_hbm, resid_ref))
        )
    ]
    for load in loads:
        load.start()
    partner = index_of(y, z, 1 - c)
    z_peer = [index_of(y, lax.rem(z + d, 4), c) for d in range(4)]
    y_peer = [index_of(lax.rem(y + d, 4), z, c) for d in range(4)]
    rate = rate_ref[...]
    earlier = lax.broadcasted_iota(jnp.int32, (TOK, TOK), 0)
    later = lax.broadcasted_iota(jnp.int32, (TOK, TOK), 1)
    cum_ref[...] = jnp.dot(
        rate, (earlier <= later).astype(F32), precision=HIGH, preferred_element_type=F32
    )
    total_ref[...] = jnp.dot(
        rate, jnp.ones((TOK, TOK), F32), precision=HIGH, preferred_element_type=F32
    )
    copies = []

    def remote(src, dst, send_sem, recv_sem, peer):
        copy = pltpu.make_async_remote_copy(
            src_ref=src, dst_ref=dst, send_sem=send_sem, recv_sem=recv_sem, device_id={"ctx": peer}
        )
        copy.start()
        copies.append(copy)
        return copy

    def tile(i):
        return pl.ds(pl.multiple_of(i * HEAD, HEAD), HEAD)

    def state_of(h):
        row = jnp.exp(total_ref[pl.ds(h, 1), :] - cum_ref[pl.ds(h, 1), :])
        keys = k_ref[:, columns(h)].astype(F32).T * row
        high, low = parts(keys)
        values = v_ref[:, columns(h)]
        return dot(high, values) + dot(low, values)

    def states(half, s):
        def one(n, carry):
            own_state[half, s, tile(n), :] = state_of(half * 24 + s * BATCH + n)
            return carry

        lax.fori_loop(0, BATCH, one, 0, unroll=BATCH)

    loads[0].wait()
    loads[1].wait()
    states(1 - c, 0)
    pl.semaphore_wait(barrier, 15)
    totals = remote(total_ref, partner_total, small_sems.at[0], small_sems.at[1], partner)
    zero_first = c == 0

    def swap(s):
        return remote(
            own_state.at[1 - c, s], partner_state.at[s], ps_send_sems.at[s], ps_recv_sems.at[s], partner
        )

    order = (2, 1, 3, 0)
    t_copies = {}

    def join(s):
        for d in order:
            j = lax.rem(z + d, 4)
            target = t_recv.at[s, 0] if d == 0 else t_send.at[s, d - 1]
            for i in range(SUB):
                h = c * 24 + s * BATCH + j * SUB + i
                rows = tile(j * SUB + i)
                mine = total_ref[pl.ds(h, 1), :]
                other = partner_total[pl.ds(h, 1), :]
                keep = jnp.exp(jnp.where(zero_first, other, 0.0))
                take = jnp.exp(jnp.where(zero_first, 0.0, mine))
                target[i * HEAD : (i + 1) * HEAD, :] = (
                    keep * own_state[c, s, rows, :] + take * partner_state[s, rows, :]
                )
                target[ROWS + i : ROWS + i + 1, :] = mine + other
            target[ROWS + SUB :, :] = jnp.zeros((8 - SUB, HEAD), F32)
            if d:
                t_copies[s, d] = remote(
                    target, t_recv.at[s, d], t_send_sems.at[s, d - 1], t_recv_sems.at[s, d - 1], z_peer[d]
                )

    lower = earlier >= later

    def intra(first, last):
        def one(h, carry):
            across = jnp.broadcast_to(cum_ref[pl.ds(h, 1), :], (TOK, TOK))
            weights = jnp.exp(jnp.where(lower, across.T - across, -1e30))
            scores = dot_t(q_ref[:, columns(h)], k_ref[:, columns(h)]) * weights
            high, low = parts(scores)
            values = v_ref[:, columns(h)]
            attn_ref[:, columns(h)] = dot(high, values) + dot(low, values)
            return carry

        lax.fori_loop(first, last, one, 0, unroll=6)

    r_copies = {}

    def row_sum(s):
        for d in (1, 3, 2):
            t_copies[s, d].wait_recv()
        for i in range(SUB):
            rows = slice(i * HEAD, (i + 1) * HEAD)
            label = slice(ROWS + i, ROWS + i + 1)
            state = t_recv[s, z, rows, :]
            within[s, 1, rows, :] = state
            for other in range(1, 4):
                slot = lax.rem(z - other + 4, 4)
                state = state * jnp.exp(t_recv[s, slot, label, :]) + t_recv[s, slot, rows, :]
                if other < 3:
                    within[s, other + 1, rows, :] = state
            r_send[s, rows, :] = state
            r_send[s, label, :] = (
                t_recv[s, 0, label, :] + t_recv[s, 1, label, :]
                + t_recv[s, 2, label, :] + t_recv[s, 3, label, :]
            )
        r_send[s, ROWS + SUB :, :] = jnp.zeros((8 - SUB, HEAD), F32)
        for d in (2, 1, 3):
            r_copies[s, d] = remote(
                r_send.at[s], r_recv.at[s, d], r_send_sems.at[s, d - 1], r_recv_sems.at[s, d - 1], y_peer[d]
            )
        r_recv[s, 0] = r_send[s]

    p_copies = {}

    def chip_prefixes(s):
        for d in (1, 3, 2):
            r_copies[s, d].wait_recv()
        for i in range(SUB):
            rows = slice(i * HEAD, (i + 1) * HEAD)
            label = slice(ROWS + i, ROWS + i + 1)
            state = jnp.zeros((HEAD, HEAD), F32)
            for other in range(3):
                slot = lax.rem(y - other + 4, 4)
                joined = state * jnp.exp(r_recv[s, slot, label, :]) + r_recv[s, slot, rows, :]
                state = jnp.where(other < y, joined, state)
            within[s, 0, rows, :] = state
        for d in order:
            to = lax.rem(z + d, 4)
            target = chip_prefix.at[s, 0] if d == 0 else p_send.at[s, d - 1]
            for i in range(SUB):
                rows = slice(i * HEAD, (i + 1) * HEAD)
                label = slice(ROWS + i, ROWS + i + 1)
                gone = jnp.zeros((1, HEAD), F32)
                for other in range(3):
                    slot = lax.rem(z - other + 4, 4)
                    gone = gone + jnp.where(other < to, t_recv[s, slot, label, :], 0.0)
                inside = within[s, jnp.maximum(to, 1), rows, :]
                target[rows, :] = within[s, 0, rows, :] * jnp.exp(gone) + jnp.where(to > 0, inside, 0.0)
            if d:
                p_copies[s, d] = remote(
                    target, chip_prefix.at[s, d], p_send_sems.at[s, d - 1], p_recv_sems.at[s, d - 1], z_peer[d]
                )

    f_copies = {}

    def finish(s):
        for d in (0, 1, 3, 2):
            if d:
                p_copies[s, d].wait_recv()
            j = lax.rem(z - d + 4, 4)
            for i in range(SUB):
                h = c * 24 + s * BATCH + j * SUB + i
                rows = tile(j * SUB + i)
                first_total = jnp.where(
                    zero_first, total_ref[pl.ds(h, 1), :], partner_total[pl.ds(h, 1), :]
                )
                first_state = jnp.where(zero_first, own_state[c, s, rows, :], partner_state[s, rows, :])
                base = chip_prefix[s, d, i * HEAD : (i + 1) * HEAD, :]
                full = base * jnp.exp(first_total) + first_state
                prefix[c, s, rows, :] = jnp.where(zero_first, base, full)
                f_send[s, rows, :] = jnp.where(zero_first, full, base)
        f_copies[s] = remote(f_send.at[s], prefix.at[c, s], f_send_sems.at[s], f_recv_sems.at[s], partner)

    square_ref[...] = jnp.zeros_like(square_ref)

    def tables():
        expert, slot = later // CAP, lax.rem(later, CAP)
        chosen = [
            jnp.broadcast_to(experts_ref[j : j + 1, :].astype(F32), (TOK, TOK)).T for j in range(2)
        ]
        weight = [jnp.broadcast_to(combine_ref[j : j + 1, :], (TOK, TOK)).T for j in range(2)]
        window = later < FLY * CAP
        named = [(one == expert.astype(F32)) & window for one in chosen]
        either = named[0] | named[1]
        ahead = dot((earlier > later).astype(F32).astype(BF), either.astype(F32).astype(BF))
        match = either & (ahead == slot.astype(F32))
        found = match.astype(F32)
        select_ref[...] = found.T[: FLY * CAP, :].astype(BF)
        first = jnp.where(chosen[0] < FLY, named[0].astype(F32), named[1].astype(F32)) * found
        first_ref[...] = first.T[: FLY * CAP, :].astype(BF)
        mixing_ref[...] = found.astype(BF)
        weighted = (jnp.where(named[0], weight[0], weight[1]) * found).T[: FLY * CAP, :]
        weight_ref[...] = jnp.broadcast_to(jnp.sum(weighted, axis=1, keepdims=True), (FLY * CAP, TOK))

    def inter(half, s):
        def one(n, carry):
            h = half * 24 + s * BATCH + n
            across = jnp.broadcast_to(cum_ref[pl.ds(h, 1), :], (TOK, TOK)).T
            high, low = parts(prefix[half, s, tile(n), :])
            query = q_ref[:, columns(h)]
            out = attn_ref[:, columns(h)] + jnp.exp(across) * (dot(query, high) + dot(query, low))
            attn_ref[:, columns(h)] = out
            square_ref[...] += out * out
            return carry

        lax.fori_loop(0, BATCH, one, 0, unroll=BATCH)

    swaps = [swap(0)]
    states(c, 0)
    totals.wait_recv()
    swaps[0].wait_recv()
    join(0)
    for s in range(1, GROUPS):
        states(1 - c, s)
        swaps.append(swap(s))
        states(c, s)
        swaps[s].wait_recv()
        join(s)
    loads[2].wait()
    tables()
    intra(0, 12)
    row_sum(0)
    intra(12, 24)
    row_sum(1)
    chip_prefixes(0)
    intra(24, 36)
    row_sum(2)
    chip_prefixes(1)
    intra(36, 48)
    chip_prefixes(2)
    for s in range(GROUPS):
        finish(s)
        inter(c, s)
        f_copies[s].wait_recv()
        inter(1 - c, s)
    loads[3].wait()
    scale = lax.rsqrt(jnp.sum(square_ref[...], axis=1, keepdims=True) * (1.0 / D) + 1e-6)
    scale = jnp.broadcast_to(scale, (TOK, HEAD))
    square_ref[...] = jnp.zeros_like(square_ref)

    def residual(h, carry):
        out = resid_ref[:, columns(h)].astype(F32) + attn_ref[:, columns(h)] * scale * attn_gain_ref[:, columns(h)]
        attn_ref[:, columns(h)] = out
        square_ref[...] += out * out
        return carry

    lax.fori_loop(0, HEADS, residual, 0, unroll=6)
    scale_2 = lax.rsqrt(jnp.sum(square_ref[...], axis=1, keepdims=True) * (1.0 / D) + 1e-6)
    scale_2 = jnp.broadcast_to(scale_2, (TOK, HEAD))
    select = select_ref[...]

    def norm(h, carry):
        out = attn_ref[:, columns(h)]
        normed = (out * scale_2 * moe_gain_ref[:, columns(h)]).astype(BF)
        outbox_ref[:, columns(h)] = dot(select, normed).astype(BF)
        return carry

    lax.fori_loop(0, HEADS, norm, 0, unroll=6)
    for copy in copies:
        copy.wait_send()


def expert_window(
    where,
    attn_ref, first_ref, weight_ref, outbox_ref, high_ref, low_ref, mixing_ref,
    up_hbm, down_hbm, high_in, low_in, weight_in, mixing_in, sums_ref,
    rows_ref, partner_part, relay_in, near_in, far_in,
    load_sems, y_send, y_recv, core_send, core_recv, z_send, z_recv, hop_send, hop_recv,
    part_send, part_recv, ring_send, ring_recv, next_send, next_recv, sums_send, sums_recv,
    low_send, low_recv, weight_send, weight_recv,
    up_ref, down_ref, total_ref, hidden_ref, part_ref, sum_ref, relay_out, final_ref,
):
    y, z, c = where
    section = lax.axis_index("section")
    after = lax.rem(section + 1, 4)
    before = lax.rem(section + 3, 4)
    loads = [
        pltpu.make_async_copy(up_hbm, up_ref, load_sems.at[0]),
        pltpu.make_async_copy(down_hbm, down_ref, load_sems.at[1]),
    ]
    for load in loads:
        load.start()
    partner = index_of(y, z, 1 - c)
    plus, minus = index_of(y, lax.rem(z + 1, 4), c), index_of(y, lax.rem(z + 3, 4), c)
    y_peer = [index_of(lax.rem(y + d, 4), z, c) for d in range(4)]
    sent = []

    def send(src, dst, send_sem, recv_sem, peer, section_to=None):
        target = {"ctx": peer} if section_to is None else {"section": section_to, "ctx": peer}
        copy = pltpu.make_async_remote_copy(
            src_ref=src, dst_ref=dst, send_sem=send_sem, recv_sem=recv_sem, device_id=target
        )
        copy.start()
        sent.append(copy)

    def arrived(dst, recv_sem, peer, section_to=None):
        target = {"ctx": peer} if section_to is None else {"section": section_to, "ctx": peer}
        pltpu.make_async_remote_copy(
            src_ref=dst, dst_ref=dst, send_sem=recv_sem, recv_sem=recv_sem, device_id=target
        ).wait_recv()

    spot = (0, 1, 3, 2)

    def piece(block, core, p):
        row = p // 2 * 4 * BLOCK + block * BLOCK + core * PAIR + p % 2 * CAP
        return rows_ref.at[pl.ds(pl.multiple_of(row, CAP), CAP), :]

    def box(e):
        return pl.ds(pl.multiple_of(e * CAP, CAP), CAP)

    def to_column(d):
        send(
            outbox_ref.at[box(lax.rem(y + d, 4)), :], piece(0, c, spot[d]),
            y_send.at[d - 1], y_recv.at[d - 1], y_peer[d],
        )

    to_column(1)
    to_column(3)
    rows_ref[pl.ds(pl.multiple_of(c * PAIR, CAP), CAP), :] = outbox_ref[box(y), :]

    def spread(p):
        src = piece(0, c, p)
        send(src, piece(1, c, p), z_send.at[0, p], z_recv.at[0, p], plus)
        send(src, piece(2, c, p), z_send.at[1, p], z_recv.at[1, p], minus)
        send(src, src, core_send.at[0, p], core_recv.at[0, p], partner)

    def from_minus(p):
        src = piece(1, c, p)
        arrived(src, z_recv.at[0, p], minus)
        if p % 2 == 0:
            send(src, piece(3, c, p), hop_send.at[p], hop_recv.at[p], plus)
        send(src, src, core_send.at[1, p], core_recv.at[1, p], partner)

    def from_plus(p):
        src = piece(2, c, p)
        arrived(src, z_recv.at[1, p], plus)
        if p % 2 == 1:
            send(src, piece(3, c, p), hop_send.at[p], hop_recv.at[p], minus)
        send(src, src, core_send.at[2, p], core_recv.at[2, p], partner)

    def from_far(p):
        src = piece(3, c, p)
        arrived(src, hop_recv.at[p], plus if p % 2 else minus)
        send(src, src, core_send.at[3, p], core_recv.at[3, p], partner)

    def from_column(d):
        arrived(piece(0, c, spot[d]), y_recv.at[d - 1], y_peer[4 - d])
        spread(spot[d])

    def up(g):
        first, count = g * 4 * BLOCK, 4 * BLOCK
        for block in range(4):
            for p in (2 * g, 2 * g + 1):
                arrived(piece(block, 1 - c, p), core_recv.at[block, p], partner)
        total_ref[...] = jnp.zeros_like(total_ref)

        def one(i, carry):
            at = pl.ds(pl.multiple_of(i * STEP, STEP), STEP)
            total_ref[...] += dot(rows_ref[first : first + count, at], up_ref[at, :])
            return carry

        lax.fori_loop(0, D // STEP, one, 0)
        hidden_ref[first : first + count, :] = jax.nn.gelu(total_ref[...], approximate=True).astype(BF)

    def down(g, q):
        first = g * 4 * BLOCK

        def one(i, carry):
            at = pl.ds(pl.multiple_of(i * NARROW, NARROW), NARROW)
            from_at = pl.ds(pl.multiple_of(q * WIDE + i * NARROW, NARROW), NARROW)
            out = dot(hidden_ref[first : first + 4 * BLOCK, :], down_ref[:, from_at]).astype(BF)
            for block in range(4):
                for core in range(2):
                    row = block * BLOCK + core * PAIR
                    part_ref[g, q, core, block * PAIR : (block + 1) * PAIR, at] = out[row : row + PAIR, :]
            return carry

        lax.fori_loop(0, WIDE // NARROW, one, 0)
        send(
            part_ref.at[g, q, 1 - c], partner_part.at[g, q], part_send.at[g, q], part_recv.at[g, q], partner
        )

    def over_columns(body):
        def one(i, carry):
            body(pl.ds(pl.multiple_of(i * NARROW, NARROW), NARROW))
            return carry

        lax.fori_loop(0, WIDE // NARROW, one, 0)

    def share(g, q, block, i):
        first = block * PAIR + i * CAP
        return sum_ref.at[g, q, first : first + CAP, :]

    def core_sum(g, q):
        arrived(partner_part.at[g, q], part_recv.at[g, q], partner)

        def add(at):
            sum_ref[g, q, :, at] = (
                part_ref[g, q, c, :, at].astype(F32) + partner_part[g, q, :, at].astype(F32)
            ).astype(BF)

        over_columns(add)
        out, back = ring_send.at[g, q], ring_recv.at[g, q]
        send(share(g, q, 3, 0), relay_in.at[g, q, 0], out.at[2], back.at[2], plus)
        send(share(g, q, 3, 1), relay_in.at[g, q, 1], out.at[3], back.at[3], minus)
        send(share(g, q, 2, 1), near_in.at[g, q, 0], out.at[0], back.at[0], plus)
        send(share(g, q, 1, 0), near_in.at[g, q, 1], out.at[1], back.at[1], minus)

    def relay(g, q):
        for side in range(2):
            arrived(relay_in.at[g, q, side], ring_recv.at[g, q, 2 + side], (minus, plus)[side])
            mine = share(g, q, 2 - side, side)

            def add(at, side=side, mine=mine):
                relay_out[g, q, side, :, at] = (
                    mine[:, at].astype(F32) + relay_in[g, q, side, :, at].astype(F32)
                ).astype(BF)

            over_columns(add)
            send(
                relay_out.at[g, q, side], far_in.at[g, q, side],
                ring_send.at[g, q, 4 + side], ring_recv.at[g, q, 4 + side], (plus, minus)[side],
            )

    def final(g, q):
        arrived(near_in.at[g, q, 0], ring_recv.at[g, q, 0], minus)
        arrived(near_in.at[g, q, 1], ring_recv.at[g, q, 1], plus)
        arrived(far_in.at[g, q, 0], ring_recv.at[g, q, 4], minus)
        arrived(far_in.at[g, q, 1], ring_recv.at[g, q, 5], plus)
        for i in range(2):
            mine = share(g, q, 0, i)
            p = 2 * g + i

            weight = jnp.concatenate([weight_in[p]] * (NARROW // TOK), axis=1)

            def add(n, carry, i=i, p=p, mine=mine, weight=weight):
                at = pl.ds(pl.multiple_of(n * NARROW, NARROW), NARROW)
                low_at = pl.ds(pl.multiple_of(q * WIDE + n * NARROW, NARROW), NARROW)
                total = (
                    mine[:, at].astype(F32)
                    + near_in[g, q, 1 - i, :, at].astype(F32)
                    + far_in[g, q, i, :, at].astype(F32)
                )
                final_ref[q, p * CAP : (p + 1) * CAP, at] = (
                    total * weight + low_in[p, :, low_at].astype(F32)
                ).astype(BF)
                return carry

            lax.fori_loop(0, WIDE // NARROW, add, 0)
            d = spot[p]
            send(
                final_ref.at[q, p * CAP : (p + 1) * CAP, :], sums_ref.at[box(y), q * WIDE : (q + 1) * WIDE],
                sums_send.at[q, d], sums_recv.at[q, d], y_peer[(4 - d) % 4], after,
            )

    spread(0)

    def split(h, carry):
        high, low = parts(attn_ref[:, columns(h)])
        high_ref[:, columns(h)] = high
        low_ref[:, columns(h)] = dot(first_ref[...], low).astype(BF)
        return carry

    lax.fori_loop(0, HEADS, split, 0, unroll=6)
    send(high_ref, high_in, next_send.at[0], next_recv.at[0], y_peer[0], after)
    send(mixing_ref, mixing_in, next_send.at[1], next_recv.at[1], y_peer[0], after)
    from_column(1)
    to_column(2)
    from_column(3)
    from_minus(0)
    from_plus(0)
    from_column(2)
    low_in[0] = low_ref[box(y), :]
    weight_in[0] = weight_ref[box(y), :]
    for d in (1, 3, 2):
        e = box(lax.rem(y + d, 4))
        send(low_ref.at[e, :], low_in.at[spot[d]], low_send.at[d - 1], low_recv.at[d - 1], y_peer[d])
        send(
            weight_ref.at[e, :], weight_in.at[spot[d]],
            weight_send.at[d - 1], weight_recv.at[d - 1], y_peer[d],
        )
    from_minus(1)
    from_plus(1)
    from_far(0)
    from_far(1)
    loads[0].wait()
    up(0)
    for p in (2, 3):
        from_minus(p)
        from_plus(p)
    loads[1].wait()
    down(0, 0)
    down(0, 1)
    core_sum(0, 0)
    down(0, 2)
    core_sum(0, 1)
    core_sum(0, 2)
    from_far(2)
    from_far(3)
    up(1)
    for q in range(CHUNKS):
        relay(0, q)
    for d in (1, 3, 2):
        arrived(low_in.at[spot[d]], low_recv.at[d - 1], y_peer[4 - d])
        arrived(weight_in.at[spot[d]], weight_recv.at[d - 1], y_peer[4 - d])
    down(1, 0)
    down(1, 1)
    core_sum(1, 0)
    down(1, 2)
    core_sum(1, 1)
    final(0, 0)
    core_sum(1, 2)
    final(0, 1)
    relay(1, 0)
    final(0, 2)
    relay(1, 1)
    final(1, 0)
    relay(1, 2)
    arrived(high_in, next_recv.at[0], y_peer[0], before)
    arrived(mixing_in, next_recv.at[1], y_peer[0], before)
    final(1, 1)
    final(1, 2)
    for q in range(CHUNKS):
        for d in range(4):
            arrived(sums_ref.at[0:CAP, q * WIDE : (q + 1) * WIDE], sums_recv.at[q, d], y_peer[d], before)
    for copy in sent:
        copy.wait_send()


def layer_kernel(
    q_hbm, k_hbm, v_hbm, resid_hbm, rate_ref, attn_gain_ref, moe_gain_ref, experts_ref, combine_ref,
    up_hbm, down_hbm,
    high_in, mixing_in, sums_ref,
    attn_ref, first_ref, weight_ref, high_ref, low_ref, outbox_ref, mixing_ref, low_in, weight_in,
    partner_total, partner_state, t_recv, r_recv, chip_prefix, prefix,
    rows_ref, partner_part, relay_in, near_in, far_in,
    *sems,
):
    y, z, c = place()
    section = lax.axis_index("section")
    barrier = pltpu.get_barrier_semaphore()
    ring = [index_of(y, lax.rem(z + d, 4), c) for d in (1, 2, 3)]
    column = [index_of(lax.rem(y + d, 4), z, c) for d in range(4)]
    for peer in [index_of(y, z, 1 - c)] + ring + column[1:]:
        pl.semaphore_signal(barrier, inc=1, device_id={"ctx": peer})
    for step in (1, 3):
        for peer in column:
            pl.semaphore_signal(
                barrier, inc=1, device_id={"section": lax.rem(section + step, 4), "ctx": peer}
            )

    def first(*local_refs):
        scan_attention(
            (y, z, c), barrier,
            q_hbm, k_hbm, v_hbm, resid_hbm, rate_ref, attn_gain_ref, moe_gain_ref, experts_ref, combine_ref,
            attn_ref, first_ref, weight_ref, outbox_ref, mixing_ref,
            partner_total, partner_state, t_recv, r_recv, chip_prefix, prefix,
            *sems[:12], *local_refs,
        )

    pl.run_scoped(
        first,
        pltpu.VMEM((TOK, D), BF),
        pltpu.VMEM((TOK, D), BF),
        pltpu.VMEM((TOK, D), BF),
        pltpu.VMEM((TOK, D), BF),
        pltpu.VMEM((HEADS, TOK), F32),
        pltpu.VMEM((HEADS, TOK), F32),
        pltpu.VMEM((2, GROUPS, 4 * ROWS, HEAD), F32),
        pltpu.VMEM((GROUPS, 3, MESSAGE, HEAD), F32),
        pltpu.VMEM((GROUPS, 4, ROWS, HEAD), F32),
        pltpu.VMEM((GROUPS, MESSAGE, HEAD), F32),
        pltpu.VMEM((GROUPS, 3, ROWS, HEAD), F32),
        pltpu.VMEM((GROUPS, 4 * ROWS, HEAD), F32),
        pltpu.VMEM((TOK, HEAD), F32),
        pltpu.VMEM((FLY * CAP, TOK), BF),
    )

    def second(*local_refs):
        expert_window(
            (y, z, c), attn_ref, first_ref, weight_ref, outbox_ref, high_ref, low_ref, mixing_ref,
            up_hbm, down_hbm, high_in, low_in, weight_in, mixing_in, sums_ref,
            rows_ref, partner_part, relay_in, near_in, far_in,
            *sems[12:], *local_refs,
        )

    pl.run_scoped(
        second,
        pltpu.VMEM((D, UNITS), BF),
        pltpu.VMEM((UNITS, D), BF),
        pltpu.VMEM((4 * BLOCK, UNITS), F32),
        pltpu.VMEM((8 * BLOCK, UNITS), BF),
        pltpu.VMEM((2, CHUNKS, 2, 4 * PAIR, WIDE), BF),
        pltpu.VMEM((2, CHUNKS, 4 * PAIR, WIDE), BF),
        pltpu.VMEM((2, CHUNKS, 2, CAP, WIDE), BF),
        pltpu.VMEM((CHUNKS, BLOCK, WIDE), BF),
    )


def layer(queries, keys, values, resid, rate, attn_gain, moe_gain, experts, combine, w_up, w_down):
    vmem = pl.BlockSpec(memory_space=pltpu.VMEM)
    hbm = pl.BlockSpec(memory_space=pl.ANY)
    dma = pltpu.SemaphoreType.DMA
    return pl.pallas_call(
        layer_kernel,
        out_shape=(
            jax.ShapeDtypeStruct((TOK, D), BF),
            jax.ShapeDtypeStruct((TOK, TOK), BF),
            jax.ShapeDtypeStruct((BLOCK, D), BF),
        ),
        in_specs=[hbm] * 4 + [vmem] * 5 + [hbm] * 2,
        out_specs=(hbm, hbm, hbm),
        scratch_shapes=[
            pltpu.VMEM((TOK, D), F32),
            pltpu.VMEM((BLOCK, TOK), BF),
            pltpu.VMEM((BLOCK, TOK), F32),
            pltpu.VMEM((TOK, D), BF),
            pltpu.VMEM((BLOCK, D), BF),
            pltpu.VMEM((BLOCK, D), BF),
            pltpu.VMEM((TOK, TOK), BF),
            pltpu.VMEM((4, CAP, D), BF),
            pltpu.VMEM((4, CAP, TOK), F32),
            pltpu.VMEM((HEADS, TOK), F32),
            pltpu.VMEM((GROUPS, 4 * ROWS, HEAD), F32),
            pltpu.VMEM((GROUPS, 4, MESSAGE, HEAD), F32),
            pltpu.VMEM((GROUPS, 4, MESSAGE, HEAD), F32),
            pltpu.VMEM((GROUPS, 4, ROWS, HEAD), F32),
            pltpu.VMEM((2, GROUPS, 4 * ROWS, HEAD), F32),
            pltpu.VMEM((8 * BLOCK, D), BF),
            pltpu.VMEM((2, CHUNKS, 4 * PAIR, WIDE), BF),
            pltpu.VMEM((2, CHUNKS, 2, CAP, WIDE), BF),
            pltpu.VMEM((2, CHUNKS, 2, CAP, WIDE), BF),
            pltpu.VMEM((2, CHUNKS, 2, CAP, WIDE), BF),
            dma((4,)), dma((2,)), dma((GROUPS,)), dma((GROUPS,)), dma((GROUPS, 3)), dma((GROUPS, 3)),
            dma((GROUPS, 3)), dma((GROUPS, 3)), dma((GROUPS, 3)), dma((GROUPS, 3)), dma((GROUPS,)),
            dma((GROUPS,)),
            dma((2,)), dma((3,)), dma((3,)), dma((4, 4)), dma((4, 4)), dma((2, 4)), dma((2, 4)),
            dma((4,)), dma((4,)), dma((2, CHUNKS)), dma((2, CHUNKS)),
            dma((2, CHUNKS, 6)), dma((2, CHUNKS, 6)),
            dma((2,)), dma((2,)), dma((CHUNKS, 4)), dma((CHUNKS, 4)),
            dma((3,)), dma((3,)), dma((3,)), dma((3,)),
        ],
        compiler_params=pltpu.CompilerParams(
            collective_id=0, has_side_effects=True, vmem_limit_bytes=60 * 2**20
        ),
        name="layer",
    )(queries, keys, values, resid, rate, attn_gain, moe_gain, experts, combine, w_up, w_down)


def mix_kernel(high_ref, mixing_ref, sums_ref, out_ref):
    mixing = mixing_ref[:, :BLOCK]
    for i in range(D // 2 // NARROW):
        at = slice(i * NARROW, (i + 1) * NARROW)
        out_ref[:, at] = (high_ref[:, at].astype(F32) + dot(mixing, sums_ref[:, at])).astype(BF)


def mix(high, mixing, sums):
    wide = D // 2
    return pl.pallas_call(
        mix_kernel,
        out_shape=jax.ShapeDtypeStruct((TOK, D), BF),
        grid=(D // wide,),
        in_specs=[
            pl.BlockSpec((TOK, wide), lambda i: (0, i)),
            pl.BlockSpec((TOK, TOK), lambda i: (0, 0)),
            pl.BlockSpec((BLOCK, wide), lambda i: (0, i)),
        ],
        out_specs=pl.BlockSpec((TOK, wide), lambda i: (0, i)),
        compiler_params=pltpu.CompilerParams(vmem_limit_bytes=60 * 2**20),
        name="mix",
    )(high, mixing, sums)


def local(
    resid, queries, keys, values, log_decay, attn_gain, moe_gain, experts, combine_weight, w_up, w_down
):
    high, mixing, sums = layer(
        queries[0], keys[0], values[0], resid[0], log_decay[0].T, attn_gain, moe_gain,
        experts[0].T, combine_weight[0].T, w_up[0], w_down[0],
    )
    return mix(high, mixing, sums)[None]


def solution(mesh):
    token = P("section", "ctx", None)
    return jax.shard_map(
        local,
        mesh=mesh,
        in_specs=(
            token, token, token, token, token,
            P("section", None), P("section", None),
            token, token,
            P("section", None, "ctx"), token,
        ),
        out_specs=token,
        check_vma=False,
    )
```

```python
import jax
import jax.numpy as jnp
from jax import lax
from jax.experimental import pallas as pl
from jax.experimental.pallas import tpu as pltpu
from jax.sharding import PartitionSpec as P

D = 6144
HEADS = 48
HEAD = 128
TOK = 128
CAP = 16
FLY = 4
GROUPS = 3
SUB = 2
BATCH = 4 * SUB
ROWS = SUB * HEAD
MESSAGE = ROWS + 8
BF = jnp.bfloat16
F32 = jnp.float32
HIGH = lax.Precision.HIGHEST


def dot(a, b):
    return jnp.dot(a, b, preferred_element_type=F32)


def dot_t(a, b):
    return lax.dot_general(a, b, (((1,), (1,)), ((), ())), preferred_element_type=F32)


def parts(x):
    high = x.astype(BF)
    return high, (x - high.astype(F32)).astype(BF)


def place():
    me = lax.axis_index("ctx")
    return me // 8, lax.rem(me // 2, 4), lax.rem(me, 2)


def index_of(y, z, c):
    return (y * 4 + z) * 2 + c


def columns(h):
    return pl.ds(pl.multiple_of(h * HEAD, HEAD), HEAD)


BLOCK = 4 * CAP
STEP = 1024
UNITS = 640
CHUNKS = 3
PAIR = 2 * CAP
WIDE = D // CHUNKS
NARROW = 512


def scan_attention(
    where, barrier,
    q_hbm, k_hbm, v_hbm, resid_hbm, rate_ref, attn_gain_ref, moe_gain_ref, experts_ref, combine_ref,
    attn_ref, first_ref, weight_ref, outbox_ref, mixing_ref,
    partner_total, partner_state, t_recv, r_recv, chip_prefix, prefix,
    load_sems, small_sems, ps_send_sems, ps_recv_sems, t_send_sems, t_recv_sems,
    r_send_sems, r_recv_sems, p_send_sems, p_recv_sems, f_send_sems, f_recv_sems,
    q_ref, k_ref, v_ref, resid_ref, cum_ref, total_ref, own_state,
    t_send, within, r_send, p_send, f_send, square_ref, select_ref,
):
    y, z, c = where
    loads = [
        pltpu.make_async_copy(a, b, load_sems.at[i])
        for i, (a, b) in enumerate(
            ((k_hbm, k_ref), (v_hbm, v_ref), (q_hbm, q_ref), (resid_hbm, resid_ref))
        )
    ]
    for load in loads:
        load.start()
    partner = index_of(y, z, 1 - c)
    z_peer = [index_of(y, lax.rem(z + d, 4), c) for d in range(4)]
    y_peer = [index_of(lax.rem(y + d, 4), z, c) for d in range(4)]
    rate = rate_ref[...]
    earlier = lax.broadcasted_iota(jnp.int32, (TOK, TOK), 0)
    later = lax.broadcasted_iota(jnp.int32, (TOK, TOK), 1)
    cum_ref[...] = jnp.dot(
        rate, (earlier <= later).astype(F32), precision=HIGH, preferred_element_type=F32
    )
    total_ref[...] = jnp.dot(
        rate, jnp.ones((TOK, TOK), F32), precision=HIGH, preferred_element_type=F32
    )
    copies = []

    def remote(src, dst, send_sem, recv_sem, peer):
        copy = pltpu.make_async_remote_copy(
            src_ref=src, dst_ref=dst, send_sem=send_sem, recv_sem=recv_sem, device_id={"ctx": peer}
        )
        copy.start()
        copies.append(copy)
        return copy

    def tile(i):
        return pl.ds(pl.multiple_of(i * HEAD, HEAD), HEAD)

    def state_of(h):
        row = jnp.exp(total_ref[pl.ds(h, 1), :] - cum_ref[pl.ds(h, 1), :])
        keys = k_ref[:, columns(h)].astype(F32).T * row
        high, low = parts(keys)
        values = v_ref[:, columns(h)]
        return dot(high, values) + dot(low, values)

    def states(half, s):
        def one(n, carry):
            own_state[half, s, tile(n), :] = state_of(half * 24 + s * BATCH + n)
            return carry

        lax.fori_loop(0, BATCH, one, 0, unroll=BATCH)

    loads[0].wait()
    loads[1].wait()
    states(1 - c, 0)
    pl.semaphore_wait(barrier, 15)
    totals = remote(total_ref, partner_total, small_sems.at[0], small_sems.at[1], partner)
    zero_first = c == 0

    def swap(s):
        return remote(
            own_state.at[1 - c, s], partner_state.at[s], ps_send_sems.at[s], ps_recv_sems.at[s], partner
        )

    order = (2, 1, 3, 0)
    t_copies = {}

    def join(s):
        for d in order:
            j = lax.rem(z + d, 4)
            target = t_recv.at[s, 0] if d == 0 else t_send.at[s, d - 1]
            for i in range(SUB):
                h = c * 24 + s * BATCH + j * SUB + i
                rows = tile(j * SUB + i)
                mine = total_ref[pl.ds(h, 1), :]
                other = partner_total[pl.ds(h, 1), :]
                keep = jnp.exp(jnp.where(zero_first, other, 0.0))
                take = jnp.exp(jnp.where(zero_first, 0.0, mine))
                target[i * HEAD : (i + 1) * HEAD, :] = (
                    keep * own_state[c, s, rows, :] + take * partner_state[s, rows, :]
                )
                target[ROWS + i : ROWS + i + 1, :] = mine + other
            target[ROWS + SUB :, :] = jnp.zeros((8 - SUB, HEAD), F32)
            if d:
                t_copies[s, d] = remote(
                    target, t_recv.at[s, d], t_send_sems.at[s, d - 1], t_recv_sems.at[s, d - 1], z_peer[d]
                )

    lower = earlier >= later

    def intra(first, last):
        def one(h, carry):
            across = jnp.broadcast_to(cum_ref[pl.ds(h, 1), :], (TOK, TOK))
            weights = jnp.exp(jnp.where(lower, across.T - across, -1e30))
            scores = dot_t(q_ref[:, columns(h)], k_ref[:, columns(h)]) * weights
            high, low = parts(scores)
            values = v_ref[:, columns(h)]
            attn_ref[:, columns(h)] = dot(high, values) + dot(low, values)
            return carry

        lax.fori_loop(first, last, one, 0, unroll=6)

    r_copies = {}

    def row_sum(s):
        for d in (1, 3, 2):
            t_copies[s, d].wait_recv()
        for i in range(SUB):
            rows = slice(i * HEAD, (i + 1) * HEAD)
            label = slice(ROWS + i, ROWS + i + 1)
            state = t_recv[s, z, rows, :]
            within[s, 1, rows, :] = state
            for other in range(1, 4):
                slot = lax.rem(z - other + 4, 4)
                state = state * jnp.exp(t_recv[s, slot, label, :]) + t_recv[s, slot, rows, :]
                if other < 3:
                    within[s, other + 1, rows, :] = state
            r_send[s, rows, :] = state
            r_send[s, label, :] = (
                t_recv[s, 0, label, :] + t_recv[s, 1, label, :]
                + t_recv[s, 2, label, :] + t_recv[s, 3, label, :]
            )
        r_send[s, ROWS + SUB :, :] = jnp.zeros((8 - SUB, HEAD), F32)
        for d in (2, 1, 3):
            r_copies[s, d] = remote(
                r_send.at[s], r_recv.at[s, d], r_send_sems.at[s, d - 1], r_recv_sems.at[s, d - 1], y_peer[d]
            )
        r_recv[s, 0] = r_send[s]

    p_copies = {}

    def chip_prefixes(s):
        for d in (1, 3, 2):
            r_copies[s, d].wait_recv()
        for i in range(SUB):
            rows = slice(i * HEAD, (i + 1) * HEAD)
            label = slice(ROWS + i, ROWS + i + 1)
            state = jnp.zeros((HEAD, HEAD), F32)
            for other in range(3):
                slot = lax.rem(y - other + 4, 4)
                joined = state * jnp.exp(r_recv[s, slot, label, :]) + r_recv[s, slot, rows, :]
                state = jnp.where(other < y, joined, state)
            within[s, 0, rows, :] = state
        for d in order:
            to = lax.rem(z + d, 4)
            target = chip_prefix.at[s, 0] if d == 0 else p_send.at[s, d - 1]
            for i in range(SUB):
                rows = slice(i * HEAD, (i + 1) * HEAD)
                label = slice(ROWS + i, ROWS + i + 1)
                gone = jnp.zeros((1, HEAD), F32)
                for other in range(3):
                    slot = lax.rem(z - other + 4, 4)
                    gone = gone + jnp.where(other < to, t_recv[s, slot, label, :], 0.0)
                inside = within[s, jnp.maximum(to, 1), rows, :]
                target[rows, :] = within[s, 0, rows, :] * jnp.exp(gone) + jnp.where(to > 0, inside, 0.0)
            if d:
                p_copies[s, d] = remote(
                    target, chip_prefix.at[s, d], p_send_sems.at[s, d - 1], p_recv_sems.at[s, d - 1], z_peer[d]
                )

    f_copies = {}

    def finish(s):
        for d in (0, 1, 3, 2):
            if d:
                p_copies[s, d].wait_recv()
            j = lax.rem(z - d + 4, 4)
            for i in range(SUB):
                h = c * 24 + s * BATCH + j * SUB + i
                rows = tile(j * SUB + i)
                first_total = jnp.where(
                    zero_first, total_ref[pl.ds(h, 1), :], partner_total[pl.ds(h, 1), :]
                )
                first_state = jnp.where(zero_first, own_state[c, s, rows, :], partner_state[s, rows, :])
                base = chip_prefix[s, d, i * HEAD : (i + 1) * HEAD, :]
                full = base * jnp.exp(first_total) + first_state
                prefix[c, s, rows, :] = jnp.where(zero_first, base, full)
                f_send[s, rows, :] = jnp.where(zero_first, full, base)
        f_copies[s] = remote(f_send.at[s], prefix.at[c, s], f_send_sems.at[s], f_recv_sems.at[s], partner)

    square_ref[...] = jnp.zeros_like(square_ref)

    def tables():
        expert, slot = later // CAP, lax.rem(later, CAP)
        chosen = [
            jnp.broadcast_to(experts_ref[j : j + 1, :].astype(F32), (TOK, TOK)).T for j in range(2)
        ]
        weight = [jnp.broadcast_to(combine_ref[j : j + 1, :], (TOK, TOK)).T for j in range(2)]
        window = later < FLY * CAP
        named = [(one == expert.astype(F32)) & window for one in chosen]
        either = named[0] | named[1]
        ahead = dot((earlier > later).astype(F32).astype(BF), either.astype(F32).astype(BF))
        match = either & (ahead == slot.astype(F32))
        found = match.astype(F32)
        select_ref[...] = found.T[: FLY * CAP, :].astype(BF)
        first = jnp.where(chosen[0] < FLY, named[0].astype(F32), named[1].astype(F32)) * found
        first_ref[...] = first.T[: FLY * CAP, :].astype(BF)
        mixing_ref[...] = found.astype(BF)
        weighted = (jnp.where(named[0], weight[0], weight[1]) * found).T[: FLY * CAP, :]
        weight_ref[...] = jnp.broadcast_to(jnp.sum(weighted, axis=1, keepdims=True), (FLY * CAP, TOK))

    def inter(half, s):
        def one(n, carry):
            h = half * 24 + s * BATCH + n
            across = jnp.broadcast_to(cum_ref[pl.ds(h, 1), :], (TOK, TOK)).T
            high, low = parts(prefix[half, s, tile(n), :])
            query = q_ref[:, columns(h)]
            out = attn_ref[:, columns(h)] + jnp.exp(across) * (dot(query, high) + dot(query, low))
            attn_ref[:, columns(h)] = out
            square_ref[...] += out * out
            return carry

        lax.fori_loop(0, BATCH, one, 0, unroll=BATCH)

    swaps = [swap(0)]
    states(c, 0)
    totals.wait_recv()
    swaps[0].wait_recv()
    join(0)
    for s in range(1, GROUPS):
        states(1 - c, s)
        swaps.append(swap(s))
        states(c, s)
        swaps[s].wait_recv()
        join(s)
    loads[2].wait()
    tables()
    intra(0, 12)
    row_sum(0)
    intra(12, 24)
    row_sum(1)
    chip_prefixes(0)
    intra(24, 36)
    row_sum(2)
    chip_prefixes(1)
    intra(36, 48)
    chip_prefixes(2)
    for s in range(GROUPS):
        finish(s)
        inter(c, s)
        f_copies[s].wait_recv()
        inter(1 - c, s)
    loads[3].wait()
    scale = lax.rsqrt(jnp.sum(square_ref[...], axis=1, keepdims=True) * (1.0 / D) + 1e-6)
    scale = jnp.broadcast_to(scale, (TOK, HEAD))
    square_ref[...] = jnp.zeros_like(square_ref)

    def residual(h, carry):
        out = resid_ref[:, columns(h)].astype(F32) + attn_ref[:, columns(h)] * scale * attn_gain_ref[:, columns(h)]
        attn_ref[:, columns(h)] = out
        square_ref[...] += out * out
        return carry

    lax.fori_loop(0, HEADS, residual, 0, unroll=6)
    scale_2 = lax.rsqrt(jnp.sum(square_ref[...], axis=1, keepdims=True) * (1.0 / D) + 1e-6)
    scale_2 = jnp.broadcast_to(scale_2, (TOK, HEAD))
    select = select_ref[...]

    def norm(h, carry):
        out = attn_ref[:, columns(h)]
        normed = (out * scale_2 * moe_gain_ref[:, columns(h)]).astype(BF)
        outbox_ref[:, columns(h)] = dot(select, normed).astype(BF)
        return carry

    lax.fori_loop(0, HEADS, norm, 0, unroll=6)
    for copy in copies:
        copy.wait_send()


def expert_window(
    where,
    attn_ref, first_ref, weight_ref, outbox_ref, high_ref, low_ref, mixing_ref,
    up_hbm, down_hbm, high_in, low_in, weight_in, mixing_in, sums_ref,
    rows_ref, partner_part, relay_in, near_in, far_in,
    load_sems, y_send, y_recv, core_send, core_recv, z_send, z_recv, hop_send, hop_recv,
    part_send, part_recv, ring_send, ring_recv, next_send, next_recv, sums_send, sums_recv,
    low_send, low_recv, weight_send, weight_recv,
    up_ref, down_ref, total_ref, hidden_ref, part_ref, sum_ref, relay_out, final_ref,
):
    y, z, c = where
    section = lax.axis_index("section")
    after = lax.rem(section + 1, 4)
    before = lax.rem(section + 3, 4)
    loads = [
        pltpu.make_async_copy(up_hbm, up_ref, load_sems.at[0]),
        pltpu.make_async_copy(down_hbm, down_ref, load_sems.at[1]),
    ]
    for load in loads:
        load.start()
    partner = index_of(y, z, 1 - c)
    plus, minus = index_of(y, lax.rem(z + 1, 4), c), index_of(y, lax.rem(z + 3, 4), c)
    y_peer = [index_of(lax.rem(y + d, 4), z, c) for d in range(4)]
    sent = []

    def send(src, dst, send_sem, recv_sem, peer, section_to=None):
        target = {"ctx": peer} if section_to is None else {"section": section_to, "ctx": peer}
        copy = pltpu.make_async_remote_copy(
            src_ref=src, dst_ref=dst, send_sem=send_sem, recv_sem=recv_sem, device_id=target
        )
        copy.start()
        sent.append(copy)

    def arrived(dst, recv_sem, peer, section_to=None):
        target = {"ctx": peer} if section_to is None else {"section": section_to, "ctx": peer}
        pltpu.make_async_remote_copy(
            src_ref=dst, dst_ref=dst, send_sem=recv_sem, recv_sem=recv_sem, device_id=target
        ).wait_recv()

    spot = (0, 1, 3, 2)

    def piece(block, core, p):
        row = p // 2 * 4 * BLOCK + block * BLOCK + core * PAIR + p % 2 * CAP
        return rows_ref.at[pl.ds(pl.multiple_of(row, CAP), CAP), :]

    def box(e):
        return pl.ds(pl.multiple_of(e * CAP, CAP), CAP)

    def to_column(d):
        send(
            outbox_ref.at[box(lax.rem(y + d, 4)), :], piece(0, c, spot[d]),
            y_send.at[d - 1], y_recv.at[d - 1], y_peer[d],
        )

    to_column(1)
    to_column(3)
    rows_ref[pl.ds(pl.multiple_of(c * PAIR, CAP), CAP), :] = outbox_ref[box(y), :]

    def spread(p):
        src = piece(0, c, p)
        send(src, piece(1, c, p), z_send.at[0, p], z_recv.at[0, p], plus)
        send(src, piece(2, c, p), z_send.at[1, p], z_recv.at[1, p], minus)
        send(src, src, core_send.at[0, p], core_recv.at[0, p], partner)

    def from_minus(p):
        src = piece(1, c, p)
        arrived(src, z_recv.at[0, p], minus)
        if p % 2 == 0:
            send(src, piece(3, c, p), hop_send.at[p], hop_recv.at[p], plus)
        send(src, src, core_send.at[1, p], core_recv.at[1, p], partner)

    def from_plus(p):
        src = piece(2, c, p)
        arrived(src, z_recv.at[1, p], plus)
        if p % 2 == 1:
            send(src, piece(3, c, p), hop_send.at[p], hop_recv.at[p], minus)
        send(src, src, core_send.at[2, p], core_recv.at[2, p], partner)

    def from_far(p):
        src = piece(3, c, p)
        arrived(src, hop_recv.at[p], plus if p % 2 else minus)
        send(src, src, core_send.at[3, p], core_recv.at[3, p], partner)

    def from_column(d):
        arrived(piece(0, c, spot[d]), y_recv.at[d - 1], y_peer[4 - d])
        spread(spot[d])

    def up(g):
        first, count = g * 4 * BLOCK, 4 * BLOCK
        for block in range(4):
            for p in (2 * g, 2 * g + 1):
                arrived(piece(block, 1 - c, p), core_recv.at[block, p], partner)
        total_ref[...] = jnp.zeros_like(total_ref)

        def one(i, carry):
            at = pl.ds(pl.multiple_of(i * STEP, STEP), STEP)
            total_ref[...] += dot(rows_ref[first : first + count, at], up_ref[at, :])
            return carry

        lax.fori_loop(0, D // STEP, one, 0)
        hidden_ref[first : first + count, :] = jax.nn.gelu(total_ref[...], approximate=True).astype(BF)

    def down(g, q):
        first = g * 4 * BLOCK

        def one(i, carry):
            at = pl.ds(pl.multiple_of(i * NARROW, NARROW), NARROW)
            from_at = pl.ds(pl.multiple_of(q * WIDE + i * NARROW, NARROW), NARROW)
            out = dot(hidden_ref[first : first + 4 * BLOCK, :], down_ref[:, from_at]).astype(BF)
            for block in range(4):
                for core in range(2):
                    row = block * BLOCK + core * PAIR
                    part_ref[g, q, core, block * PAIR : (block + 1) * PAIR, at] = out[row : row + PAIR, :]
            return carry

        lax.fori_loop(0, WIDE // NARROW, one, 0)
        send(
            part_ref.at[g, q, 1 - c], partner_part.at[g, q], part_send.at[g, q], part_recv.at[g, q], partner
        )

    def over_columns(body):
        def one(i, carry):
            body(pl.ds(pl.multiple_of(i * NARROW, NARROW), NARROW))
            return carry

        lax.fori_loop(0, WIDE // NARROW, one, 0)

    def share(g, q, block, i):
        first = block * PAIR + i * CAP
        return sum_ref.at[g, q, first : first + CAP, :]

    def core_add(g, q):
        arrived(partner_part.at[g, q], part_recv.at[g, q], partner)

        def add(at):
            sum_ref[g, q, :, at] = (
                part_ref[g, q, c, :, at].astype(F32) + partner_part[g, q, :, at].astype(F32)
            ).astype(BF)

        over_columns(add)

    def ring_out(g, q):
        out, back = ring_send.at[g, q], ring_recv.at[g, q]
        send(share(g, q, 3, 0), relay_in.at[g, q, 0], out.at[2], back.at[2], plus)
        send(share(g, q, 3, 1), relay_in.at[g, q, 1], out.at[3], back.at[3], minus)
        send(share(g, q, 2, 1), near_in.at[g, q, 0], out.at[0], back.at[0], plus)
        send(share(g, q, 1, 0), near_in.at[g, q, 1], out.at[1], back.at[1], minus)

    def core_sum(g, q):
        core_add(g, q)
        ring_out(g, q)

    def relay(g, q):
        for side in range(2):
            arrived(relay_in.at[g, q, side], ring_recv.at[g, q, 2 + side], (minus, plus)[side])
            mine = share(g, q, 2 - side, side)

            def add(at, side=side, mine=mine):
                relay_out[g, q, side, :, at] = (
                    mine[:, at].astype(F32) + relay_in[g, q, side, :, at].astype(F32)
                ).astype(BF)

            over_columns(add)
            send(
                relay_out.at[g, q, side], far_in.at[g, q, side],
                ring_send.at[g, q, 4 + side], ring_recv.at[g, q, 4 + side], (plus, minus)[side],
            )

    def final(g, q):
        arrived(near_in.at[g, q, 0], ring_recv.at[g, q, 0], minus)
        arrived(near_in.at[g, q, 1], ring_recv.at[g, q, 1], plus)
        arrived(far_in.at[g, q, 0], ring_recv.at[g, q, 4], minus)
        arrived(far_in.at[g, q, 1], ring_recv.at[g, q, 5], plus)
        for i in range(2):
            mine = share(g, q, 0, i)
            p = 2 * g + i

            weight = jnp.concatenate([weight_in[p]] * (NARROW // TOK), axis=1)

            def add(n, carry, i=i, p=p, mine=mine, weight=weight):
                at = pl.ds(pl.multiple_of(n * NARROW, NARROW), NARROW)
                low_at = pl.ds(pl.multiple_of(q * WIDE + n * NARROW, NARROW), NARROW)
                total = (
                    mine[:, at].astype(F32)
                    + near_in[g, q, 1 - i, :, at].astype(F32)
                    + far_in[g, q, i, :, at].astype(F32)
                )
                final_ref[q, p * CAP : (p + 1) * CAP, at] = (
                    total * weight + low_in[p, :, low_at].astype(F32)
                ).astype(BF)
                return carry

            lax.fori_loop(0, WIDE // NARROW, add, 0)
            d = spot[p]
            send(
                final_ref.at[q, p * CAP : (p + 1) * CAP, :], sums_ref.at[box(y), q * WIDE : (q + 1) * WIDE],
                sums_send.at[q, d], sums_recv.at[q, d], y_peer[(4 - d) % 4], after,
            )

    spread(0)

    def split(h, carry):
        high, low = parts(attn_ref[:, columns(h)])
        high_ref[:, columns(h)] = high
        low_ref[:, columns(h)] = dot(first_ref[...], low).astype(BF)
        return carry

    lax.fori_loop(0, HEADS, split, 0, unroll=6)
    send(high_ref, high_in, next_send.at[0], next_recv.at[0], y_peer[0], after)
    send(mixing_ref, mixing_in, next_send.at[1], next_recv.at[1], y_peer[0], after)
    from_column(1)
    to_column(2)
    from_minus(0)
    from_plus(0)
    from_minus(1)
    from_plus(1)
    from_column(3)
    low_in[0] = low_ref[box(y), :]
    weight_in[0] = weight_ref[box(y), :]
    for d in (1, 3, 2):
        e = box(lax.rem(y + d, 4))
        send(low_ref.at[e, :], low_in.at[spot[d]], low_send.at[d - 1], low_recv.at[d - 1], y_peer[d])
        send(
            weight_ref.at[e, :], weight_in.at[spot[d]],
            weight_send.at[d - 1], weight_recv.at[d - 1], y_peer[d],
        )
    from_far(0)
    from_far(1)
    from_column(2)
    loads[0].wait()
    up(0)
    for p in (2, 3):
        from_minus(p)
        from_plus(p)
    loads[1].wait()
    down(0, 0)
    down(0, 1)
    core_add(0, 0)
    down(0, 2)
    core_add(0, 1)
    core_add(0, 2)
    from_far(2)
    ring_out(0, 0)
    from_far(3)
    ring_out(0, 1)
    ring_out(0, 2)
    up(1)
    for q in range(CHUNKS):
        relay(0, q)
    for d in (1, 3, 2):
        arrived(low_in.at[spot[d]], low_recv.at[d - 1], y_peer[4 - d])
        arrived(weight_in.at[spot[d]], weight_recv.at[d - 1], y_peer[4 - d])
    down(1, 0)
    down(1, 1)
    core_sum(1, 0)
    down(1, 2)
    final(0, 0)
    final(0, 1)
    core_add(1, 1)
    relay(1, 0)
    ring_out(1, 1)
    final(0, 2)
    core_add(1, 2)
    relay(1, 1)
    ring_out(1, 2)
    final(1, 0)
    relay(1, 2)
    final(1, 1)
    final(1, 2)
    arrived(high_in, next_recv.at[0], y_peer[0], before)
    arrived(mixing_in, next_recv.at[1], y_peer[0], before)
    for q in range(CHUNKS):
        for d in range(4):
            arrived(sums_ref.at[0:CAP, q * WIDE : (q + 1) * WIDE], sums_recv.at[q, d], y_peer[d], before)
    for copy in sent:
        copy.wait_send()


def layer_kernel(
    q_hbm, k_hbm, v_hbm, resid_hbm, rate_ref, attn_gain_ref, moe_gain_ref, experts_ref, combine_ref,
    up_hbm, down_hbm,
    high_in, mixing_in, sums_ref,
    attn_ref, first_ref, weight_ref, high_ref, low_ref, outbox_ref, mixing_ref, low_in, weight_in,
    partner_total, partner_state, t_recv, r_recv, chip_prefix, prefix,
    rows_ref, partner_part, relay_in, near_in, far_in,
    *sems,
):
    y, z, c = place()
    section = lax.axis_index("section")
    barrier = pltpu.get_barrier_semaphore()
    ring = [index_of(y, lax.rem(z + d, 4), c) for d in (1, 2, 3)]
    column = [index_of(lax.rem(y + d, 4), z, c) for d in range(4)]
    for peer in [index_of(y, z, 1 - c)] + ring + column[1:]:
        pl.semaphore_signal(barrier, inc=1, device_id={"ctx": peer})
    for step in (1, 3):
        for peer in column:
            pl.semaphore_signal(
                barrier, inc=1, device_id={"section": lax.rem(section + step, 4), "ctx": peer}
            )

    def first(*local_refs):
        scan_attention(
            (y, z, c), barrier,
            q_hbm, k_hbm, v_hbm, resid_hbm, rate_ref, attn_gain_ref, moe_gain_ref, experts_ref, combine_ref,
            attn_ref, first_ref, weight_ref, outbox_ref, mixing_ref,
            partner_total, partner_state, t_recv, r_recv, chip_prefix, prefix,
            *sems[:12], *local_refs,
        )

    pl.run_scoped(
        first,
        pltpu.VMEM((TOK, D), BF),
        pltpu.VMEM((TOK, D), BF),
        pltpu.VMEM((TOK, D), BF),
        pltpu.VMEM((TOK, D), BF),
        pltpu.VMEM((HEADS, TOK), F32),
        pltpu.VMEM((HEADS, TOK), F32),
        pltpu.VMEM((2, GROUPS, 4 * ROWS, HEAD), F32),
        pltpu.VMEM((GROUPS, 3, MESSAGE, HEAD), F32),
        pltpu.VMEM((GROUPS, 4, ROWS, HEAD), F32),
        pltpu.VMEM((GROUPS, MESSAGE, HEAD), F32),
        pltpu.VMEM((GROUPS, 3, ROWS, HEAD), F32),
        pltpu.VMEM((GROUPS, 4 * ROWS, HEAD), F32),
        pltpu.VMEM((TOK, HEAD), F32),
        pltpu.VMEM((FLY * CAP, TOK), BF),
    )

    def second(*local_refs):
        expert_window(
            (y, z, c), attn_ref, first_ref, weight_ref, outbox_ref, high_ref, low_ref, mixing_ref,
            up_hbm, down_hbm, high_in, low_in, weight_in, mixing_in, sums_ref,
            rows_ref, partner_part, relay_in, near_in, far_in,
            *sems[12:], *local_refs,
        )

    pl.run_scoped(
        second,
        pltpu.VMEM((D, UNITS), BF),
        pltpu.VMEM((UNITS, D), BF),
        pltpu.VMEM((4 * BLOCK, UNITS), F32),
        pltpu.VMEM((8 * BLOCK, UNITS), BF),
        pltpu.VMEM((2, CHUNKS, 2, 4 * PAIR, WIDE), BF),
        pltpu.VMEM((2, CHUNKS, 4 * PAIR, WIDE), BF),
        pltpu.VMEM((2, CHUNKS, 2, CAP, WIDE), BF),
        pltpu.VMEM((CHUNKS, BLOCK, WIDE), BF),
    )


def layer(queries, keys, values, resid, rate, attn_gain, moe_gain, experts, combine, w_up, w_down):
    vmem = pl.BlockSpec(memory_space=pltpu.VMEM)
    hbm = pl.BlockSpec(memory_space=pl.ANY)
    dma = pltpu.SemaphoreType.DMA
    return pl.pallas_call(
        layer_kernel,
        out_shape=(
            jax.ShapeDtypeStruct((TOK, D), BF),
            jax.ShapeDtypeStruct((TOK, TOK), BF),
            jax.ShapeDtypeStruct((BLOCK, D), BF),
        ),
        in_specs=[hbm] * 4 + [vmem] * 5 + [hbm] * 2,
        out_specs=(hbm, hbm, hbm),
        scratch_shapes=[
            pltpu.VMEM((TOK, D), F32),
            pltpu.VMEM((BLOCK, TOK), BF),
            pltpu.VMEM((BLOCK, TOK), F32),
            pltpu.VMEM((TOK, D), BF),
            pltpu.VMEM((BLOCK, D), BF),
            pltpu.VMEM((BLOCK, D), BF),
            pltpu.VMEM((TOK, TOK), BF),
            pltpu.VMEM((4, CAP, D), BF),
            pltpu.VMEM((4, CAP, TOK), F32),
            pltpu.VMEM((HEADS, TOK), F32),
            pltpu.VMEM((GROUPS, 4 * ROWS, HEAD), F32),
            pltpu.VMEM((GROUPS, 4, MESSAGE, HEAD), F32),
            pltpu.VMEM((GROUPS, 4, MESSAGE, HEAD), F32),
            pltpu.VMEM((GROUPS, 4, ROWS, HEAD), F32),
            pltpu.VMEM((2, GROUPS, 4 * ROWS, HEAD), F32),
            pltpu.VMEM((8 * BLOCK, D), BF),
            pltpu.VMEM((2, CHUNKS, 4 * PAIR, WIDE), BF),
            pltpu.VMEM((2, CHUNKS, 2, CAP, WIDE), BF),
            pltpu.VMEM((2, CHUNKS, 2, CAP, WIDE), BF),
            pltpu.VMEM((2, CHUNKS, 2, CAP, WIDE), BF),
            dma((4,)), dma((2,)), dma((GROUPS,)), dma((GROUPS,)), dma((GROUPS, 3)), dma((GROUPS, 3)),
            dma((GROUPS, 3)), dma((GROUPS, 3)), dma((GROUPS, 3)), dma((GROUPS, 3)), dma((GROUPS,)),
            dma((GROUPS,)),
            dma((2,)), dma((3,)), dma((3,)), dma((4, 4)), dma((4, 4)), dma((2, 4)), dma((2, 4)),
            dma((4,)), dma((4,)), dma((2, CHUNKS)), dma((2, CHUNKS)),
            dma((2, CHUNKS, 6)), dma((2, CHUNKS, 6)),
            dma((2,)), dma((2,)), dma((CHUNKS, 4)), dma((CHUNKS, 4)),
            dma((3,)), dma((3,)), dma((3,)), dma((3,)),
        ],
        compiler_params=pltpu.CompilerParams(
            collective_id=0, has_side_effects=True, vmem_limit_bytes=60 * 2**20
        ),
        name="layer",
    )(queries, keys, values, resid, rate, attn_gain, moe_gain, experts, combine, w_up, w_down)


def mix_kernel(high_ref, mixing_ref, sums_ref, out_ref):
    mixing = mixing_ref[:, :BLOCK]
    for i in range(D // 2 // NARROW):
        at = slice(i * NARROW, (i + 1) * NARROW)
        out_ref[:, at] = (high_ref[:, at].astype(F32) + dot(mixing, sums_ref[:, at])).astype(BF)


def mix(high, mixing, sums):
    wide = D // 2
    return pl.pallas_call(
        mix_kernel,
        out_shape=jax.ShapeDtypeStruct((TOK, D), BF),
        grid=(D // wide,),
        in_specs=[
            pl.BlockSpec((TOK, wide), lambda i: (0, i)),
            pl.BlockSpec((TOK, TOK), lambda i: (0, 0)),
            pl.BlockSpec((BLOCK, wide), lambda i: (0, i)),
        ],
        out_specs=pl.BlockSpec((TOK, wide), lambda i: (0, i)),
        compiler_params=pltpu.CompilerParams(vmem_limit_bytes=60 * 2**20),
        name="mix",
    )(high, mixing, sums)


def local(
    resid, queries, keys, values, log_decay, attn_gain, moe_gain, experts, combine_weight, w_up, w_down
):
    high, mixing, sums = layer(
        queries[0], keys[0], values[0], resid[0], log_decay[0].T, attn_gain, moe_gain,
        experts[0].T, combine_weight[0].T, w_up[0], w_down[0],
    )
    return mix(high, mixing, sums)[None]


def solution(mesh):
    token = P("section", "ctx", None)
    return jax.shard_map(
        local,
        mesh=mesh,
        in_specs=(
            token, token, token, token, token,
            P("section", None), P("section", None),
            token, token,
            P("section", None, "ctx"), token,
        ),
        out_specs=token,
        check_vma=False,
    )
```

```python
import jax
import jax.numpy as jnp
from jax import lax
from jax.experimental import pallas as pl
from jax.experimental.pallas import tpu as pltpu
from jax.sharding import PartitionSpec as P

D = 6144
HEADS = 48
HEAD = 128
TOK = 128
CAP = 16
FLY = 4
GROUPS = 3
SUB = 2
BATCH = 4 * SUB
ROWS = SUB * HEAD
MESSAGE = ROWS + 8
BF = jnp.bfloat16
F32 = jnp.float32
HIGH = lax.Precision.HIGHEST


def dot(a, b):
    return jnp.dot(a, b, preferred_element_type=F32)


def dot_t(a, b):
    return lax.dot_general(a, b, (((1,), (1,)), ((), ())), preferred_element_type=F32)


def parts(x):
    high = x.astype(BF)
    return high, (x - high.astype(F32)).astype(BF)


def place():
    me = lax.axis_index("ctx")
    return me // 8, lax.rem(me // 2, 4), lax.rem(me, 2)


def index_of(y, z, c):
    return (y * 4 + z) * 2 + c


def columns(h):
    return pl.ds(pl.multiple_of(h * HEAD, HEAD), HEAD)


BLOCK = 4 * CAP
STEP = 1024
UNITS = 640
CHUNKS = 3
PAIR = 2 * CAP
WIDE = D // CHUNKS
NARROW = 512


def scan_attention(
    where, barrier,
    q_hbm, k_hbm, v_hbm, resid_hbm, rate_ref, attn_gain_ref, moe_gain_ref, experts_ref, combine_ref,
    attn_ref, first_ref, weight_ref, outbox_ref, mixing_ref,
    partner_total, partner_state, t_recv, r_recv, chip_prefix, prefix,
    load_sems, small_sems, ps_send_sems, ps_recv_sems, t_send_sems, t_recv_sems,
    r_send_sems, r_recv_sems, p_send_sems, p_recv_sems, f_send_sems, f_recv_sems,
    q_ref, k_ref, v_ref, resid_ref, cum_ref, total_ref, own_state,
    t_send, within, r_send, p_send, f_send, square_ref, select_ref,
):
    y, z, c = where
    loads = [
        pltpu.make_async_copy(a, b, load_sems.at[i])
        for i, (a, b) in enumerate(
            ((k_hbm, k_ref), (v_hbm, v_ref), (q_hbm, q_ref), (resid_hbm, resid_ref))
        )
    ]
    loads[0].start()
    loads[1].start()
    partner = index_of(y, z, 1 - c)
    z_peer = [index_of(y, lax.rem(z + d, 4), c) for d in range(4)]
    y_peer = [index_of(lax.rem(y + d, 4), z, c) for d in range(4)]
    rate = rate_ref[...]
    earlier = lax.broadcasted_iota(jnp.int32, (TOK, TOK), 0)
    later = lax.broadcasted_iota(jnp.int32, (TOK, TOK), 1)
    cum_ref[...] = jnp.dot(
        rate, (earlier <= later).astype(F32), precision=HIGH, preferred_element_type=F32
    )
    total_ref[...] = jnp.dot(
        rate, jnp.ones((TOK, TOK), F32), precision=HIGH, preferred_element_type=F32
    )
    copies = []

    def remote(src, dst, send_sem, recv_sem, peer):
        copy = pltpu.make_async_remote_copy(
            src_ref=src, dst_ref=dst, send_sem=send_sem, recv_sem=recv_sem, device_id={"ctx": peer}
        )
        copy.start()
        copies.append(copy)
        return copy

    def tile(i):
        return pl.ds(pl.multiple_of(i * HEAD, HEAD), HEAD)

    def state_of(h):
        row = jnp.exp(total_ref[pl.ds(h, 1), :] - cum_ref[pl.ds(h, 1), :])
        keys = k_ref[:, columns(h)].astype(F32).T * row
        high, low = parts(keys)
        values = v_ref[:, columns(h)]
        return dot(high, values) + dot(low, values)

    def states(half, s):
        def one(n, carry):
            own_state[half, s, tile(n), :] = state_of(half * 24 + s * BATCH + n)
            return carry

        lax.fori_loop(0, BATCH, one, 0, unroll=BATCH)

    loads[0].wait()
    loads[1].wait()
    loads[2].start()
    loads[3].start()
    states(1 - c, 0)
    pl.semaphore_wait(barrier, 15)
    totals = remote(total_ref, partner_total, small_sems.at[0], small_sems.at[1], partner)
    zero_first = c == 0

    def swap(s):
        return remote(
            own_state.at[1 - c, s], partner_state.at[s], ps_send_sems.at[s], ps_recv_sems.at[s], partner
        )

    order = (2, 1, 3, 0)
    t_copies = {}

    def join(s):
        for d in order:
            j = lax.rem(z + d, 4)
            target = t_recv.at[s, 0] if d == 0 else t_send.at[s, d - 1]
            for i in range(SUB):
                h = c * 24 + s * BATCH + j * SUB + i
                rows = tile(j * SUB + i)
                mine = total_ref[pl.ds(h, 1), :]
                other = partner_total[pl.ds(h, 1), :]
                keep = jnp.exp(jnp.where(zero_first, other, 0.0))
                take = jnp.exp(jnp.where(zero_first, 0.0, mine))
                target[i * HEAD : (i + 1) * HEAD, :] = (
                    keep * own_state[c, s, rows, :] + take * partner_state[s, rows, :]
                )
                target[ROWS + i : ROWS + i + 1, :] = mine + other
            target[ROWS + SUB :, :] = jnp.zeros((8 - SUB, HEAD), F32)
            if d:
                t_copies[s, d] = remote(
                    target, t_recv.at[s, d], t_send_sems.at[s, d - 1], t_recv_sems.at[s, d - 1], z_peer[d]
                )

    lower = earlier >= later

    def intra(first, last):
        def one(h, carry):
            across = jnp.broadcast_to(cum_ref[pl.ds(h, 1), :], (TOK, TOK))
            weights = jnp.exp(jnp.where(lower, across.T - across, -1e30))
            scores = dot_t(q_ref[:, columns(h)], k_ref[:, columns(h)]) * weights
            high, low = parts(scores)
            values = v_ref[:, columns(h)]
            attn_ref[:, columns(h)] = dot(high, values) + dot(low, values)
            return carry

        lax.fori_loop(first, last, one, 0, unroll=6)

    r_copies = {}

    def row_sum(s):
        for d in (1, 3, 2):
            t_copies[s, d].wait_recv()
        for i in range(SUB):
            rows = slice(i * HEAD, (i + 1) * HEAD)
            label = slice(ROWS + i, ROWS + i + 1)
            state = t_recv[s, z, rows, :]
            within[s, 1, rows, :] = state
            for other in range(1, 4):
                slot = lax.rem(z - other + 4, 4)
                state = state * jnp.exp(t_recv[s, slot, label, :]) + t_recv[s, slot, rows, :]
                if other < 3:
                    within[s, other + 1, rows, :] = state
            r_send[s, rows, :] = state
            r_send[s, label, :] = (
                t_recv[s, 0, label, :] + t_recv[s, 1, label, :]
                + t_recv[s, 2, label, :] + t_recv[s, 3, label, :]
            )
        r_send[s, ROWS + SUB :, :] = jnp.zeros((8 - SUB, HEAD), F32)
        for d in (2, 1, 3):
            r_copies[s, d] = remote(
                r_send.at[s], r_recv.at[s, d], r_send_sems.at[s, d - 1], r_recv_sems.at[s, d - 1], y_peer[d]
            )
        r_recv[s, 0] = r_send[s]

    p_copies = {}

    def chip_prefixes(s):
        for d in (1, 3, 2):
            r_copies[s, d].wait_recv()
        for i in range(SUB):
            rows = slice(i * HEAD, (i + 1) * HEAD)
            label = slice(ROWS + i, ROWS + i + 1)
            state = jnp.zeros((HEAD, HEAD), F32)
            for other in range(3):
                slot = lax.rem(y - other + 4, 4)
                joined = state * jnp.exp(r_recv[s, slot, label, :]) + r_recv[s, slot, rows, :]
                state = jnp.where(other < y, joined, state)
            within[s, 0, rows, :] = state
        for d in order:
            to = lax.rem(z + d, 4)
            target = chip_prefix.at[s, 0] if d == 0 else p_send.at[s, d - 1]
            for i in range(SUB):
                rows = slice(i * HEAD, (i + 1) * HEAD)
                label = slice(ROWS + i, ROWS + i + 1)
                gone = jnp.zeros((1, HEAD), F32)
                for other in range(3):
                    slot = lax.rem(z - other + 4, 4)
                    gone = gone + jnp.where(other < to, t_recv[s, slot, label, :], 0.0)
                inside = within[s, jnp.maximum(to, 1), rows, :]
                target[rows, :] = within[s, 0, rows, :] * jnp.exp(gone) + jnp.where(to > 0, inside, 0.0)
            if d:
                p_copies[s, d] = remote(
                    target, chip_prefix.at[s, d], p_send_sems.at[s, d - 1], p_recv_sems.at[s, d - 1], z_peer[d]
                )

    f_copies = {}

    def finish(s):
        for d in (0, 1, 3, 2):
            if d:
                p_copies[s, d].wait_recv()
            j = lax.rem(z - d + 4, 4)
            for i in range(SUB):
                h = c * 24 + s * BATCH + j * SUB + i
                rows = tile(j * SUB + i)
                first_total = jnp.where(
                    zero_first, total_ref[pl.ds(h, 1), :], partner_total[pl.ds(h, 1), :]
                )
                first_state = jnp.where(zero_first, own_state[c, s, rows, :], partner_state[s, rows, :])
                base = chip_prefix[s, d, i * HEAD : (i + 1) * HEAD, :]
                full = base * jnp.exp(first_total) + first_state
                prefix[c, s, rows, :] = jnp.where(zero_first, base, full)
                f_send[s, rows, :] = jnp.where(zero_first, full, base)
        f_copies[s] = remote(f_send.at[s], prefix.at[c, s], f_send_sems.at[s], f_recv_sems.at[s], partner)

    square_ref[...] = jnp.zeros_like(square_ref)

    def tables():
        expert, slot = later // CAP, lax.rem(later, CAP)
        chosen = [
            jnp.broadcast_to(experts_ref[j : j + 1, :].astype(F32), (TOK, TOK)).T for j in range(2)
        ]
        weight = [jnp.broadcast_to(combine_ref[j : j + 1, :], (TOK, TOK)).T for j in range(2)]
        window = later < FLY * CAP
        named = [(one == expert.astype(F32)) & window for one in chosen]
        either = named[0] | named[1]
        ahead = dot((earlier > later).astype(F32).astype(BF), either.astype(F32).astype(BF))
        match = either & (ahead == slot.astype(F32))
        found = match.astype(F32)
        select_ref[...] = found.T[: FLY * CAP, :].astype(BF)
        first = jnp.where(chosen[0] < FLY, named[0].astype(F32), named[1].astype(F32)) * found
        first_ref[...] = first.T[: FLY * CAP, :].astype(BF)
        mixing_ref[...] = found.astype(BF)
        weighted = (jnp.where(named[0], weight[0], weight[1]) * found).T[: FLY * CAP, :]
        weight_ref[...] = jnp.broadcast_to(jnp.sum(weighted, axis=1, keepdims=True), (FLY * CAP, TOK))

    def inter(half, s):
        def one(n, carry):
            h = half * 24 + s * BATCH + n
            across = jnp.broadcast_to(cum_ref[pl.ds(h, 1), :], (TOK, TOK)).T
            high, low = parts(prefix[half, s, tile(n), :])
            query = q_ref[:, columns(h)]
            out = attn_ref[:, columns(h)] + jnp.exp(across) * (dot(query, high) + dot(query, low))
            attn_ref[:, columns(h)] = out
            square_ref[...] += out * out
            return carry

        lax.fori_loop(0, BATCH, one, 0, unroll=BATCH)

    swaps = [swap(0)]
    states(c, 0)
    totals.wait_recv()
    swaps[0].wait_recv()
    join(0)
    for s in range(1, GROUPS):
        states(1 - c, s)
        swaps.append(swap(s))
        states(c, s)
        swaps[s].wait_recv()
        join(s)
    loads[2].wait()
    tables()
    intra(0, 12)
    row_sum(0)
    intra(12, 24)
    row_sum(1)
    chip_prefixes(0)
    intra(24, 36)
    row_sum(2)
    chip_prefixes(1)
    chip_prefixes(2)
    intra(36, 48)
    for s in range(GROUPS):
        finish(s)
        inter(c, s)
        if s:
            f_copies[s - 1].wait_recv()
            inter(1 - c, s - 1)
    f_copies[GROUPS - 1].wait_recv()
    inter(1 - c, GROUPS - 1)
    loads[3].wait()
    scale = lax.rsqrt(jnp.sum(square_ref[...], axis=1, keepdims=True) * (1.0 / D) + 1e-6)
    scale = jnp.broadcast_to(scale, (TOK, HEAD))
    square_ref[...] = jnp.zeros_like(square_ref)

    def residual(h, carry):
        out = resid_ref[:, columns(h)].astype(F32) + attn_ref[:, columns(h)] * scale * attn_gain_ref[:, columns(h)]
        attn_ref[:, columns(h)] = out
        square_ref[...] += out * out
        return carry

    lax.fori_loop(0, HEADS, residual, 0, unroll=12)
    scale_2 = lax.rsqrt(jnp.sum(square_ref[...], axis=1, keepdims=True) * (1.0 / D) + 1e-6)
    scale_2 = jnp.broadcast_to(scale_2, (TOK, HEAD))
    select = select_ref[...]

    def norm(h, carry):
        out = attn_ref[:, columns(h)]
        normed = (out * scale_2 * moe_gain_ref[:, columns(h)]).astype(BF)
        outbox_ref[:, columns(h)] = dot(select, normed).astype(BF)
        return carry

    lax.fori_loop(0, HEADS, norm, 0, unroll=12)
    for copy in copies:
        copy.wait_send()


def expert_window(
    where,
    attn_ref, first_ref, weight_ref, outbox_ref, high_ref, low_ref, mixing_ref,
    up_hbm, down_hbm, high_in, low_in, weight_in, mixing_in, sums_ref,
    rows_ref, partner_part, relay_in, near_in, far_in,
    load_sems, y_send, y_recv, core_send, core_recv, z_send, z_recv, hop_send, hop_recv,
    part_send, part_recv, ring_send, ring_recv, next_send, next_recv, sums_send, sums_recv,
    low_send, low_recv, weight_send, weight_recv,
    up_ref, down_ref, total_ref, hidden_ref, part_ref, sum_ref, relay_out, final_ref,
):
    y, z, c = where
    section = lax.axis_index("section")
    after = lax.rem(section + 1, 4)
    before = lax.rem(section + 3, 4)
    loads = [
        pltpu.make_async_copy(up_hbm, up_ref, load_sems.at[0]),
        pltpu.make_async_copy(down_hbm, down_ref, load_sems.at[1]),
    ]
    for load in loads:
        load.start()
    partner = index_of(y, z, 1 - c)
    plus, minus = index_of(y, lax.rem(z + 1, 4), c), index_of(y, lax.rem(z + 3, 4), c)
    y_peer = [index_of(lax.rem(y + d, 4), z, c) for d in range(4)]
    sent = []

    def send(src, dst, send_sem, recv_sem, peer, section_to=None):
        target = {"ctx": peer} if section_to is None else {"section": section_to, "ctx": peer}
        copy = pltpu.make_async_remote_copy(
            src_ref=src, dst_ref=dst, send_sem=send_sem, recv_sem=recv_sem, device_id=target
        )
        copy.start()
        sent.append(copy)

    def arrived(dst, recv_sem, peer, section_to=None):
        target = {"ctx": peer} if section_to is None else {"section": section_to, "ctx": peer}
        pltpu.make_async_remote_copy(
            src_ref=dst, dst_ref=dst, send_sem=recv_sem, recv_sem=recv_sem, device_id=target
        ).wait_recv()

    spot = (0, 1, 3, 2)

    def piece(block, core, p):
        row = p // 2 * 4 * BLOCK + block * BLOCK + core * PAIR + p % 2 * CAP
        return rows_ref.at[pl.ds(pl.multiple_of(row, CAP), CAP), :]

    def box(e):
        return pl.ds(pl.multiple_of(e * CAP, CAP), CAP)

    def to_column(d):
        send(
            outbox_ref.at[box(lax.rem(y + d, 4)), :], piece(0, c, spot[d]),
            y_send.at[d - 1], y_recv.at[d - 1], y_peer[d],
        )

    to_column(1)
    to_column(3)
    rows_ref[pl.ds(pl.multiple_of(c * PAIR, CAP), CAP), :] = outbox_ref[box(y), :]

    def spread(p):
        src = piece(0, c, p)
        send(src, piece(1, c, p), z_send.at[0, p], z_recv.at[0, p], plus)
        send(src, piece(2, c, p), z_send.at[1, p], z_recv.at[1, p], minus)
        send(src, src, core_send.at[0, p], core_recv.at[0, p], partner)

    def from_minus(p):
        src = piece(1, c, p)
        arrived(src, z_recv.at[0, p], minus)
        if p % 2 == 0:
            send(src, piece(3, c, p), hop_send.at[p], hop_recv.at[p], plus)
        send(src, src, core_send.at[1, p], core_recv.at[1, p], partner)

    def from_plus(p):
        src = piece(2, c, p)
        arrived(src, z_recv.at[1, p], plus)
        if p % 2 == 1:
            send(src, piece(3, c, p), hop_send.at[p], hop_recv.at[p], minus)
        send(src, src, core_send.at[2, p], core_recv.at[2, p], partner)

    def from_far(p):
        src = piece(3, c, p)
        arrived(src, hop_recv.at[p], plus if p % 2 else minus)
        send(src, src, core_send.at[3, p], core_recv.at[3, p], partner)

    def from_column(d):
        arrived(piece(0, c, spot[d]), y_recv.at[d - 1], y_peer[4 - d])
        spread(spot[d])

    def up(g):
        first, count = g * 4 * BLOCK, 4 * BLOCK
        for block in range(4):
            for p in (2 * g, 2 * g + 1):
                arrived(piece(block, 1 - c, p), core_recv.at[block, p], partner)
        total_ref[...] = jnp.zeros_like(total_ref)

        def one(i, carry):
            at = pl.ds(pl.multiple_of(i * STEP, STEP), STEP)
            total_ref[...] += dot(rows_ref[first : first + count, at], up_ref[at, :])
            return carry

        lax.fori_loop(0, D // STEP, one, 0)
        hidden_ref[first : first + count, :] = jax.nn.gelu(total_ref[...], approximate=True).astype(BF)

    def down(g, q):
        first = g * 4 * BLOCK

        def one(i, carry):
            at = pl.ds(pl.multiple_of(i * NARROW, NARROW), NARROW)
            from_at = pl.ds(pl.multiple_of(q * WIDE + i * NARROW, NARROW), NARROW)
            out = dot(hidden_ref[first : first + 4 * BLOCK, :], down_ref[:, from_at]).astype(BF)
            for block in range(4):
                for core in range(2):
                    row = block * BLOCK + core * PAIR
                    part_ref[g, q, core, block * PAIR : (block + 1) * PAIR, at] = out[row : row + PAIR, :]
            return carry

        lax.fori_loop(0, WIDE // NARROW, one, 0)
        send(
            part_ref.at[g, q, 1 - c], partner_part.at[g, q], part_send.at[g, q], part_recv.at[g, q], partner
        )

    def over_columns(body):
        def one(i, carry):
            body(pl.ds(pl.multiple_of(i * NARROW, NARROW), NARROW))
            return carry

        lax.fori_loop(0, WIDE // NARROW, one, 0)

    def share(g, q, block, i):
        first = block * PAIR + i * CAP
        return sum_ref.at[g, q, first : first + CAP, :]

    def core_add(g, q):
        arrived(partner_part.at[g, q], part_recv.at[g, q], partner)

        def add(at):
            sum_ref[g, q, :, at] = (
                part_ref[g, q, c, :, at].astype(F32) + partner_part[g, q, :, at].astype(F32)
            ).astype(BF)

        over_columns(add)

    def ring_out(g, q):
        out, back = ring_send.at[g, q], ring_recv.at[g, q]
        send(share(g, q, 3, 0), relay_in.at[g, q, 0], out.at[2], back.at[2], plus)
        send(share(g, q, 3, 1), relay_in.at[g, q, 1], out.at[3], back.at[3], minus)
        send(share(g, q, 2, 1), near_in.at[g, q, 0], out.at[0], back.at[0], plus)
        send(share(g, q, 1, 0), near_in.at[g, q, 1], out.at[1], back.at[1], minus)

    def core_sum(g, q):
        core_add(g, q)
        ring_out(g, q)

    def relay(g, q):
        for side in range(2):
            arrived(relay_in.at[g, q, side], ring_recv.at[g, q, 2 + side], (minus, plus)[side])
            mine = share(g, q, 2 - side, side)

            def add(at, side=side, mine=mine):
                relay_out[g, q, side, :, at] = (
                    mine[:, at].astype(F32) + relay_in[g, q, side, :, at].astype(F32)
                ).astype(BF)

            over_columns(add)
            send(
                relay_out.at[g, q, side], far_in.at[g, q, side],
                ring_send.at[g, q, 4 + side], ring_recv.at[g, q, 4 + side], (plus, minus)[side],
            )

    def final(g, q):
        arrived(near_in.at[g, q, 0], ring_recv.at[g, q, 0], minus)
        arrived(near_in.at[g, q, 1], ring_recv.at[g, q, 1], plus)
        arrived(far_in.at[g, q, 0], ring_recv.at[g, q, 4], minus)
        arrived(far_in.at[g, q, 1], ring_recv.at[g, q, 5], plus)
        for i in range(2):
            mine = share(g, q, 0, i)
            p = 2 * g + i

            weight = jnp.concatenate([weight_in[p]] * (NARROW // TOK), axis=1)

            def add(n, carry, i=i, p=p, mine=mine, weight=weight):
                at = pl.ds(pl.multiple_of(n * NARROW, NARROW), NARROW)
                low_at = pl.ds(pl.multiple_of(q * WIDE + n * NARROW, NARROW), NARROW)
                total = (
                    mine[:, at].astype(F32)
                    + near_in[g, q, 1 - i, :, at].astype(F32)
                    + far_in[g, q, i, :, at].astype(F32)
                )
                final_ref[q, p * CAP : (p + 1) * CAP, at] = (
                    total * weight + low_in[p, :, low_at].astype(F32)
                ).astype(BF)
                return carry

            lax.fori_loop(0, WIDE // NARROW, add, 0)
            d = spot[p]
            send(
                final_ref.at[q, p * CAP : (p + 1) * CAP, :], sums_ref.at[box(y), q * WIDE : (q + 1) * WIDE],
                sums_send.at[q, d], sums_recv.at[q, d], y_peer[(4 - d) % 4], after,
            )

    spread(0)

    def split(h, carry):
        high, low = parts(attn_ref[:, columns(h)])
        high_ref[:, columns(h)] = high
        low_ref[:, columns(h)] = dot(first_ref[...], low).astype(BF)
        return carry

    lax.fori_loop(0, HEADS, split, 0, unroll=6)
    send(high_ref, high_in, next_send.at[0], next_recv.at[0], y_peer[0], after)
    send(mixing_ref, mixing_in, next_send.at[1], next_recv.at[1], y_peer[0], after)
    from_column(1)
    to_column(2)
    from_minus(0)
    from_plus(0)
    from_minus(1)
    from_plus(1)
    from_column(3)
    low_in[0] = low_ref[box(y), :]
    weight_in[0] = weight_ref[box(y), :]
    for d in (1, 3, 2):
        e = box(lax.rem(y + d, 4))
        send(low_ref.at[e, :], low_in.at[spot[d]], low_send.at[d - 1], low_recv.at[d - 1], y_peer[d])
        send(
            weight_ref.at[e, :], weight_in.at[spot[d]],
            weight_send.at[d - 1], weight_recv.at[d - 1], y_peer[d],
        )
    from_far(0)
    from_far(1)
    from_column(2)
    loads[0].wait()
    up(0)
    for p in (2, 3):
        from_minus(p)
        from_plus(p)
    loads[1].wait()
    down(0, 0)
    down(0, 1)
    core_add(0, 0)
    down(0, 2)
    core_add(0, 1)
    core_add(0, 2)
    from_far(2)
    ring_out(0, 0)
    from_far(3)
    ring_out(0, 1)
    ring_out(0, 2)
    up(1)
    for q in range(CHUNKS):
        relay(0, q)
    for d in (1, 3, 2):
        arrived(low_in.at[spot[d]], low_recv.at[d - 1], y_peer[4 - d])
        arrived(weight_in.at[spot[d]], weight_recv.at[d - 1], y_peer[4 - d])
    down(1, 0)
    down(1, 1)
    core_sum(1, 0)
    down(1, 2)
    final(0, 0)
    final(0, 1)
    core_add(1, 1)
    relay(1, 0)
    ring_out(1, 1)
    final(0, 2)
    core_add(1, 2)
    relay(1, 1)
    ring_out(1, 2)
    final(1, 0)
    relay(1, 2)
    final(1, 1)
    final(1, 2)
    arrived(high_in, next_recv.at[0], y_peer[0], before)
    arrived(mixing_in, next_recv.at[1], y_peer[0], before)
    for q in range(CHUNKS):
        for d in range(4):
            arrived(sums_ref.at[0:CAP, q * WIDE : (q + 1) * WIDE], sums_recv.at[q, d], y_peer[d], before)
    for copy in sent:
        copy.wait_send()


def layer_kernel(
    q_hbm, k_hbm, v_hbm, resid_hbm, rate_ref, attn_gain_ref, moe_gain_ref, experts_ref, combine_ref,
    up_hbm, down_hbm,
    high_in, mixing_in, sums_ref,
    attn_ref, first_ref, weight_ref, high_ref, low_ref, outbox_ref, mixing_ref, low_in, weight_in,
    partner_total, partner_state, t_recv, r_recv, chip_prefix, prefix,
    rows_ref, partner_part, relay_in, near_in, far_in,
    *sems,
):
    y, z, c = place()
    section = lax.axis_index("section")
    barrier = pltpu.get_barrier_semaphore()
    ring = [index_of(y, lax.rem(z + d, 4), c) for d in (1, 2, 3)]
    column = [index_of(lax.rem(y + d, 4), z, c) for d in range(4)]
    for peer in [index_of(y, z, 1 - c)] + ring + column[1:]:
        pl.semaphore_signal(barrier, inc=1, device_id={"ctx": peer})
    for step in (1, 3):
        for peer in column:
            pl.semaphore_signal(
                barrier, inc=1, device_id={"section": lax.rem(section + step, 4), "ctx": peer}
            )

    def first(*local_refs):
        scan_attention(
            (y, z, c), barrier,
            q_hbm, k_hbm, v_hbm, resid_hbm, rate_ref, attn_gain_ref, moe_gain_ref, experts_ref, combine_ref,
            attn_ref, first_ref, weight_ref, outbox_ref, mixing_ref,
            partner_total, partner_state, t_recv, r_recv, chip_prefix, prefix,
            *sems[:12], *local_refs,
        )

    pl.run_scoped(
        first,
        pltpu.VMEM((TOK, D), BF),
        pltpu.VMEM((TOK, D), BF),
        pltpu.VMEM((TOK, D), BF),
        pltpu.VMEM((TOK, D), BF),
        pltpu.VMEM((HEADS, TOK), F32),
        pltpu.VMEM((HEADS, TOK), F32),
        pltpu.VMEM((2, GROUPS, 4 * ROWS, HEAD), F32),
        pltpu.VMEM((GROUPS, 3, MESSAGE, HEAD), F32),
        pltpu.VMEM((GROUPS, 4, ROWS, HEAD), F32),
        pltpu.VMEM((GROUPS, MESSAGE, HEAD), F32),
        pltpu.VMEM((GROUPS, 3, ROWS, HEAD), F32),
        pltpu.VMEM((GROUPS, 4 * ROWS, HEAD), F32),
        pltpu.VMEM((TOK, HEAD), F32),
        pltpu.VMEM((FLY * CAP, TOK), BF),
    )

    def second(*local_refs):
        expert_window(
            (y, z, c), attn_ref, first_ref, weight_ref, outbox_ref, high_ref, low_ref, mixing_ref,
            up_hbm, down_hbm, high_in, low_in, weight_in, mixing_in, sums_ref,
            rows_ref, partner_part, relay_in, near_in, far_in,
            *sems[12:], *local_refs,
        )

    pl.run_scoped(
        second,
        pltpu.VMEM((D, UNITS), BF),
        pltpu.VMEM((UNITS, D), BF),
        pltpu.VMEM((4 * BLOCK, UNITS), F32),
        pltpu.VMEM((8 * BLOCK, UNITS), BF),
        pltpu.VMEM((2, CHUNKS, 2, 4 * PAIR, WIDE), BF),
        pltpu.VMEM((2, CHUNKS, 4 * PAIR, WIDE), BF),
        pltpu.VMEM((2, CHUNKS, 2, CAP, WIDE), BF),
        pltpu.VMEM((CHUNKS, BLOCK, WIDE), BF),
    )


def layer(queries, keys, values, resid, rate, attn_gain, moe_gain, experts, combine, w_up, w_down):
    vmem = pl.BlockSpec(memory_space=pltpu.VMEM)
    hbm = pl.BlockSpec(memory_space=pl.ANY)
    dma = pltpu.SemaphoreType.DMA
    return pl.pallas_call(
        layer_kernel,
        out_shape=(
            jax.ShapeDtypeStruct((TOK, D), BF),
            jax.ShapeDtypeStruct((TOK, TOK), BF),
            jax.ShapeDtypeStruct((BLOCK, D), BF),
        ),
        in_specs=[hbm] * 4 + [vmem] * 5 + [hbm] * 2,
        out_specs=(hbm, hbm, hbm),
        scratch_shapes=[
            pltpu.VMEM((TOK, D), F32),
            pltpu.VMEM((BLOCK, TOK), BF),
            pltpu.VMEM((BLOCK, TOK), F32),
            pltpu.VMEM((TOK, D), BF),
            pltpu.VMEM((BLOCK, D), BF),
            pltpu.VMEM((BLOCK, D), BF),
            pltpu.VMEM((TOK, TOK), BF),
            pltpu.VMEM((4, CAP, D), BF),
            pltpu.VMEM((4, CAP, TOK), F32),
            pltpu.VMEM((HEADS, TOK), F32),
            pltpu.VMEM((GROUPS, 4 * ROWS, HEAD), F32),
            pltpu.VMEM((GROUPS, 4, MESSAGE, HEAD), F32),
            pltpu.VMEM((GROUPS, 4, MESSAGE, HEAD), F32),
            pltpu.VMEM((GROUPS, 4, ROWS, HEAD), F32),
            pltpu.VMEM((2, GROUPS, 4 * ROWS, HEAD), F32),
            pltpu.VMEM((8 * BLOCK, D), BF),
            pltpu.VMEM((2, CHUNKS, 4 * PAIR, WIDE), BF),
            pltpu.VMEM((2, CHUNKS, 2, CAP, WIDE), BF),
            pltpu.VMEM((2, CHUNKS, 2, CAP, WIDE), BF),
            pltpu.VMEM((2, CHUNKS, 2, CAP, WIDE), BF),
            dma((4,)), dma((2,)), dma((GROUPS,)), dma((GROUPS,)), dma((GROUPS, 3)), dma((GROUPS, 3)),
            dma((GROUPS, 3)), dma((GROUPS, 3)), dma((GROUPS, 3)), dma((GROUPS, 3)), dma((GROUPS,)),
            dma((GROUPS,)),
            dma((2,)), dma((3,)), dma((3,)), dma((4, 4)), dma((4, 4)), dma((2, 4)), dma((2, 4)),
            dma((4,)), dma((4,)), dma((2, CHUNKS)), dma((2, CHUNKS)),
            dma((2, CHUNKS, 6)), dma((2, CHUNKS, 6)),
            dma((2,)), dma((2,)), dma((CHUNKS, 4)), dma((CHUNKS, 4)),
            dma((3,)), dma((3,)), dma((3,)), dma((3,)),
        ],
        compiler_params=pltpu.CompilerParams(
            collective_id=0, has_side_effects=True, vmem_limit_bytes=60 * 2**20
        ),
        name="layer",
    )(queries, keys, values, resid, rate, attn_gain, moe_gain, experts, combine, w_up, w_down)


def mix_kernel(high_ref, mixing_ref, sums_ref, out_ref):
    mixing = mixing_ref[:, :BLOCK]
    for i in range(D // 2 // NARROW):
        at = slice(i * NARROW, (i + 1) * NARROW)
        out_ref[:, at] = (high_ref[:, at].astype(F32) + dot(mixing, sums_ref[:, at])).astype(BF)


def mix(high, mixing, sums):
    wide = D // 2
    return pl.pallas_call(
        mix_kernel,
        out_shape=jax.ShapeDtypeStruct((TOK, D), BF),
        grid=(D // wide,),
        in_specs=[
            pl.BlockSpec((TOK, wide), lambda i: (0, i)),
            pl.BlockSpec((TOK, TOK), lambda i: (0, 0)),
            pl.BlockSpec((BLOCK, wide), lambda i: (0, i)),
        ],
        out_specs=pl.BlockSpec((TOK, wide), lambda i: (0, i)),
        compiler_params=pltpu.CompilerParams(vmem_limit_bytes=60 * 2**20),
        name="mix",
    )(high, mixing, sums)


def local(
    resid, queries, keys, values, log_decay, attn_gain, moe_gain, experts, combine_weight, w_up, w_down
):
    high, mixing, sums = layer(
        queries[0], keys[0], values[0], resid[0], log_decay[0].T, attn_gain, moe_gain,
        experts[0].T, combine_weight[0].T, w_up[0], w_down[0],
    )
    return mix(high, mixing, sums)[None]


def solution(mesh):
    token = P("section", "ctx", None)
    return jax.shard_map(
        local,
        mesh=mesh,
        in_specs=(
            token, token, token, token, token,
            P("section", None), P("section", None),
            token, token,
            P("section", None, "ctx"), token,
        ),
        out_specs=token,
        check_vma=False,
    )
```
